256 devices in a mesh: seq: 32 (over x, y, z_hi), tensor: 8 (over z_lo, core).
Axes of the slice: x: 4, y: 4, z: 8 (z_hi: 2, z_lo: 4; z = z_hi * 4 + z_lo), core: 2. Of those that a mesh axis runs over, the one named last changes fastest.
Arguments:
- queries: bfloat16 [4096, 4096], P('seq', 'tensor'), may hold values from -100 to 100
- keys: bfloat16 [4096, 1024], P('seq', 'tensor'), may hold values from -4 to 4
- values: bfloat16 [4096, 1024], P('seq', 'tensor'), may hold values from -5 to 5
- prefix_keys: bfloat16 [4096, 1024], P('seq', 'tensor'), may hold values from -5 to 5
- prefix_values: bfloat16 [4096, 1024], P('seq', 'tensor'), may hold values from -5 to 5
- doc_start: int32 [1], replicated, may hold values from 0 to 2047
- out_weight: bfloat16 [4096, 8192], P('tensor'), may hold values from -0.75 to 0.75
- residual: bfloat16 [4096, 8192], P(('seq', 'tensor')), may hold values from -6 to 6
- student_hidden: bfloat16 [4096, 3072], P('seq', 'tensor'), may hold values from -6 to 6
- student_gain: float32 [3072], replicated, may hold values from 0.1 to 1.9
- proj_weight: bfloat16 [3072, 8192], P('seq', 'tensor'), may hold values from -0.109375 to 0.109375
Outputs:
- teacher_hidden: bfloat16 [4096, 8192], P('seq', 'tensor')
- student_grad: bfloat16 [4096, 3072], P('seq', 'tensor')
- proj_grad: float32 [3072, 8192], P('seq', 'tensor')
- gain_grad: float32 [3072], P('tensor')
The draws below stay inside these ranges and needn't reach their ends.
All inputs are finite; a program needn't handle non-finite values.
Results may differ from the reference program's by a relative error of at most 0.02.
Values may be sent and summed in bfloat16 or wider, within the bound.
A program may use at most 128 MiB of HBM per device.

```python
import jax
import jax.numpy as jnp
from jax import lax

D_T = 8192
HEADS = 32
KV_HEADS = 8
HEAD_DIM = 128
D_S = 3072
TOKENS = 4096
PREFIX = 4096


def drawn_keys(key):
    key_table = jnp.clip(jax.random.normal(jax.random.fold_in(key, 11), (PREFIX, KV_HEADS * HEAD_DIM), jnp.float32), -4.0, 4.0)
    return key_table


def draw_prefix_keys(key, part):
    return drawn_keys(key).astype(jnp.bfloat16)


def draw_queries(key, part):
    drawn = 2.0 * jnp.clip(jax.random.normal(jax.random.fold_in(key, 21), (TOKENS, HEADS * HEAD_DIM), jnp.float32), -4.0, 4.0)
    return drawn.astype(jnp.bfloat16)


def with_spikes(result, rng, source, target, parts, factor):
    owner, partner = [(jnp.arange(result.shape[dim]) // (result.shape[dim] // parts)).reshape([-1 if axis == dim else 1 for axis in range(result.ndim)]) for dim in (source, target)]
    chosen = jax.random.permutation(rng, parts)[partner]
    strong = (owner == chosen) | (owner == (partner + parts // 2) % parts)
    return jnp.where(strong, factor * result, result)


def level_of(key, dims, shards, low, largest):
    gain, own = 1.0, jax.random.fold_in(key, 6)
    for dim, blocks in shards:
        heights = jnp.exp(jax.random.uniform(jax.random.fold_in(own, dim), (blocks,), jnp.float32, low / len(shards), largest / len(shards)))
        gain = gain * jnp.repeat(heights, dims[dim] // blocks).reshape([-1 if axis == dim else 1 for axis in range(len(dims))])
    return gain


def centred(own_key, shape, width, most, cuts=(), kind=jnp.bfloat16):
    factor_of = level_of(own_key, shape, cuts, -0.22, 0.18) if cuts else 1.0
    result = jax.random.normal(own_key, shape, jnp.float32) * width * factor_of
    return jnp.minimum(jnp.maximum(result, -most), most).astype(kind)


def heavy_noise(rng, dims, deviation, reach, cuts, heavy, kind=jnp.bfloat16):
    values = deviation * jax.random.normal(rng, dims, jnp.float32)
    if cuts:
        values = values * level_of(rng, dims, cuts, -0.22, 0.18)
    return jnp.clip(with_spikes(values, jax.random.fold_in(rng, 3), *heavy), -reach, reach).astype(kind)


def setup_inputs(seed: int = 0) -> dict:
    streams_of = jax.random.split(jax.random.key(seed), 12)
    queries = draw_queries(jax.random.fold_in(streams_of[11], 71), 0)
    keys = centred(streams_of[1], (TOKENS, KV_HEADS * HEAD_DIM), 1.0, 4.0, ((0, 32), (1, 8)))
    values = centred(streams_of[2], (TOKENS, KV_HEADS * HEAD_DIM), 1.0, 5.0, ((0, 32), (1, 8)))
    prefix_keys = draw_prefix_keys(jax.random.fold_in(streams_of[11], 71), 0)
    prefix_values = centred(streams_of[4], (PREFIX, KV_HEADS * HEAD_DIM), 1.0, 5.0, ((0, 32), (1, 8)))
    doc_start = jax.random.randint(streams_of[5], (1,), 0, PREFIX // 2).astype(jnp.int32)
    out_weight = centred(streams_of[6], (HEADS * HEAD_DIM, D_T), (HEADS * HEAD_DIM // 64) ** -0.5, 0.75, ((0, 8),))
    residual = centred(streams_of[7], (TOKENS, D_T), 1.0, 6.0, ((0, 256),))
    student_hidden = heavy_noise(streams_of[8], (TOKENS, D_S), 1.0, 6.0, ((0, 32), (1, 8)), (0, 1, 32, 2.75))
    student_gain = jnp.clip(1.0 + 0.18 * jax.random.normal(streams_of[9], (D_S,), jnp.float32), 0.1, 1.9)
    proj_weight = centred(streams_of[10], (D_S, D_T), D_S ** -0.5, 0.109375, ((0, 32), (1, 8)))
    return {"queries": queries, "keys": keys, "values": values, "prefix_keys": prefix_keys, "prefix_values": prefix_values, "doc_start": doc_start, "out_weight": out_weight, "residual": residual, "student_hidden": student_hidden, "student_gain": student_gain, "proj_weight": proj_weight}


large_negative = -1e+30

def reference(queries, keys, values, prefix_keys, prefix_values, doc_start, out_weight, residual, student_hidden, student_gain, proj_weight):
    group_size = HEADS // KV_HEADS
    all_keys = jnp.concatenate([prefix_keys, keys], 0)
    all_values = jnp.concatenate([prefix_values, values], 0)
    key_position = jnp.arange(PREFIX + TOKENS, dtype=jnp.int32)
    query_position = PREFIX + jnp.arange(TOKENS, dtype=jnp.int32)
    visible = (key_position[None, :] <= query_position[:, None]) & (key_position[None, :] >= doc_start[0])
    score_scale = 1.0 / HEAD_DIM ** 0.5

    def one_head(head):
        kv_head = head // group_size
        query_rows = lax.dynamic_slice_in_dim(queries, (head * HEAD_DIM).astype(jnp.int32), HEAD_DIM, 1)
        key_rows = lax.dynamic_slice_in_dim(all_keys, (kv_head * HEAD_DIM).astype(jnp.int32), HEAD_DIM, 1)
        value_rows = lax.dynamic_slice_in_dim(all_values, (kv_head * HEAD_DIM).astype(jnp.int32), HEAD_DIM, 1)
        scores = jnp.dot(query_rows, key_rows.T, preferred_element_type=jnp.float32) * score_scale
        scores = jnp.where(visible, scores, large_negative)
        row_max = lax.optimization_barrier(jnp.max(scores, axis=1, keepdims=True))
        weights_exp = jnp.where(visible, jnp.exp(scores - row_max), 0.0)
        row_total = lax.optimization_barrier(jnp.sum(weights_exp, axis=1, keepdims=True))
        summed = jnp.dot(weights_exp.astype(jnp.bfloat16), value_rows, preferred_element_type=jnp.float32)
        return (summed / row_total).astype(jnp.bfloat16)
    per_head = lax.map(one_head, jnp.arange(HEADS, dtype=jnp.int32))
    attended = jnp.transpose(per_head, (1, 0, 2)).reshape(TOKENS, HEADS * HEAD_DIM)
    teacher_hidden = (residual.astype(jnp.float32) + jnp.dot(attended, out_weight, preferred_element_type=jnp.float32)).astype(jnp.bfloat16)
    hidden_wide = student_hidden.astype(jnp.float32)
    inverse = lax.rsqrt(lax.optimization_barrier(jnp.mean(hidden_wide * hidden_wide, axis=1, keepdims=True)) + 1e-05)
    normed = (hidden_wide * inverse * student_gain).astype(jnp.bfloat16)
    mismatch = (jnp.dot(normed, proj_weight, preferred_element_type=jnp.float32) - teacher_hidden.astype(jnp.float32)).astype(jnp.bfloat16)
    normed_grad = jnp.dot(mismatch, proj_weight.T, preferred_element_type=jnp.float32)
    row_inner = lax.optimization_barrier(jnp.mean(normed_grad * student_gain * hidden_wide, axis=1, keepdims=True))
    student_grad = (inverse * student_gain * normed_grad - hidden_wide * inverse * inverse * inverse * row_inner).astype(jnp.bfloat16)
    grad_scale = 1.0 / TOKENS ** 0.5
    proj_grad = jnp.dot(normed.T, mismatch, preferred_element_type=jnp.float32) * grad_scale
    gain_grad = lax.optimization_barrier(jnp.sum(normed_grad * hidden_wide * inverse, axis=0)) * grad_scale
    return (teacher_hidden, student_grad, proj_grad, gain_grad)
```

```python
import math

import jax
import jax.numpy as jnp
from jax import lax
from jax.experimental import pallas as pl
from jax.experimental.pallas import tpu as pltpu
from jax.sharding import Mesh
from jax.sharding import PartitionSpec as P

MESH = pl.DeviceIdType.MESH
F32 = jnp.float32
BF16 = jnp.bfloat16
NEG = -1e30
SEQ = ("x", "y", "zh")
TEN = ("zl", "c")
SEMS = 192


def mod4(v):
    return lax.rem(v, 4)


class Wire:
    def __init__(self, send, recv):
        self.send, self.recv, self.used, self.all = send, recv, 0, []

    def copy(self, src, dst, dev):
        i = self.used
        self.used += 1
        d = pltpu.make_async_remote_copy(
            src_ref=src,
            dst_ref=dst,
            send_sem=self.send.at[i],
            recv_sem=self.recv.at[i],
            device_id=dev,
            device_id_type=MESH,
        )
        d.start()
        self.all.append(d)
        return d

    def drain(self):
        for d in self.all:
            d.wait_send()


class Gather:
    def __init__(self, wire, at, first, second, coord):
        self.wire, self.at, self.first, self.second = wire, at, first, second
        self.a, self.b, self.z = coord[first], coord[second], coord["zh"]
        self.r, self.l, self.hr, self.hl = {}, {}, {}, {}
        a = self.a
        self.order = (a, mod4(a + 3), mod4(a + 1), mod4(a + 2))

    def z_send(self):
        own = self.at(self.a, self.b, self.z, 1, None)
        self.zd = self.wire.copy(own, own, {"zh": 1 - self.z})

    def z_wait(self):
        self.zd.wait_recv()

    def ring(self, key, ref_of, axis, pos):
        own = ref_of(pos, None)
        self.r[key] = self.wire.copy(own, own, {axis: mod4(pos + 1)})
        self.l[key] = self.wire.copy(own, own, {axis: mod4(pos + 3)})

    def forward(self, key, ref_of, axis, pos):
        self.r[key].wait_recv()
        left = ref_of(mod4(pos + 3), 0)
        self.hr[key] = self.wire.copy(left, left, {axis: mod4(pos + 1)})
        self.l[key].wait_recv()
        right = ref_of(mod4(pos + 1), 1)
        self.hl[key] = self.wire.copy(right, right, {axis: mod4(pos + 3)})

    def done(self, key):
        self.hr[key].wait_recv()
        self.hl[key].wait_recv()

    def one(self, j):
        zq = self.z if j == 0 else 1 - self.z
        return lambda pos, half: self.at(pos, self.b, zq, 1, half)

    def two(self, k):
        aq = self.order[k]
        return lambda pos, half: self.at(aq, pos, 0, 2, half)

    def p1_send(self, j):
        self.ring(("1", j), self.one(j), self.first, self.a)

    def p1_fwd(self, j):
        self.forward(("1", j), self.one(j), self.first, self.a)

    def p1_done(self, j):
        self.done(("1", j))

    def p2_send(self, k):
        self.ring(("2", k), self.two(k), self.second, self.b)

    def p2_fwd(self, k):
        self.forward(("2", k), self.two(k), self.second, self.b)

    def p2_done(self, k):
        self.done(("2", k))


class Scatter:
    def __init__(self, wire, part, near, far, axis, pos):
        self.wire, self.part, self.near, self.far = wire, part, near, far
        self.axis, self.pos = axis, pos

    def start(self):
        p, ax = self.pos, self.axis
        opp = mod4(p + 2)
        self.r1 = self.wire.copy(self.part(opp, 0), self.near.at[0], {ax: mod4(p + 1)})
        self.l1 = self.wire.copy(self.part(opp, 1), self.near.at[1], {ax: mod4(p + 3)})

    def middle(self):
        p, ax = self.pos, self.axis
        right, left = mod4(p + 1), mod4(p + 3)
        self.r1.wait_recv()
        ref = self.part(right, 0)
        ref[...] = (ref[...].astype(F32) + self.near[0].astype(F32)).astype(BF16)
        self.r2 = self.wire.copy(self.part(right, None), self.far.at[0], {ax: right})
        self.l1.wait_recv()
        ref = self.part(left, 1)
        ref[...] = (ref[...].astype(F32) + self.near[1].astype(F32)).astype(BF16)
        self.l2 = self.wire.copy(self.part(left, None), self.far.at[1], {ax: left})

    def finish(self):
        self.r2.wait_recv()
        self.l2.wait_recv()
        ref = self.part(self.pos, None)
        ref[...] = (
            ref[...].astype(F32) + self.far[0].astype(F32) + self.far[1].astype(F32)
        ).astype(BF16)


def kernel(
    q_hbm, k_hbm, v_hbm, pk_hbm, pv_hbm, doc, w_hbm, res_hbm, hid_hbm, gain, proj_hbm,
    teacher_out, sgrad_out, pgrad_out, ggrad_out,
    kv0, kv1, pj, w, q, qs, hid, res, mx, tot, acc, att,
    bsend, brecv, bz, zrecv, tacc, nrm, nrmt, mis,
    fsend, frecv, fz, fzrecv, rowbuf, gx, gy, gz,
    gp, an1, an2, am1, am2, bn1, bn2, bm1, bm2, a3, b3,
    ssem, rsem, lsem,
):
    x, y, z = lax.axis_index("x"), lax.axis_index("y"), lax.axis_index("zh")
    zl, c = lax.axis_index("zl"), lax.axis_index("c")
    coord = {"x": x, "y": y, "zh": z}
    seq = (x * 4 + y) * 2 + z
    t = zl * 2 + c
    wire = Wire(ssem, rsem)

    def tensor_peer(dz, dc):
        return {"zl": mod4(zl + dz), "c": c if dc == 0 else 1 - c}

    def tensor_index(dz, dc):
        return mod4(zl + dz) * 2 + (c if dc == 0 else 1 - c)

    peers = [(dz, dc) for dz in (2, 1, 3, 0) for dc in (0, 1) if (dz, dc) != (0, 0)]

    loads = [
        (pk_hbm, kv0.at[seq, 0]),
        (pv_hbm, kv0.at[seq, 1]),
        (k_hbm, kv1.at[seq, 0]),
        (v_hbm, kv1.at[seq, 1]),
        (proj_hbm, pj.at[seq]),
        (hid_hbm, hid.at[t]),
        (q_hbm, q),
        (
            res_hbm.at[:, pl.ds(pl.multiple_of(t * 1024, 1024), 1024)],
            res.at[pl.ds(pl.multiple_of(t * 16, 16), 16), :],
        ),
        (w_hbm, w),
    ]
    local = [pltpu.make_async_copy(s, d, lsem.at[i]) for i, (s, d) in enumerate(loads)]
    for d in local:
        d.start()

    barrier = pltpu.get_barrier_semaphore()
    greet = [
        {"x": mod4(x + 1)}, {"x": mod4(x + 2)}, {"x": mod4(x + 3)},
        {"y": mod4(y + 1)}, {"y": mod4(y + 2)}, {"y": mod4(y + 3)},
        {"zh": 1 - z},
    ] + [tensor_peer(*p) for p in peers]
    for dev in greet:
        pl.semaphore_signal(barrier, inc=1, device_id=dev, device_id_type=MESH)
    pl.semaphore_wait(barrier, len(greet))

    def kv_at(buf, x_first):
        def at(a, b, zq, count, half):
            slot = ((a * 4 + b) if x_first else (b * 4 + a)) * 2 + zq
            where = slot if count == 1 else pl.ds(slot, 2)
            return buf.at[where] if half is None else buf.at[where, half]

        return at

    def pj_at(low, x_first):
        def at(a, b, zq, count, half):
            slot = ((a * 4 + b) if x_first else (b * 4 + a)) * 2 + zq
            where = slot if count == 1 else pl.ds(slot, 2)
            cols = pl.ds(0, 1024) if half is None else pl.ds(512 * half, 512)
            return pj.at[where, pl.ds(low, 48), cols]

        return at

    kv = (
        Gather(wire, kv_at(kv0, True), "x", "y", coord),
        Gather(wire, kv_at(kv1, False), "y", "x", coord),
    )
    pr = (
        Gather(wire, pj_at(0, True), "x", "y", coord),
        Gather(wire, pj_at(48, False), "y", "x", coord),
    )

    def both(streams, name, *args):
        for s in streams:
            getattr(s, name)(*args)

    for d in local[:4]:
        d.wait()
    both(kv, "z_send")
    both(kv, "p1_send", 0)
    both(kv, "p1_fwd", 0)
    both(kv, "z_wait")
    both(kv, "p1_send", 1)
    both(kv, "p2_send", 0)
    local[4].wait()
    both(pr, "z_send")
    both(kv, "p1_fwd", 1)
    both(kv, "p2_send", 1)
    both(kv, "p2_send", 2)
    local[5].wait()
    hsend, rsend = [], []
    for p in peers:
        hsend.append(wire.copy(hid.at[t], hid.at[t], tensor_peer(*p)))
        cols = pl.ds(pl.multiple_of(tensor_index(*p) * 1024, 1024), 1024)
        rsend.append(
            wire.copy(
                res_hbm.at[:, cols],
                res.at[pl.ds(pl.multiple_of(t * 16, 16), 16), :],
                tensor_peer(*p),
            )
        )
    both(kv, "p1_done", 0)
    both(kv, "p1_done", 1)
    both(kv, "p2_send", 3)
    for k in range(4):
        both(kv, "p2_fwd", k)
    both(pr, "p1_send", 0)
    both(pr, "z_wait")
    both(pr, "p1_send", 1)
    both(pr, "p2_send", 0)

    local[6].wait()
    for h in range(4):
        qs[pl.ds(h * 128, 128), :] = q[:, h * 128 : (h + 1) * 128]
    mx[...] = jnp.full((512, 128), NEG, F32)
    tot[...] = jnp.zeros((512, 128), F32)
    acc[...] = jnp.zeros((512, 128), F32)
    factor = 128 ** (-0.5) * math.log2(math.e)

    def wide(v):
        return jnp.concatenate([v] * 4, axis=1)

    def block(j, buf, visible):
        kb = buf[pl.ds(4 * j, 4), 0].reshape(512, 128)
        vb = buf[pl.ds(4 * j, 4), 1].reshape(512, 128)
        s = lax.dot_general(
            qs[...], kb, (((1,), (1,)), ((), ())), preferred_element_type=F32
        ) * factor
        if visible is not None:
            s = jnp.where(visible(j), s, NEG)
        old = mx[...]
        new = jnp.maximum(old, jnp.broadcast_to(jnp.max(s, axis=1, keepdims=True), (512, 128)))
        p = jnp.exp2(s - wide(new))
        scale = jnp.exp2(old - new)
        mx[...] = new
        tot[...] = tot[...] * scale + jnp.broadcast_to(
            jnp.sum(p, axis=1, keepdims=True), (512, 128)
        )
        acc[...] = acc[...] * scale + jnp.dot(p.astype(BF16), vb, preferred_element_type=F32)

    column = lax.broadcasted_iota(jnp.int32, (512, 512), 1)
    token = lax.rem(lax.broadcasted_iota(jnp.int32, (512, 512), 0), 128)

    def in_document(j):
        return column + j * 512 >= doc[0]

    def causal(j):
        return column + j * 512 <= token + seq * 128

    for k in range(4):
        both(kv, "p2_done", k)

    def loop(lo, hi, buf, visible):
        lax.fori_loop(lo, hi, lambda j, _: (block(j, buf, visible), 0)[1], 0)

    loop(0, 4, kv0, in_document)
    both(pr, "p1_fwd", 0)
    both(pr, "p1_fwd", 1)
    both(pr, "p2_send", 1)
    both(pr, "p2_send", 2)
    loop(4, 8, kv0, None)
    both(pr, "p1_done", 0)
    both(pr, "p1_done", 1)
    both(pr, "p2_send", 3)
    both(pr, "p2_fwd", 0)
    own = seq // 4
    loop(0, own, kv1, None)
    block(own, kv1, causal)
    both(pr, "p2_fwd", 1)
    both(pr, "p2_fwd", 2)
    for h in range(4):
        rows = pl.ds(h * 128, 128)
        att[:, h * 128 : (h + 1) * 128] = (acc[rows, :] / tot[rows, :]).astype(BF16)

    local[8].wait()
    turns = (2, 1, 3, 0)

    def projected(dz, dc):
        cols = pl.ds(pl.multiple_of(tensor_index(dz, dc) * 1024, 1024), 1024)
        return jnp.dot(att[...], w[:, cols], preferred_element_type=F32)

    mate = {"c": 1 - c}
    half = {}
    for dz in turns:
        bsend[dz] = projected(dz, 1).astype(BF16)
        half[dz] = wire.copy(bsend.at[dz], brecv.at[dz], mate)
    zsum = {}
    for dz in turns:
        mine = projected(dz, 0)
        half[dz].wait_recv()
        mine = mine + brecv[dz].astype(F32)
        if dz:
            bz[dz - 1] = mine.astype(BF16)
            zsum[dz] = wire.copy(bz.at[dz - 1], zrecv.at[dz - 1], tensor_peer(dz, 0))
        else:
            tacc[...] = mine
    both(pr, "p2_fwd", 3)

    for d in hsend:
        d.wait_recv()
    square = jnp.zeros((128, 384), F32)
    for i in range(8):
        h = hid[i].astype(F32)
        square = square + h * h
    inverse = lax.rsqrt(jnp.sum(square, axis=1, keepdims=True) / 3072.0 + 1e-05)
    for i in range(8):
        n = (hid[i].astype(F32) * inverse * gain[i]).astype(BF16)
        nrm[:, i * 384 : (i + 1) * 384] = n
        nrmt[pl.ds(i * 384, 384), :] = n.T
    for k in range(4):
        both(pr, "p2_done", k)
    pre = jnp.zeros((128, 1024), F32)
    for i in range(4):
        pre = pre + jnp.dot(
            nrm[:, i * 768 : (i + 1) * 768],
            pj[pl.ds(8 * i, 8)].reshape(768, 1024),
            preferred_element_type=F32,
        )
    for d in rsend:
        d.wait_recv()
    local[7].wait()
    tacc[...] = tacc[...] + res[...].astype(F32)
    for dz in turns[:3]:
        zsum[dz].wait_recv()
    teacher = (
        tacc[...] + zrecv[0].astype(F32) + zrecv[1].astype(F32) + zrecv[2].astype(F32)
    ).astype(BF16)
    teacher_out[...] = teacher
    mis[...] = (pre - teacher.astype(F32)).astype(BF16)

    def product(xd):
        rows = pl.ds(pl.multiple_of(xd * 768, 768), 768)
        g = jnp.dot(nrmt[rows, :], mis[...], preferred_element_type=F32)
        gp[xd] = g.astype(BF16).reshape(8, 96, 1024)

    def cols_of(base, h):
        return pl.ds(base, 512) if h is None else pl.ds(base + 256 * h, 256)

    sa1 = Scatter(wire, lambda p, h: gp.at[p, :, :, cols_of(0, h)], an1, an2, "x", x)
    sa2 = Scatter(
        wire, lambda p, h: gp.at[x, pl.ds(2 * p, 2), :, cols_of(0, h)], am1, am2, "y", y
    )
    sb1 = Scatter(
        wire, lambda p, h: gp.at[:, pl.ds(2 * p, 2), :, cols_of(512, h)], bn1, bn2, "y", y
    )
    sb2 = Scatter(
        wire, lambda p, h: gp.at[p, pl.ds(2 * y, 2), :, cols_of(512, h)], bm1, bm2, "x", x
    )
    product(mod4(x + 2))
    sa1.start()
    for d in (1, 3, 0):
        product(mod4(x + d))
    sb1.start()

    def state_grad(dz, dc):
        rows = pj[pl.ds(4 * tensor_index(dz, dc), 4)].reshape(384, 1024)
        return lax.dot_general(
            mis[...], rows, (((1,), (1,)), ((), ())), preferred_element_type=F32
        )

    for dz in turns:
        fsend[dz] = state_grad(dz, 1).astype(BF16)
        half[dz] = wire.copy(fsend.at[dz], frecv.at[dz], mate)
    grad = None
    for dz in turns:
        mine = state_grad(dz, 0)
        half[dz].wait_recv()
        mine = mine + frecv[dz].astype(F32)
        if dz:
            fz[dz - 1] = mine.astype(BF16)
            zsum[dz] = wire.copy(fz.at[dz - 1], fzrecv.at[dz - 1], tensor_peer(dz, 0))
        else:
            grad = mine
    sa1.middle()
    sb1.middle()
    for dz in turns[:3]:
        zsum[dz].wait_recv()
    grad = grad + fzrecv[0].astype(F32) + fzrecv[1].astype(F32) + fzrecv[2].astype(F32)
    hidden = hid[t].astype(F32)
    own_gain = gain[t]
    inner = jnp.sum(grad * own_gain * hidden, axis=1, keepdims=True)
    diagonal = lax.broadcasted_iota(jnp.int32, (128, 128), 0) == lax.broadcasted_iota(
        jnp.int32, (128, 128), 1
    )
    as_row = jnp.sum(jnp.where(diagonal, inner, 0.0), axis=0, keepdims=True)
    rowbuf[0] = jnp.broadcast_to(as_row, (8, 128))
    rows = [wire.copy(rowbuf.at[0], rowbuf.at[1 + i], tensor_peer(*p)) for i, p in enumerate(peers)]
    part = jnp.sum(grad * hidden * inverse, axis=0, keepdims=True)
    gx[0] = jnp.broadcast_to(part, (8, 384))
    gxd = [wire.copy(gx.at[0], gx.at[d], {"x": mod4(x + d)}) for d in (1, 2, 3)]
    for d in rows:
        d.wait_recv()
    total = rowbuf[0]
    for i in range(7):
        total = total + rowbuf[1 + i]
    row_inner = (
        jnp.sum(jnp.where(diagonal, total[0:1, :], 0.0), axis=1, keepdims=True) / 3072.0
    )
    sgrad_out[...] = (
        inverse * own_gain * grad - hidden * inverse * inverse * inverse * row_inner
    ).astype(BF16)
    for d in gxd:
        d.wait_recv()
    gy[0] = gx[0] + gx[1] + gx[2] + gx[3]
    gyd = [wire.copy(gy.at[0], gy.at[d], {"y": mod4(y + d)}) for d in (1, 2, 3)]

    sa1.finish()
    sa2.start()
    sb1.finish()
    sb2.start()
    for d in gyd:
        d.wait_recv()
    gz[0] = gy[0] + gy[1] + gy[2] + gy[3]
    gzd = wire.copy(gz.at[0], gz.at[1], {"zh": 1 - z})
    sa2.middle()
    sb2.middle()
    grad_scale = 1.0 / 64.0
    slot = 2 * y + z
    other = 2 * y + 1 - z
    sa2.finish()
    a3d = wire.copy(gp.at[x, other, :, pl.ds(0, 512)], a3, {"zh": 1 - z})
    sb2.finish()
    b3d = wire.copy(gp.at[x, other, :, pl.ds(512, 512)], b3, {"zh": 1 - z})
    gzd.wait_recv()
    ggrad_out[...] = (gz[0] + gz[1]) * grad_scale
    a3d.wait_recv()
    pgrad_out[:, 0:512] = (
        gp[x, slot, :, 0:512].astype(F32) + a3[...].astype(F32)
    ) * grad_scale
    b3d.wait_recv()
    pgrad_out[:, 512:1024] = (
        gp[x, slot, :, 512:1024].astype(F32) + b3[...].astype(F32)
    ) * grad_scale
    wire.drain()


def local(
    queries, keys, values, prefix_keys, prefix_values, doc_start, out_weight, residual,
    student_hidden, student_gain, proj_weight,
):
    vmem = pl.BlockSpec(memory_space=pltpu.VMEM)
    anyspace = pl.BlockSpec(memory_space=pl.ANY)
    smem = pl.BlockSpec(memory_space=pltpu.SMEM)
    v = pltpu.VMEM
    outs = pl.pallas_call(
        kernel,
        out_shape=(
            jax.ShapeDtypeStruct((128, 1024), BF16),
            jax.ShapeDtypeStruct((128, 384), BF16),
            jax.ShapeDtypeStruct((96, 1024), F32),
            jax.ShapeDtypeStruct((8, 384), F32),
        ),
        in_specs=[anyspace] * 5 + [smem] + [anyspace] * 3 + [vmem] + [anyspace],
        out_specs=(vmem, vmem, vmem, vmem),
        scratch_shapes=[
            v((32, 2, 128, 128), BF16),
            v((32, 2, 128, 128), BF16),
            v((32, 96, 1024), BF16),
            v((512, 8192), BF16),
            v((128, 512), BF16),
            v((512, 128), BF16),
            v((8, 128, 384), BF16),
            v((128, 1024), BF16),
            v((512, 128), F32),
            v((512, 128), F32),
            v((512, 128), F32),
            v((128, 512), BF16),
            v((4, 128, 1024), BF16),
            v((4, 128, 1024), BF16),
            v((3, 128, 1024), BF16),
            v((3, 128, 1024), BF16),
            v((128, 1024), F32),
            v((128, 3072), BF16),
            v((3072, 128), BF16),
            v((128, 1024), BF16),
            v((4, 128, 384), BF16),
            v((4, 128, 384), BF16),
            v((3, 128, 384), BF16),
            v((3, 128, 384), BF16),
            v((8, 8, 128), F32),
            v((4, 8, 384), F32),
            v((4, 8, 384), F32),
            v((2, 8, 384), F32),
            v((4, 8, 96, 1024), BF16),
            v((2, 8, 96, 256), BF16),
            v((2, 8, 96, 512), BF16),
            v((2, 2, 96, 256), BF16),
            v((2, 2, 96, 512), BF16),
            v((2, 4, 2, 96, 256), BF16),
            v((2, 4, 2, 96, 512), BF16),
            v((2, 2, 96, 256), BF16),
            v((2, 2, 96, 512), BF16),
            v((96, 512), BF16),
            v((96, 512), BF16),
            pltpu.SemaphoreType.DMA((SEMS,)),
            pltpu.SemaphoreType.DMA((SEMS,)),
            pltpu.SemaphoreType.DMA((9,)),
        ],
        compiler_params=pltpu.CompilerParams(
            collective_id=0, has_side_effects=True, vmem_limit_bytes=60 * 1024 * 1024
        ),
    )(
        queries, keys, values, prefix_keys, prefix_values, doc_start, out_weight, residual,
        student_hidden, student_gain.reshape(8, 1, 384), proj_weight,
    )
    teacher, sgrad, pgrad, ggrad = outs
    return teacher, sgrad, pgrad, ggrad[0]


def solution(mesh):
    finer = Mesh(mesh.devices.reshape(4, 4, 2, 4, 2), SEQ + TEN)
    rows = P(SEQ, TEN)
    return jax.shard_map(
        local,
        mesh=finer,
        in_specs=(
            rows, rows, rows, rows, rows, P(), P(TEN, None), P(SEQ + TEN, None), rows, P(), rows,
        ),
        out_specs=(rows, rows, rows, P(TEN)),
        check_vma=False,
    )
```

```python
import math

import jax
import jax.numpy as jnp
from jax import lax
from jax.experimental import pallas as pl
from jax.experimental.pallas import tpu as pltpu
from jax.sharding import Mesh
from jax.sharding import PartitionSpec as P

MESH = pl.DeviceIdType.MESH
F32 = jnp.float32
BF16 = jnp.bfloat16
NEG = -1e30
SEQ = ("x", "y", "zh")
TEN = ("zl", "c")
SEMS = 256


def mod4(v):
    return lax.rem(v, 4)


class Wire:
    def __init__(self, send, recv):
        self.send, self.recv, self.used, self.all = send, recv, 0, []

    def copy(self, src, dst, dev):
        i = self.used
        self.used += 1
        d = pltpu.make_async_remote_copy(
            src_ref=src,
            dst_ref=dst,
            send_sem=self.send.at[i],
            recv_sem=self.recv.at[i],
            device_id=dev,
            device_id_type=MESH,
        )
        d.start()
        self.all.append(d)
        return d

    def drain(self):
        for d in self.all:
            d.wait_send()


class Gather:
    def __init__(self, wire, at, first, second, coord):
        self.wire, self.at, self.first, self.second = wire, at, first, second
        self.a, self.b, self.z = coord[first], coord[second], coord["zh"]
        self.r, self.l, self.hr, self.hl = {}, {}, {}, {}
        a = self.a
        self.order = (a, mod4(a + 3), mod4(a + 1), mod4(a + 2))

    def z_send(self):
        own = self.at(self.a, self.b, self.z, 1, None)
        self.zd = self.wire.copy(own, own, {"zh": 1 - self.z})

    def z_wait(self):
        self.zd.wait_recv()

    def ring(self, key, ref_of, axis, pos):
        own = ref_of(pos, None)
        self.r[key] = self.wire.copy(own, own, {axis: mod4(pos + 1)})
        self.l[key] = self.wire.copy(own, own, {axis: mod4(pos + 3)})

    def forward(self, key, ref_of, axis, pos):
        self.r[key].wait_recv()
        left = ref_of(mod4(pos + 3), 0)
        self.hr[key] = self.wire.copy(left, left, {axis: mod4(pos + 1)})
        self.l[key].wait_recv()
        right = ref_of(mod4(pos + 1), 1)
        self.hl[key] = self.wire.copy(right, right, {axis: mod4(pos + 3)})

    def done(self, key):
        self.hr[key].wait_recv()
        self.hl[key].wait_recv()

    def one(self, j):
        zq = self.z if j == 0 else 1 - self.z
        return lambda pos, half: self.at(pos, self.b, zq, 1, half)

    def two(self, j, k):
        aq = self.order[k]
        if j is None:
            return lambda pos, half: self.at(aq, pos, 0, 2, half)
        zq = self.z if j == 0 else 1 - self.z
        return lambda pos, half: self.at(aq, pos, zq, 1, half)

    def p1_send(self, j):
        self.ring(("1", j), self.one(j), self.first, self.a)

    def p1_fwd(self, j):
        self.forward(("1", j), self.one(j), self.first, self.a)

    def p1_done(self, j):
        self.done(("1", j))

    def p2_send(self, j, k):
        self.ring(("2", j, k), self.two(j, k), self.second, self.b)

    def p2_fwd(self, j, k):
        self.forward(("2", j, k), self.two(j, k), self.second, self.b)

    def p2_done(self, j, k):
        self.done(("2", j, k))


class Scatter:
    def __init__(self, wire, part, near, far, axis, pos):
        self.wire, self.part, self.near, self.far = wire, part, near, far
        self.axis, self.pos = axis, pos

    def start(self):
        p, ax = self.pos, self.axis
        opp = mod4(p + 2)
        self.r1 = self.wire.copy(self.part(opp, 0), self.near.at[0], {ax: mod4(p + 1)})
        self.l1 = self.wire.copy(self.part(opp, 1), self.near.at[1], {ax: mod4(p + 3)})

    def middle(self):
        p, ax = self.pos, self.axis
        right, left = mod4(p + 1), mod4(p + 3)
        self.r1.wait_recv()
        ref = self.part(right, 0)
        ref[...] = (ref[...].astype(F32) + self.near[0].astype(F32)).astype(BF16)
        self.r2 = self.wire.copy(self.part(right, None), self.far.at[0], {ax: right})
        self.l1.wait_recv()
        ref = self.part(left, 1)
        ref[...] = (ref[...].astype(F32) + self.near[1].astype(F32)).astype(BF16)
        self.l2 = self.wire.copy(self.part(left, None), self.far.at[1], {ax: left})

    def finish(self):
        self.r2.wait_recv()
        self.l2.wait_recv()
        ref = self.part(self.pos, None)
        ref[...] = (
            ref[...].astype(F32) + self.far[0].astype(F32) + self.far[1].astype(F32)
        ).astype(BF16)


def kernel(
    q_hbm, k_hbm, v_hbm, pk_hbm, pv_hbm, doc, w_hbm, res_hbm, hid_hbm, gain, proj_hbm,
    teacher_out, sgrad_out, pgrad_out, ggrad_out,
    kv0, kv1, pj, w, q, qs, hid, res, mx, tot, acc, att,
    bsend, brecv, bz, zrecv, tacc, nrm, nrmt, nxt, mis, mch,
    fsend, frecv, fz, fzrecv, rowbuf, gx, gy, gz,
    gp, near, far, zpart,
    ssem, rsem, lsem,
):
    x, y, z = lax.axis_index("x"), lax.axis_index("y"), lax.axis_index("zh")
    zl, c = lax.axis_index("zl"), lax.axis_index("c")
    coord = {"x": x, "y": y, "zh": z}
    seq = (x * 4 + y) * 2 + z
    t = zl * 2 + c
    wire = Wire(ssem, rsem)
    mate = {"c": 1 - c}

    def tensor_peer(dz, dc):
        return {"zl": mod4(zl + dz), "c": c if dc == 0 else 1 - c}

    def tensor_index(dz, dc):
        return mod4(zl + dz) * 2 + (c if dc == 0 else 1 - c)

    peers = [(dz, dc) for dz in (2, 1, 3, 0) for dc in (0, 1) if (dz, dc) != (0, 0)]

    loads = [
        (pk_hbm, kv0.at[x, y, z, 0]),
        (pv_hbm, kv0.at[x, y, z, 1]),
        (k_hbm, kv1.at[x, y, z, 0]),
        (v_hbm, kv1.at[x, y, z, 1]),
        (proj_hbm, pj.at[seq]),
        (hid_hbm, hid.at[t]),
        (q_hbm, q),
        (
            res_hbm.at[:, pl.ds(pl.multiple_of(t * 1024, 1024), 1024)],
            res.at[pl.ds(pl.multiple_of(t * 16, 16), 16), :],
        ),
        (w_hbm, w),
    ]
    local = [pltpu.make_async_copy(s, d, lsem.at[i]) for i, (s, d) in enumerate(loads)]
    for d in local:
        d.start()

    barrier = pltpu.get_barrier_semaphore()
    greet = [
        {"x": mod4(x + 1)}, {"x": mod4(x + 2)}, {"x": mod4(x + 3)},
        {"y": mod4(y + 1)}, {"y": mod4(y + 2)}, {"y": mod4(y + 3)},
        {"zh": 1 - z},
    ] + [tensor_peer(*p) for p in peers]
    for dev in greet:
        pl.semaphore_signal(barrier, inc=1, device_id=dev, device_id_type=MESH)
    pl.semaphore_wait(barrier, len(greet))

    def kv_at(buf, x_first):
        def at(a, b, zq, count, half):
            ref = buf.at[a, b, zq] if x_first else buf.at[b, a, zq]
            return ref if half is None else ref.at[half]

        return at

    def pj_at(low, x_first):
        def at(a, b, zq, count, half):
            slot = ((a * 4 + b) if x_first else (b * 4 + a)) * 2 + zq
            where = slot if count == 1 else pl.ds(slot, 2)
            cols = pl.ds(0, 1024) if half is None else pl.ds(512 * half, 512)
            return pj.at[where, pl.ds(low, 48), cols]

        return at

    kv = (
        Gather(wire, kv_at(kv0, True), "x", "y", coord),
        Gather(wire, kv_at(kv1, False), "y", "x", coord),
    )
    pr = (
        Gather(wire, pj_at(0, True), "x", "y", coord),
        Gather(wire, pj_at(48, False), "y", "x", coord),
    )

    def both(streams, name, *args):
        for s in streams:
            getattr(s, name)(*args)

    factor = 128 ** (-0.5) * math.log2(math.e)
    column = lax.broadcasted_iota(jnp.int32, (512, 512), 1)
    token = lax.rem(lax.broadcasted_iota(jnp.int32, (512, 512), 0), 128) + seq * 128
    within = lax.rem(column, 128)
    piece = column // 128

    def wide(v):
        return jnp.concatenate([v] * 4, axis=1)

    def block(kb, vb, visible):
        s = lax.dot_general(
            qs[...], kb.reshape(512, 128), (((1,), (1,)), ((), ())), preferred_element_type=F32
        ) * factor
        s = jnp.where(visible, s, NEG)
        old = mx[...]
        new = jnp.maximum(old, jnp.broadcast_to(jnp.max(s, axis=1, keepdims=True), (512, 128)))
        p = jnp.exp2(s - wide(new))
        scale = jnp.exp2(old - new)
        mx[...] = new
        tot[...] = tot[...] * scale + jnp.broadcast_to(
            jnp.sum(p, axis=1, keepdims=True), (512, 128)
        )
        acc[...] = acc[...] * scale + jnp.dot(
            p.astype(BF16), vb.reshape(512, 128), preferred_element_type=F32
        )

    def attend(j, k):
        zq = z if j == 0 else 1 - z
        xq, yq = kv[0].order[k], kv[1].order[k]
        position = piece * 256 + within + (xq * 1024 + zq * 128)
        block(kv0[xq, :, zq, 0], kv0[xq, :, zq, 1], position >= doc[0])
        position = piece * 1024 + within + (yq * 256 + zq * 128)
        block(kv1[:, yq, zq, 0], kv1[:, yq, zq, 1], position <= token)

    for d in local[:4]:
        d.wait()
    both(kv, "z_send")
    both(kv, "p1_send", 0)
    both(kv, "p2_send", 0, 0)
    local[6].wait()
    for h in range(4):
        qs[pl.ds(h * 128, 128), :] = q[:, h * 128 : (h + 1) * 128]
    mx[...] = jnp.full((512, 128), NEG, F32)
    tot[...] = jnp.zeros((512, 128), F32)
    acc[...] = jnp.zeros((512, 128), F32)
    both(kv, "p1_fwd", 0)
    both(kv, "p2_send", 0, 1)
    both(kv, "p2_send", 0, 2)
    both(kv, "z_wait")
    both(kv, "p1_send", 1)
    both(kv, "p2_send", 1, 0)
    local[5].wait()
    hz = {dz: wire.copy(hid.at[t], hid.at[t], tensor_peer(dz, 0)) for dz in (2, 1, 3)}
    hmate = [wire.copy(hid.at[t], hid.at[t], mate)]
    local[4].wait()
    both(pr, "z_send")
    both(kv, "p2_fwd", 0, 0)
    both(kv, "p1_done", 0)
    both(kv, "p2_send", 0, 3)
    both(kv, "p1_fwd", 1)
    both(kv, "p2_send", 1, 1)
    both(kv, "p2_send", 1, 2)
    both(kv, "p2_fwd", 0, 1)
    both(kv, "p2_done", 0, 0)
    attend(0, 0)
    both(kv, "p1_done", 1)
    both(kv, "p2_send", 1, 3)
    both(kv, "p2_fwd", 0, 2)
    rsend = []
    for p in peers:
        cols = pl.ds(pl.multiple_of(tensor_index(*p) * 1024, 1024), 1024)
        rsend.append(
            wire.copy(
                res_hbm.at[:, cols],
                res.at[pl.ds(pl.multiple_of(t * 16, 16), 16), :],
                tensor_peer(*p),
            )
        )
    both(pr, "p1_send", 0)
    both(kv, "p2_done", 0, 1)
    attend(0, 1)
    both(kv, "p2_fwd", 0, 3)
    both(kv, "p2_done", 0, 2)
    attend(0, 2)
    both(kv, "p2_fwd", 1, 0)
    for dz in (2, 1, 3):
        hz[dz].wait_recv()
        slot = mod4(zl + 4 - dz) * 2 + c
        hmate.append(wire.copy(hid.at[slot], hid.at[slot], mate))
    both(kv, "p2_done", 0, 3)
    attend(0, 3)
    both(kv, "p2_fwd", 1, 1)
    both(pr, "z_wait")
    both(pr, "p1_send", 1)
    both(pr, "p2_send", None, 0)
    both(kv, "p2_done", 1, 0)
    attend(1, 0)
    both(kv, "p2_fwd", 1, 2)
    both(pr, "p1_fwd", 0)
    both(kv, "p2_done", 1, 1)
    attend(1, 1)
    both(kv, "p2_fwd", 1, 3)
    both(kv, "p2_done", 1, 2)
    attend(1, 2)
    both(pr, "p1_fwd", 1)
    both(pr, "p2_send", None, 1)
    both(pr, "p2_send", None, 2)
    both(kv, "p2_done", 1, 3)
    attend(1, 3)
    for h in range(4):
        rows = pl.ds(h * 128, 128)
        att[:, h * 128 : (h + 1) * 128] = (acc[rows, :] / tot[rows, :]).astype(BF16)

    local[8].wait()
    turns = (2, 1, 3, 0)

    def projected(dz, dc):
        cols = pl.ds(pl.multiple_of(tensor_index(dz, dc) * 1024, 1024), 1024)
        return jnp.dot(att[...], w[:, cols], preferred_element_type=F32)

    half = {}
    for dz in turns:
        bsend[dz] = projected(dz, 1).astype(BF16)
        half[dz] = wire.copy(bsend.at[dz], brecv.at[dz], mate)
    zsum = {}
    for dz in turns:
        mine = projected(dz, 0)
        half[dz].wait_recv()
        mine = mine + brecv[dz].astype(F32)
        if dz:
            bz[dz - 1] = mine.astype(BF16)
            zsum[dz] = wire.copy(bz.at[dz - 1], zrecv.at[dz - 1], tensor_peer(dz, 0))
        else:
            tacc[...] = mine
    both(pr, "p1_done", 0)
    both(pr, "p1_done", 1)
    both(pr, "p2_send", None, 3)

    for d in hmate:
        d.wait_recv()
    square = jnp.zeros((128, 384), F32)
    for i in range(8):
        h = hid[i].astype(F32)
        square = square + h * h
    inverse = lax.rsqrt(jnp.sum(square, axis=1, keepdims=True) / 3072.0 + 1e-05)
    for i in range(8):
        n = (hid[i].astype(F32) * inverse * gain[i]).astype(BF16)
        nrm[:, i * 384 : (i + 1) * 384] = n
        nrmt[i] = n.T

    def nxt_at(xq, core):
        return nxt.at[
            pl.ds(pl.multiple_of(core * 384, 384), 384),
            pl.ds(pl.multiple_of(xq * 128, 128), 128),
        ]

    nx = {}
    for d in (2, 1, 3):
        nx[d] = wire.copy(nrmt.at[mod4(x + d) * 2 + c], nxt_at(x, c), {"x": mod4(x + d)})
    for i in range(2):
        nxt[i * 384 : (i + 1) * 384, pl.ds(pl.multiple_of(x * 128, 128), 128)] = nrmt[2 * x + i]
    both(pr, "p2_fwd", None, 0)
    both(pr, "p2_fwd", None, 1)
    both(pr, "p2_fwd", None, 2)
    nmate = []
    for d in (2, 1, 3):
        nx[d].wait_recv()
        came = nxt_at(mod4(x + 4 - d), c)
        nmate.append(wire.copy(came, came, mate))
    both(pr, "p2_fwd", None, 3)
    for d in rsend:
        d.wait_recv()
    local[7].wait()
    tacc[...] = tacc[...] + res[...].astype(F32)
    for k in range(4):
        both(pr, "p2_done", None, k)
    pre = jnp.zeros((128, 1024), F32)
    for i in range(4):
        pre = pre + jnp.dot(
            nrm[:, i * 768 : (i + 1) * 768],
            pj[pl.ds(8 * i, 8)].reshape(768, 1024),
            preferred_element_type=F32,
        )
    for dz in turns[:3]:
        zsum[dz].wait_recv()
    teacher = (
        tacc[...] + zrecv[0].astype(F32) + zrecv[1].astype(F32) + zrecv[2].astype(F32)
    ).astype(BF16)
    teacher_out[...] = teacher
    mismatch = (pre - teacher.astype(F32)).astype(BF16)
    mis[...] = mismatch
    for i in range(4):
        mch[i, x] = mismatch[:, i * 256 : (i + 1) * 256]

    def mch_at(i):
        return lambda p, h: mch.at[i, p] if h is None else mch.at[i, p, pl.ds(64 * h, 64)]

    ring = Gather(wire, None, "x", "y", coord)
    sums = []
    for i in range(4):
        ring.ring(i, mch_at(i), "x", x)
        sums.append(
            Scatter(
                wire,
                lambda p, h, i=i: gp.at[i, p] if h is None else gp.at[i, p, h],
                near.at[i],
                far.at[i],
                "y",
                y,
            )
        )

    def product(i):
        ring.done(i)
        g = jnp.dot(nxt[...], mch[i].reshape(512, 256), preferred_element_type=F32)
        gp[i] = g.astype(BF16).reshape(4, 2, 96, 256)
        sums[i].start()

    last = {}

    def across(i):
        sums[i].finish()
        last[i] = wire.copy(gp.at[i, y, 1 - z], zpart.at[i], {"zh": 1 - z})

    def state_grad(dz, dc):
        rows = pj[pl.ds(4 * tensor_index(dz, dc), 4)].reshape(384, 1024)
        return lax.dot_general(
            mis[...], rows, (((1,), (1,)), ((), ())), preferred_element_type=F32
        )

    def to_mate(dz):
        fsend[dz] = state_grad(dz, 1).astype(BF16)
        half[dz] = wire.copy(fsend.at[dz], frecv.at[dz], mate)

    def along_z(dz):
        mine = state_grad(dz, 0)
        half[dz].wait_recv()
        mine = mine + frecv[dz].astype(F32)
        if dz == 0:
            return mine
        fz[dz - 1] = mine.astype(BF16)
        zsum[dz] = wire.copy(fz.at[dz - 1], fzrecv.at[dz - 1], tensor_peer(dz, 0))
        return None

    for dz in turns:
        to_mate(dz)
    for d in nmate:
        d.wait_recv()
    for i in range(4):
        ring.forward(i, mch_at(i), "x", x)
    along_z(2)
    along_z(1)
    product(0)
    along_z(3)
    product(1)
    sums[0].middle()
    product(2)
    sums[1].middle()
    product(3)
    grad = along_z(0)
    sums[2].middle()
    across(0)
    sums[3].middle()
    across(1)
    for dz in turns[:3]:
        zsum[dz].wait_recv()
    grad = grad + fzrecv[0].astype(F32) + fzrecv[1].astype(F32) + fzrecv[2].astype(F32)
    hidden = hid[t].astype(F32)
    own_gain = gain[t]
    inner = jnp.sum(grad * own_gain * hidden, axis=1, keepdims=True)
    diagonal = lax.broadcasted_iota(jnp.int32, (128, 128), 0) == lax.broadcasted_iota(
        jnp.int32, (128, 128), 1
    )
    as_row = jnp.sum(jnp.where(diagonal, inner, 0.0), axis=0, keepdims=True)
    rowbuf[0] = jnp.broadcast_to(as_row, (8, 128))
    rows = [wire.copy(rowbuf.at[0], rowbuf.at[1 + i], tensor_peer(*p)) for i, p in enumerate(peers)]
    part = jnp.sum(grad * hidden * inverse, axis=0, keepdims=True)
    gx[0] = jnp.broadcast_to(part, (8, 384))
    gxd = [wire.copy(gx.at[0], gx.at[d], {"x": mod4(x + d)}) for d in (1, 2, 3)]
    across(2)
    for d in gxd:
        d.wait_recv()
    gy[0] = gx[0] + gx[1] + gx[2] + gx[3]
    gyd = [wire.copy(gy.at[0], gy.at[d], {"y": mod4(y + d)}) for d in (1, 2, 3)]
    across(3)
    for d in gyd:
        d.wait_recv()
    gz[0] = gy[0] + gy[1] + gy[2] + gy[3]
    gzd = wire.copy(gz.at[0], gz.at[1], {"zh": 1 - z})
    for d in rows:
        d.wait_recv()
    total = rowbuf[0]
    for i in range(7):
        total = total + rowbuf[1 + i]
    row_inner = (
        jnp.sum(jnp.where(diagonal, total[0:1, :], 0.0), axis=1, keepdims=True) / 3072.0
    )
    sgrad_out[...] = (
        inverse * own_gain * grad - hidden * inverse * inverse * inverse * row_inner
    ).astype(BF16)
    grad_scale = 1.0 / 64.0
    for i in range(4):
        last[i].wait_recv()
        pgrad_out[:, i * 256 : (i + 1) * 256] = (
            gp[i, y, z].astype(F32) + zpart[i].astype(F32)
        ) * grad_scale
    gzd.wait_recv()
    ggrad_out[...] = (gz[0] + gz[1]) * grad_scale
    wire.drain()


def hand_over(a, b, c, d, a_out, b_out, c_out, d_out):
    a_out[...] = a[...]
    b_out[...] = b[...]
    c_out[...] = c[...]
    d_out[...] = d[0]


def local(
    queries, keys, values, prefix_keys, prefix_values, doc_start, out_weight, residual,
    student_hidden, student_gain, proj_weight,
):
    vmem = pl.BlockSpec(memory_space=pltpu.VMEM)
    anyspace = pl.BlockSpec(memory_space=pl.ANY)
    smem = pl.BlockSpec(memory_space=pltpu.SMEM)
    v = pltpu.VMEM
    shapes = [
        jax.ShapeDtypeStruct((128, 1024), BF16),
        jax.ShapeDtypeStruct((128, 384), BF16),
        jax.ShapeDtypeStruct((96, 1024), F32),
    ]
    outs = pl.pallas_call(
        kernel,
        out_shape=(*shapes, jax.ShapeDtypeStruct((8, 384), F32)),
        in_specs=[anyspace] * 5 + [smem] + [anyspace] * 3 + [vmem] + [anyspace],
        out_specs=(vmem, vmem, vmem, vmem),
        scratch_shapes=[
            v((4, 4, 2, 2, 128, 128), BF16),
            v((4, 4, 2, 2, 128, 128), BF16),
            v((32, 96, 1024), BF16),
            v((512, 8192), BF16),
            v((128, 512), BF16),
            v((512, 128), BF16),
            v((8, 128, 384), BF16),
            v((128, 1024), BF16),
            v((512, 128), F32),
            v((512, 128), F32),
            v((512, 128), F32),
            v((128, 512), BF16),
            v((4, 128, 1024), BF16),
            v((4, 128, 1024), BF16),
            v((3, 128, 1024), BF16),
            v((3, 128, 1024), BF16),
            v((128, 1024), F32),
            v((128, 3072), BF16),
            v((8, 384, 128), BF16),
            v((768, 512), BF16),
            v((128, 1024), BF16),
            v((4, 4, 128, 256), BF16),
            v((4, 128, 384), BF16),
            v((4, 128, 384), BF16),
            v((3, 128, 384), BF16),
            v((3, 128, 384), BF16),
            v((8, 8, 128), F32),
            v((4, 8, 384), F32),
            v((4, 8, 384), F32),
            v((2, 8, 384), F32),
            v((4, 4, 2, 96, 256), BF16),
            v((4, 2, 96, 256), BF16),
            v((4, 2, 2, 96, 256), BF16),
            v((4, 96, 256), BF16),
            pltpu.SemaphoreType.DMA((SEMS,)),
            pltpu.SemaphoreType.DMA((SEMS,)),
            pltpu.SemaphoreType.DMA((9,)),
        ],
        compiler_params=pltpu.CompilerParams(
            collective_id=0, has_side_effects=True, vmem_limit_bytes=60 * 1024 * 1024
        ),
    )(
        queries, keys, values, prefix_keys, prefix_values, doc_start, out_weight, residual,
        student_hidden, student_gain.reshape(8, 1, 384), proj_weight,
    )
    return pl.pallas_call(
        hand_over,
        out_shape=(*shapes, jax.ShapeDtypeStruct((384,), F32)),
        in_specs=[vmem] * 4,
        out_specs=(vmem,) * 4,
    )(*outs)


def solution(mesh):
    finer = Mesh(mesh.devices.reshape(4, 4, 2, 4, 2), SEQ + TEN)
    rows = P(SEQ, TEN)
    return jax.shard_map(
        local,
        mesh=finer,
        in_specs=(
            rows, rows, rows, rows, rows, P(), P(TEN, None), P(SEQ + TEN, None), rows, P(), rows,
        ),
        out_specs=(rows, rows, rows, P(TEN)),
        check_vma=False,
    )
```

```python
import math

import jax
import jax.numpy as jnp
from jax import lax
from jax.experimental import pallas as pl
from jax.experimental.pallas import tpu as pltpu
from jax.sharding import Mesh
from jax.sharding import PartitionSpec as P

MESH = pl.DeviceIdType.MESH
F32 = jnp.float32
BF16 = jnp.bfloat16
NEG = -1e30
SEQ = ("x", "y", "zh")
TEN = ("zl", "c")
SEMS = 256


def mod4(v):
    return lax.rem(v, 4)


class Wire:
    def __init__(self, send, recv):
        self.send, self.recv, self.used, self.all = send, recv, 0, []

    def copy(self, src, dst, dev):
        i = self.used
        self.used += 1
        d = pltpu.make_async_remote_copy(
            src_ref=src,
            dst_ref=dst,
            send_sem=self.send.at[i],
            recv_sem=self.recv.at[i],
            device_id=dev,
            device_id_type=MESH,
        )
        d.start()
        self.all.append(d)
        return d

    def drain(self):
        for d in self.all:
            d.wait_send()


class Gather:
    def __init__(self, wire, at, first, second, coord):
        self.wire, self.at, self.first, self.second = wire, at, first, second
        self.a, self.b, self.z = coord[first], coord[second], coord["zh"]
        self.r, self.l, self.hr, self.hl = {}, {}, {}, {}
        a = self.a
        self.order = (a, mod4(a + 3), mod4(a + 1), mod4(a + 2))

    def z_send(self):
        own = self.at(self.a, self.b, self.z, 1, None)
        self.zd = self.wire.copy(own, own, {"zh": 1 - self.z})

    def z_wait(self):
        self.zd.wait_recv()

    def ring(self, key, ref_of, axis, pos):
        own = ref_of(pos, None)
        self.r[key] = self.wire.copy(own, own, {axis: mod4(pos + 1)})
        self.l[key] = self.wire.copy(own, own, {axis: mod4(pos + 3)})

    def forward(self, key, ref_of, axis, pos):
        self.r[key].wait_recv()
        left = ref_of(mod4(pos + 3), 0)
        self.hr[key] = self.wire.copy(left, left, {axis: mod4(pos + 1)})
        self.l[key].wait_recv()
        right = ref_of(mod4(pos + 1), 1)
        self.hl[key] = self.wire.copy(right, right, {axis: mod4(pos + 3)})

    def done(self, key):
        self.hr[key].wait_recv()
        self.hl[key].wait_recv()

    def one(self, j):
        zq = self.z if j == 0 else 1 - self.z
        return lambda pos, half: self.at(pos, self.b, zq, 1, half)

    def two(self, j, k):
        aq = self.order[k]
        if j is None:
            return lambda pos, half: self.at(aq, pos, 0, 2, half)
        zq = self.z if j == 0 else 1 - self.z
        return lambda pos, half: self.at(aq, pos, zq, 1, half)

    def p1_send(self, j):
        self.ring(("1", j), self.one(j), self.first, self.a)

    def p1_fwd(self, j):
        self.forward(("1", j), self.one(j), self.first, self.a)

    def p1_done(self, j):
        self.done(("1", j))

    def p2_send(self, j, k):
        self.ring(("2", j, k), self.two(j, k), self.second, self.b)

    def p2_fwd(self, j, k):
        self.forward(("2", j, k), self.two(j, k), self.second, self.b)

    def p2_done(self, j, k):
        self.done(("2", j, k))


class Scatter:
    def __init__(self, wire, part, near, far, axis, pos):
        self.wire, self.part, self.near, self.far = wire, part, near, far
        self.axis, self.pos = axis, pos

    def start(self):
        p, ax = self.pos, self.axis
        opp = mod4(p + 2)
        self.r1 = self.wire.copy(self.part(opp, 0), self.near.at[0], {ax: mod4(p + 1)})
        self.l1 = self.wire.copy(self.part(opp, 1), self.near.at[1], {ax: mod4(p + 3)})

    def middle(self):
        p, ax = self.pos, self.axis
        right, left = mod4(p + 1), mod4(p + 3)
        self.r1.wait_recv()
        ref = self.part(right, 0)
        ref[...] = (ref[...].astype(F32) + self.near[0].astype(F32)).astype(BF16)
        self.r2 = self.wire.copy(self.part(right, None), self.far.at[0], {ax: right})
        self.l1.wait_recv()
        ref = self.part(left, 1)
        ref[...] = (ref[...].astype(F32) + self.near[1].astype(F32)).astype(BF16)
        self.l2 = self.wire.copy(self.part(left, None), self.far.at[1], {ax: left})

    def finish(self):
        self.r2.wait_recv()
        self.l2.wait_recv()
        ref = self.part(self.pos, None)
        ref[...] = (
            ref[...].astype(F32) + self.far[0].astype(F32) + self.far[1].astype(F32)
        ).astype(BF16)


def kernel(
    q_hbm, k_hbm, v_hbm, pk_hbm, pv_hbm, doc, w_hbm, res_hbm, hid_hbm, gain, proj_hbm,
    teacher_out, sgrad_out, pgrad_out, ggrad_out,
    kv0, kv1, pj, w, q, qs, hid, res, mx, tot, acc, att,
    bsend, brecv, bz, zrecv, tacc, nrm, nrmt, nxt, mis, mch,
    fsend, frecv, fz, fzrecv, rowbuf, gx, gy, gz,
    gp, near, far, zpart, tcb, sgb, pgb, ggb,
    ssem, rsem, lsem,
):
    x, y, z = lax.axis_index("x"), lax.axis_index("y"), lax.axis_index("zh")
    zl, c = lax.axis_index("zl"), lax.axis_index("c")
    coord = {"x": x, "y": y, "zh": z}
    seq = (x * 4 + y) * 2 + z
    t = zl * 2 + c
    wire = Wire(ssem, rsem)
    mate = {"c": 1 - c}

    def tensor_peer(dz, dc):
        return {"zl": mod4(zl + dz), "c": c if dc == 0 else 1 - c}

    def tensor_index(dz, dc):
        return mod4(zl + dz) * 2 + (c if dc == 0 else 1 - c)

    peers = [(dz, dc) for dz in (2, 1, 3, 0) for dc in (0, 1) if (dz, dc) != (0, 0)]

    loads = [
        (pk_hbm, kv0.at[x, y, z, 0]),
        (pv_hbm, kv0.at[x, y, z, 1]),
        (k_hbm, kv1.at[x, y, z, 0]),
        (v_hbm, kv1.at[x, y, z, 1]),
        (proj_hbm, pj.at[seq]),
        (hid_hbm, hid.at[t]),
        (q_hbm, q),
        (
            res_hbm.at[:, pl.ds(pl.multiple_of(t * 1024, 1024), 1024)],
            res.at[pl.ds(pl.multiple_of(t * 16, 16), 16), :],
        ),
        (w_hbm, w),
    ]
    local = [pltpu.make_async_copy(s, d, lsem.at[i]) for i, (s, d) in enumerate(loads)]
    for d in local:
        d.start()

    written = []

    def put(src, dst):
        d = pltpu.make_async_copy(src, dst, lsem.at[len(loads) + len(written)])
        d.start()
        written.append(d)

    barrier = pltpu.get_barrier_semaphore()
    greet = [
        {"x": mod4(x + 1)}, {"x": mod4(x + 2)}, {"x": mod4(x + 3)},
        {"y": mod4(y + 1)}, {"y": mod4(y + 2)}, {"y": mod4(y + 3)},
        {"zh": 1 - z},
    ] + [tensor_peer(*p) for p in peers]
    for dev in greet:
        pl.semaphore_signal(barrier, inc=1, device_id=dev, device_id_type=MESH)
    pl.semaphore_wait(barrier, len(greet))

    def kv_at(buf, x_first):
        def at(a, b, zq, count, half):
            ref = buf.at[a, b, zq] if x_first else buf.at[b, a, zq]
            return ref if half is None else ref.at[half]

        return at

    def pj_at(low, x_first):
        def at(a, b, zq, count, half):
            slot = ((a * 4 + b) if x_first else (b * 4 + a)) * 2 + zq
            where = slot if count == 1 else pl.ds(slot, 2)
            cols = pl.ds(0, 1024) if half is None else pl.ds(512 * half, 512)
            return pj.at[where, pl.ds(low, 48), cols]

        return at

    kv = (
        Gather(wire, kv_at(kv0, True), "x", "y", coord),
        Gather(wire, kv_at(kv1, False), "y", "x", coord),
    )
    pr = (
        Gather(wire, pj_at(0, True), "x", "y", coord),
        Gather(wire, pj_at(48, False), "y", "x", coord),
    )

    def both(streams, name, *args):
        for s in streams:
            getattr(s, name)(*args)

    factor = 128 ** (-0.5) * math.log2(math.e)
    column = lax.broadcasted_iota(jnp.int32, (512, 512), 1)
    token = lax.rem(lax.broadcasted_iota(jnp.int32, (512, 512), 0), 128) + seq * 128
    within = lax.rem(column, 128)
    piece = column // 128

    def wide(v):
        return jnp.concatenate([v] * 4, axis=1)

    def block(kb, vb, visible):
        s = lax.dot_general(
            qs[...], kb.reshape(512, 128), (((1,), (1,)), ((), ())), preferred_element_type=F32
        ) * factor
        s = jnp.where(visible, s, NEG)
        old = mx[...]
        new = jnp.maximum(old, jnp.broadcast_to(jnp.max(s, axis=1, keepdims=True), (512, 128)))
        p = jnp.exp2(s - wide(new))
        scale = jnp.exp2(old - new)
        mx[...] = new
        tot[...] = tot[...] * scale + jnp.broadcast_to(
            jnp.sum(p, axis=1, keepdims=True), (512, 128)
        )
        acc[...] = acc[...] * scale + jnp.dot(
            p.astype(BF16), vb.reshape(512, 128), preferred_element_type=F32
        )

    def attend(j, k):
        zq = z if j == 0 else 1 - z
        xq, yq = kv[0].order[k], kv[1].order[k]
        position = piece * 256 + within + (xq * 1024 + zq * 128)
        block(kv0[xq, :, zq, 0], kv0[xq, :, zq, 1], position >= doc[0])
        position = piece * 1024 + within + (yq * 256 + zq * 128)
        block(kv1[:, yq, zq, 0], kv1[:, yq, zq, 1], position <= token)

    for d in local[:4]:
        d.wait()
    both(kv, "z_send")
    both(kv, "p1_send", 0)
    both(kv, "p2_send", 0, 0)
    local[6].wait()
    for h in range(4):
        qs[pl.ds(h * 128, 128), :] = q[:, h * 128 : (h + 1) * 128]
    mx[...] = jnp.full((512, 128), NEG, F32)
    tot[...] = jnp.zeros((512, 128), F32)
    acc[...] = jnp.zeros((512, 128), F32)
    both(kv, "p1_fwd", 0)
    both(kv, "p2_send", 0, 1)
    both(kv, "p2_send", 0, 2)
    both(kv, "z_wait")
    both(kv, "p1_send", 1)
    both(kv, "p2_send", 1, 0)
    local[5].wait()
    hz = {dz: wire.copy(hid.at[t], hid.at[t], tensor_peer(dz, 0)) for dz in (2, 1, 3)}
    hmate = [wire.copy(hid.at[t], hid.at[t], mate)]
    local[4].wait()
    both(pr, "z_send")
    both(kv, "p2_fwd", 0, 0)
    both(kv, "p1_done", 0)
    both(kv, "p2_send", 0, 3)
    both(kv, "p1_fwd", 1)
    both(kv, "p2_send", 1, 1)
    both(kv, "p2_send", 1, 2)
    both(kv, "p2_fwd", 0, 1)
    both(kv, "p2_done", 0, 0)
    attend(0, 0)
    both(kv, "p1_done", 1)
    both(kv, "p2_send", 1, 3)
    both(kv, "p2_fwd", 0, 2)
    rsend = []
    for p in peers:
        cols = pl.ds(pl.multiple_of(tensor_index(*p) * 1024, 1024), 1024)
        rsend.append(
            wire.copy(
                res_hbm.at[:, cols],
                res.at[pl.ds(pl.multiple_of(t * 16, 16), 16), :],
                tensor_peer(*p),
            )
        )
    both(pr, "p1_send", 0)
    both(kv, "p2_done", 0, 1)
    attend(0, 1)
    both(kv, "p2_fwd", 0, 3)
    both(kv, "p2_done", 0, 2)
    attend(0, 2)
    both(kv, "p2_fwd", 1, 0)
    for dz in (2, 1, 3):
        hz[dz].wait_recv()
        slot = mod4(zl + 4 - dz) * 2 + c
        hmate.append(wire.copy(hid.at[slot], hid.at[slot], mate))
    both(kv, "p2_done", 0, 3)
    attend(0, 3)
    both(kv, "p2_fwd", 1, 1)
    both(pr, "z_wait")
    both(pr, "p1_send", 1)
    both(pr, "p2_send", None, 0)
    both(kv, "p2_done", 1, 0)
    attend(1, 0)
    both(kv, "p2_fwd", 1, 2)
    both(pr, "p1_fwd", 0)
    both(kv, "p2_done", 1, 1)
    attend(1, 1)
    both(kv, "p2_fwd", 1, 3)
    both(kv, "p2_done", 1, 2)
    attend(1, 2)
    both(pr, "p1_fwd", 1)
    both(pr, "p2_send", None, 1)
    both(pr, "p2_send", None, 2)
    both(kv, "p2_done", 1, 3)
    attend(1, 3)
    for h in range(4):
        rows = pl.ds(h * 128, 128)
        att[:, h * 128 : (h + 1) * 128] = (acc[rows, :] / tot[rows, :]).astype(BF16)

    local[8].wait()
    turns = (2, 1, 3, 0)

    def projected(dz, dc):
        cols = pl.ds(pl.multiple_of(tensor_index(dz, dc) * 1024, 1024), 1024)
        return jnp.dot(att[...], w[:, cols], preferred_element_type=F32)

    half = {}
    for dz in turns:
        bsend[dz] = projected(dz, 1).astype(BF16)
        half[dz] = wire.copy(bsend.at[dz], brecv.at[dz], mate)
    zsum = {}
    for dz in turns:
        mine = projected(dz, 0)
        half[dz].wait_recv()
        mine = mine + brecv[dz].astype(F32)
        if dz:
            bz[dz - 1] = mine.astype(BF16)
            zsum[dz] = wire.copy(bz.at[dz - 1], zrecv.at[dz - 1], tensor_peer(dz, 0))
        else:
            tacc[...] = mine
    both(pr, "p1_done", 0)
    both(pr, "p1_done", 1)
    both(pr, "p2_send", None, 3)

    for d in hmate:
        d.wait_recv()
    square = jnp.zeros((128, 384), F32)
    for i in range(8):
        h = hid[i].astype(F32)
        square = square + h * h
    inverse = lax.rsqrt(jnp.sum(square, axis=1, keepdims=True) / 3072.0 + 1e-05)
    for i in range(8):
        n = (hid[i].astype(F32) * inverse * gain[i]).astype(BF16)
        nrm[:, i * 384 : (i + 1) * 384] = n
        nrmt[i] = n.T

    def nxt_at(xq, core):
        return nxt.at[
            pl.ds(pl.multiple_of(core * 384, 384), 384),
            pl.ds(pl.multiple_of(xq * 128, 128), 128),
        ]

    nx = {}
    for d in (2, 1, 3):
        nx[d] = wire.copy(nrmt.at[mod4(x + d) * 2 + c], nxt_at(x, c), {"x": mod4(x + d)})
    for i in range(2):
        nxt[i * 384 : (i + 1) * 384, pl.ds(pl.multiple_of(x * 128, 128), 128)] = nrmt[2 * x + i]
    both(pr, "p2_fwd", None, 0)
    both(pr, "p2_fwd", None, 1)
    both(pr, "p2_fwd", None, 2)
    nmate = []
    for d in (2, 1, 3):
        nx[d].wait_recv()
        came = nxt_at(mod4(x + 4 - d), c)
        nmate.append(wire.copy(came, came, mate))
    both(pr, "p2_fwd", None, 3)
    for d in rsend:
        d.wait_recv()
    local[7].wait()
    tacc[...] = tacc[...] + res[...].astype(F32)
    for k in range(4):
        both(pr, "p2_done", None, k)
    pre = jnp.zeros((128, 1024), F32)
    for i in range(4):
        pre = pre + jnp.dot(
            nrm[:, i * 768 : (i + 1) * 768],
            pj[pl.ds(8 * i, 8)].reshape(768, 1024),
            preferred_element_type=F32,
        )
    for dz in turns[:3]:
        zsum[dz].wait_recv()
    teacher = (
        tacc[...] + zrecv[0].astype(F32) + zrecv[1].astype(F32) + zrecv[2].astype(F32)
    ).astype(BF16)
    tcb[...] = teacher
    put(tcb, teacher_out)
    mismatch = (pre - teacher.astype(F32)).astype(BF16)
    mis[...] = mismatch
    for i in range(4):
        mch[i, x] = mismatch[:, i * 256 : (i + 1) * 256]

    def mch_at(i):
        return lambda p, h: mch.at[i, p] if h is None else mch.at[i, p, pl.ds(64 * h, 64)]

    ring = Gather(wire, None, "x", "y", coord)
    sums = []
    for i in range(4):
        ring.ring(i, mch_at(i), "x", x)
        sums.append(
            Scatter(
                wire,
                lambda p, h, i=i: gp.at[i, p] if h is None else gp.at[i, p, h],
                near.at[i],
                far.at[i],
                "y",
                y,
            )
        )

    def product(i):
        ring.done(i)
        g = jnp.dot(nxt[...], mch[i].reshape(512, 256), preferred_element_type=F32)
        gp[i] = g.astype(BF16).reshape(4, 2, 96, 256)
        sums[i].start()

    last = {}

    def across(i):
        sums[i].finish()
        last[i] = wire.copy(gp.at[i, y, 1 - z], zpart.at[i], {"zh": 1 - z})

    def state_grad(dz, dc):
        rows = pj[pl.ds(4 * tensor_index(dz, dc), 4)].reshape(384, 1024)
        return lax.dot_general(
            mis[...], rows, (((1,), (1,)), ((), ())), preferred_element_type=F32
        )

    def to_mate(dz):
        fsend[dz] = state_grad(dz, 1).astype(BF16)
        half[dz] = wire.copy(fsend.at[dz], frecv.at[dz], mate)

    def along_z(dz):
        mine = state_grad(dz, 0)
        half[dz].wait_recv()
        mine = mine + frecv[dz].astype(F32)
        if dz == 0:
            return mine
        fz[dz - 1] = mine.astype(BF16)
        zsum[dz] = wire.copy(fz.at[dz - 1], fzrecv.at[dz - 1], tensor_peer(dz, 0))
        return None

    for dz in turns:
        to_mate(dz)
    along_z(2)
    along_z(1)
    ring.forward(0, mch_at(0), "x", x)
    along_z(3)
    ring.forward(1, mch_at(1), "x", x)
    grad = along_z(0)
    for d in nmate:
        d.wait_recv()
    ring.forward(2, mch_at(2), "x", x)
    product(0)
    ring.forward(3, mch_at(3), "x", x)
    product(1)
    sums[0].middle()
    product(2)
    sums[1].middle()
    product(3)
    for dz in turns[:3]:
        zsum[dz].wait_recv()
    grad = grad + fzrecv[0].astype(F32) + fzrecv[1].astype(F32) + fzrecv[2].astype(F32)
    hidden = hid[t].astype(F32)
    own_gain = gain[t]
    inner = jnp.sum(grad * own_gain * hidden, axis=1, keepdims=True)
    diagonal = lax.broadcasted_iota(jnp.int32, (128, 128), 0) == lax.broadcasted_iota(
        jnp.int32, (128, 128), 1
    )
    as_row = jnp.sum(jnp.where(diagonal, inner, 0.0), axis=0, keepdims=True)
    rowbuf[0] = jnp.broadcast_to(as_row, (8, 128))
    rows = [wire.copy(rowbuf.at[0], rowbuf.at[1 + i], tensor_peer(*p)) for i, p in enumerate(peers)]
    part = jnp.sum(grad * hidden * inverse, axis=0, keepdims=True)
    gx[0] = jnp.broadcast_to(part, (8, 384))
    gxd = [wire.copy(gx.at[0], gx.at[d], {"x": mod4(x + d)}) for d in (1, 2, 3)]
    sums[2].middle()
    across(0)
    for d in gxd:
        d.wait_recv()
    gy[0] = gx[0] + gx[1] + gx[2] + gx[3]
    gyd = [wire.copy(gy.at[0], gy.at[d], {"y": mod4(y + d)}) for d in (1, 2, 3)]
    sums[3].middle()
    across(1)
    for d in rows:
        d.wait_recv()
    total = rowbuf[0]
    for i in range(7):
        total = total + rowbuf[1 + i]
    row_inner = (
        jnp.sum(jnp.where(diagonal, total[0:1, :], 0.0), axis=1, keepdims=True) / 3072.0
    )
    sgb[...] = (
        inverse * own_gain * grad - hidden * inverse * inverse * inverse * row_inner
    ).astype(BF16)
    put(sgb, sgrad_out)
    across(2)
    for d in gyd:
        d.wait_recv()
    gz[0] = gy[0] + gy[1] + gy[2] + gy[3]
    gzd = wire.copy(gz.at[0], gz.at[1], {"zh": 1 - z})
    across(3)
    grad_scale = 1.0 / 64.0
    for i in range(4):
        last[i].wait_recv()
        pgb[i] = (gp[i, y, z].astype(F32) + zpart[i].astype(F32)) * grad_scale
        put(pgb.at[i], pgrad_out.at[:, pl.ds(256 * i, 256)])
    gzd.wait_recv()
    ggb[...] = (gz[0] + gz[1]) * grad_scale
    put(ggb, ggrad_out)
    wire.drain()
    for d in written:
        d.wait()


def hand_over(a, b, c, d, a_out, b_out, c_out, d_out):
    a_out[...] = a[...]
    b_out[...] = b[...]
    c_out[...] = c[...]
    d_out[...] = d[0]


def local(
    queries, keys, values, prefix_keys, prefix_values, doc_start, out_weight, residual,
    student_hidden, student_gain, proj_weight,
):
    vmem = pl.BlockSpec(memory_space=pltpu.VMEM)
    anyspace = pl.BlockSpec(memory_space=pl.ANY)
    smem = pl.BlockSpec(memory_space=pltpu.SMEM)
    v = pltpu.VMEM
    shapes = [
        jax.ShapeDtypeStruct((128, 1024), BF16),
        jax.ShapeDtypeStruct((128, 384), BF16),
        jax.ShapeDtypeStruct((96, 1024), F32),
    ]
    outs = pl.pallas_call(
        kernel,
        out_shape=(*shapes, jax.ShapeDtypeStruct((8, 384), F32)),
        in_specs=[anyspace] * 5 + [smem] + [anyspace] * 3 + [vmem] + [anyspace],
        out_specs=(anyspace,) * 4,
        scratch_shapes=[
            v((4, 4, 2, 2, 128, 128), BF16),
            v((4, 4, 2, 2, 128, 128), BF16),
            v((32, 96, 1024), BF16),
            v((512, 8192), BF16),
            v((128, 512), BF16),
            v((512, 128), BF16),
            v((8, 128, 384), BF16),
            v((128, 1024), BF16),
            v((512, 128), F32),
            v((512, 128), F32),
            v((512, 128), F32),
            v((128, 512), BF16),
            v((4, 128, 1024), BF16),
            v((4, 128, 1024), BF16),
            v((3, 128, 1024), BF16),
            v((3, 128, 1024), BF16),
            v((128, 1024), F32),
            v((128, 3072), BF16),
            v((8, 384, 128), BF16),
            v((768, 512), BF16),
            v((128, 1024), BF16),
            v((4, 4, 128, 256), BF16),
            v((4, 128, 384), BF16),
            v((4, 128, 384), BF16),
            v((3, 128, 384), BF16),
            v((3, 128, 384), BF16),
            v((8, 8, 128), F32),
            v((4, 8, 384), F32),
            v((4, 8, 384), F32),
            v((2, 8, 384), F32),
            v((4, 4, 2, 96, 256), BF16),
            v((4, 2, 96, 256), BF16),
            v((4, 2, 2, 96, 256), BF16),
            v((4, 96, 256), BF16),
            v((128, 1024), BF16),
            v((128, 384), BF16),
            v((4, 96, 256), F32),
            v((8, 384), F32),
            pltpu.SemaphoreType.DMA((SEMS,)),
            pltpu.SemaphoreType.DMA((SEMS,)),
            pltpu.SemaphoreType.DMA((16,)),
        ],
        compiler_params=pltpu.CompilerParams(
            collective_id=0, has_side_effects=True, vmem_limit_bytes=60 * 1024 * 1024
        ),
    )(
        queries, keys, values, prefix_keys, prefix_values, doc_start, out_weight, residual,
        student_hidden, student_gain.reshape(8, 1, 384), proj_weight,
    )
    return pl.pallas_call(
        hand_over,
        out_shape=(*shapes, jax.ShapeDtypeStruct((384,), F32)),
        in_specs=[vmem] * 4,
        out_specs=(vmem,) * 4,
    )(*outs)


def solution(mesh):
    finer = Mesh(mesh.devices.reshape(4, 4, 2, 4, 2), SEQ + TEN)
    rows = P(SEQ, TEN)
    return jax.shard_map(
        local,
        mesh=finer,
        in_specs=(
            rows, rows, rows, rows, rows, P(), P(TEN, None), P(SEQ + TEN, None), rows, P(), rows,
        ),
        out_specs=(rows, rows, rows, P(TEN)),
        check_vma=False,
    )
```

```python
import math

import jax
import jax.numpy as jnp
from jax import lax
from jax.experimental import pallas as pl
from jax.experimental.pallas import tpu as pltpu
from jax.sharding import Mesh
from jax.sharding import PartitionSpec as P

MESH = pl.DeviceIdType.MESH
F32 = jnp.float32
BF16 = jnp.bfloat16
NEG = -1e30
SEQ = ("x", "y", "zh")
TEN = ("zl", "c")
SENDS, RECVS = 126, 153


def mod4(v):
    return lax.rem(v, 4)


class Wire:
    def __init__(self, send, recv):
        self.send, self.recv = send, recv
        self.recv_used, self.send_used, self.spare, self.open = 0, 0, [], []

    def copy(self, src, dst, dev):
        if self.spare:
            i = self.spare.pop(0)
        else:
            i = self.send_used
            self.send_used += 1
        d = pltpu.make_async_remote_copy(
            src_ref=src,
            dst_ref=dst,
            send_sem=self.send.at[i],
            recv_sem=self.recv.at[self.recv_used],
            device_id=dev,
            device_id_type=MESH,
        )
        self.recv_used += 1
        d.start()
        self.open.append((i, d))
        return d

    def settle(self, count=None):
        count = len(self.open) if count is None else count
        for i, d in self.open[:count]:
            d.wait_send()
            self.spare.append(i)
        self.open = self.open[count:]


class Gather:
    def __init__(self, wire, at, first, second, coord):
        self.wire, self.at, self.first, self.second = wire, at, first, second
        self.a, self.b, self.z = coord[first], coord[second], coord["zh"]
        self.r, self.l, self.hr, self.hl = {}, {}, {}, {}
        a = self.a
        self.order = (a, mod4(a + 3), mod4(a + 1), mod4(a + 2))

    def z_send(self):
        own = self.at(self.a, self.b, self.z, 1, None)
        self.zd = self.wire.copy(own, own, {"zh": 1 - self.z})

    def z_wait(self):
        self.zd.wait_recv()

    def ring(self, key, ref_of, axis, pos):
        own = ref_of(pos, None)
        self.r[key] = self.wire.copy(own, own, {axis: mod4(pos + 1)})
        self.l[key] = self.wire.copy(own, own, {axis: mod4(pos + 3)})

    def forward(self, key, ref_of, axis, pos):
        self.r[key].wait_recv()
        left = ref_of(mod4(pos + 3), 0)
        self.hr[key] = self.wire.copy(left, left, {axis: mod4(pos + 1)})
        self.l[key].wait_recv()
        right = ref_of(mod4(pos + 1), 1)
        self.hl[key] = self.wire.copy(right, right, {axis: mod4(pos + 3)})

    def done(self, key):
        self.hr[key].wait_recv()
        self.hl[key].wait_recv()

    def one(self, j):
        zq = self.z if j == 0 else 1 - self.z
        return lambda pos, half: self.at(pos, self.b, zq, 1, half)

    def two(self, j, k):
        aq = self.order[k]
        if j is None:
            return lambda pos, half: self.at(aq, pos, 0, 2, half)
        zq = self.z if j == 0 else 1 - self.z
        return lambda pos, half: self.at(aq, pos, zq, 1, half)

    def p1_send(self, j):
        self.ring(("1", j), self.one(j), self.first, self.a)

    def p1_fwd(self, j):
        self.forward(("1", j), self.one(j), self.first, self.a)

    def p1_done(self, j):
        self.done(("1", j))

    def p2_send(self, j, k):
        self.ring(("2", j, k), self.two(j, k), self.second, self.b)

    def p2_fwd(self, j, k):
        self.forward(("2", j, k), self.two(j, k), self.second, self.b)

    def p2_done(self, j, k):
        self.done(("2", j, k))


class Scatter:
    def __init__(self, wire, part, near, far, axis, pos):
        self.wire, self.part, self.near, self.far = wire, part, near, far
        self.axis, self.pos = axis, pos

    def start(self):
        p, ax = self.pos, self.axis
        opp = mod4(p + 2)
        self.r1 = self.wire.copy(self.part(opp, 0), self.near.at[0], {ax: mod4(p + 1)})
        self.l1 = self.wire.copy(self.part(opp, 1), self.near.at[1], {ax: mod4(p + 3)})

    def middle(self):
        p, ax = self.pos, self.axis
        right, left = mod4(p + 1), mod4(p + 3)
        self.r1.wait_recv()
        ref = self.part(right, 0)
        ref[...] = (ref[...].astype(F32) + self.near[0].astype(F32)).astype(BF16)
        self.r2 = self.wire.copy(self.part(right, None), self.far.at[0], {ax: right})
        self.l1.wait_recv()
        ref = self.part(left, 1)
        ref[...] = (ref[...].astype(F32) + self.near[1].astype(F32)).astype(BF16)
        self.l2 = self.wire.copy(self.part(left, None), self.far.at[1], {ax: left})

    def finish(self):
        self.r2.wait_recv()
        self.l2.wait_recv()
        ref = self.part(self.pos, None)
        ref[...] = (
            ref[...].astype(F32) + self.far[0].astype(F32) + self.far[1].astype(F32)
        ).astype(BF16)


def kernel(
    q_hbm, k_hbm, v_hbm, pk_hbm, pv_hbm, doc, w_hbm, res_hbm, hid_hbm, gain, proj_hbm,
    teacher_out, sgrad_out, pgrad_out, ggrad_out,
    kvb, pj, w, q, qs, part_of, part_in, stat_of, stat_in, hid, res, mx, tot, acc, att,
    bsend, brecv, bz, zrecv, tacc, nrm, nrmt, nxt, mis, mch,
    fsend, frecv, fz, fzrecv, rowbuf, gx, gy, gz,
    gp, near, far, zpart, tcb, sgb, pgb, ggb,
    ssem, rsem, lsem,
):
    x, y, z = lax.axis_index("x"), lax.axis_index("y"), lax.axis_index("zh")
    zl, c = lax.axis_index("zl"), lax.axis_index("c")
    coord = {"x": x, "y": y, "zh": z}
    seq = (x * 4 + y) * 2 + z
    t = zl * 2 + c
    wire = Wire(ssem, rsem)
    mate = {"c": 1 - c}

    def tensor_peer(dz, dc):
        return {"zl": mod4(zl + dz), "c": c if dc == 0 else 1 - c}

    def tensor_index(dz, dc):
        return mod4(zl + dz) * 2 + (c if dc == 0 else 1 - c)

    peers = [(dz, dc) for dz in (2, 1, 3, 0) for dc in (0, 1) if (dz, dc) != (0, 0)]

    loads = [
        (pk_hbm, kvb.at[y, z, 0]),
        (pv_hbm, kvb.at[y, z, 1]),
        (k_hbm, kvb.at[y, z, 2]),
        (v_hbm, kvb.at[y, z, 3]),
        (proj_hbm, pj.at[seq]),
        (hid_hbm, hid.at[t]),
        (q_hbm, q),
        (
            res_hbm.at[:, pl.ds(pl.multiple_of(t * 1024, 1024), 1024)],
            res.at[pl.ds(pl.multiple_of(t * 16, 16), 16), :],
        ),
        (w_hbm, w),
    ]
    local = [pltpu.make_async_copy(s, d, lsem.at[i]) for i, (s, d) in enumerate(loads)]
    for d in local:
        d.start()

    written = []

    def put(src, dst):
        d = pltpu.make_async_copy(src, dst, lsem.at[len(loads) + len(written)])
        d.start()
        written.append(d)

    barrier = pltpu.get_barrier_semaphore()
    greet = [
        {"x": mod4(x + 1)}, {"x": mod4(x + 2)}, {"x": mod4(x + 3)},
        {"y": mod4(y + 1)}, {"y": mod4(y + 2)}, {"y": mod4(y + 3)},
        {"zh": 1 - z},
    ] + [tensor_peer(*p) for p in peers]
    for dev in greet:
        pl.semaphore_signal(barrier, inc=1, device_id=dev, device_id_type=MESH)
    pl.semaphore_wait(barrier, len(greet))

    def kv_at(a, b, zq, count, half):
        return kvb.at[a, zq] if half is None else kvb.at[a, zq, pl.ds(2 * half, 2)]

    def q_at(pos, half):
        return qs.at[pos] if half is None else qs.at[pos, pl.ds(256 * half, 256)]

    def pj_at(low, x_first):
        def at(a, b, zq, count, half):
            slot = ((a * 4 + b) if x_first else (b * 4 + a)) * 2 + zq
            where = slot if count == 1 else pl.ds(slot, 2)
            cols = pl.ds(0, 1024) if half is None else pl.ds(512 * half, 512)
            return pj.at[where, pl.ds(low, 48), cols]

        return at

    kv = Gather(wire, kv_at, "y", "x", coord)
    ring = Gather(wire, None, "x", "y", coord)
    pr = (
        Gather(wire, pj_at(0, True), "x", "y", coord),
        Gather(wire, pj_at(48, False), "y", "x", coord),
    )

    def both(streams, name, *args):
        for s in streams:
            getattr(s, name)(*args)

    factor = 128 ** (-0.5) * math.log2(math.e)
    column = lax.broadcasted_iota(jnp.int32, (512, 512), 1)
    position = x * 1024 + (column // 128) * 256 + lax.rem(column, 128)
    token = lax.rem(lax.broadcasted_iota(jnp.int32, (512, 512), 0), 128) + (y * 2 + z) * 128
    diagonal = lax.broadcasted_iota(jnp.int32, (128, 128), 0) == lax.broadcasted_iota(
        jnp.int32, (128, 128), 1
    )

    def wide(v):
        return jnp.concatenate([v] * 4, axis=1)

    def block(xq, kb, vb, visible):
        s = lax.dot_general(
            qs[xq], kb.reshape(512, 128), (((1,), (1,)), ((), ())), preferred_element_type=F32
        ) * factor
        s = jnp.where(visible, s, NEG)
        old = mx[xq]
        new = jnp.maximum(old, jnp.broadcast_to(jnp.max(s, axis=1, keepdims=True), (512, 128)))
        p = jnp.exp2(s - wide(new))
        scale = jnp.exp2(old - new)
        mx[xq] = new
        tot[xq] = tot[xq] * scale + jnp.broadcast_to(
            jnp.sum(p, axis=1, keepdims=True), (512, 128)
        )
        acc[xq] = acc[xq] * scale + jnp.dot(
            p.astype(BF16), vb.reshape(512, 128), preferred_element_type=F32
        )

    def attend(j, xq):
        zq = z if j == 0 else 1 - z
        here = position + zq * 128
        block(xq, kvb[:, zq, 0], kvb[:, zq, 1], here >= doc[0])
        block(xq, kvb[:, zq, 2], kvb[:, zq, 3], here <= token + xq * 1024)

    def to_row(v):
        return jnp.sum(jnp.where(diagonal, v, 0.0), axis=0, keepdims=True)

    def to_column(v):
        wide_row = jnp.broadcast_to(v, (128, 128))
        return jnp.sum(jnp.where(diagonal, wide_row, 0.0), axis=1, keepdims=True)

    back = {}

    def give_back(d):
        xq = mod4(x + d)
        part_of[d - 1] = (acc[xq] / tot[xq]).astype(BF16)
        stat_of[d - 1] = jnp.concatenate(
            [to_row(r[xq, h * 128 : (h + 1) * 128, :]) for r in (mx, tot) for h in range(4)],
            axis=0,
        )
        back[d] = (
            wire.copy(part_of.at[d - 1], part_in.at[d - 1], {"x": xq}),
            wire.copy(stat_of.at[d - 1], stat_in.at[d - 1], {"x": xq}),
        )

    local[6].wait()
    for h in range(4):
        qs[x, h * 128 : (h + 1) * 128, :] = q[:, h * 128 : (h + 1) * 128]
    for d in local[:4]:
        d.wait()
    kv.z_send()
    kv.p1_send(0)
    ring.ring("q", q_at, "x", x)
    local[4].wait()
    both(pr, "p1_send", 0)
    both(pr, "z_send")
    local[5].wait()
    hz = {dz: wire.copy(hid.at[t], hid.at[t], tensor_peer(dz, 0)) for dz in (2, 1, 3)}
    hmate = [wire.copy(hid.at[t], hid.at[t], mate)]
    for i in range(4):
        mx[i] = jnp.full((512, 128), NEG, F32)
        tot[i] = jnp.zeros((512, 128), F32)
        acc[i] = jnp.zeros((512, 128), F32)
    ring.forward("q", q_at, "x", x)
    kv.p1_fwd(0)
    both(pr, "p1_fwd", 0)
    kv.z_wait()
    kv.p1_send(1)
    ring.done("q")
    kv.p1_done(0)
    attend(0, mod4(x + 2))
    attend(0, mod4(x + 1))
    kv.p1_fwd(1)
    attend(0, mod4(x + 3))
    attend(0, x)
    kv.p1_done(1)
    early = len(wire.open)
    attend(1, mod4(x + 2))
    give_back(2)
    attend(1, mod4(x + 1))
    give_back(1)
    both(pr, "z_wait")
    both(pr, "p1_send", 1)
    both(pr, "p2_send", None, 0)
    attend(1, mod4(x + 3))
    give_back(3)
    attend(1, x)
    both(pr, "p1_fwd", 1)
    both(pr, "p2_send", None, 1)
    both(pr, "p2_send", None, 2)
    for dz in (2, 1, 3):
        hz[dz].wait_recv()
        slot = mod4(zl + 4 - dz) * 2 + c
        hmate.append(wire.copy(hid.at[slot], hid.at[slot], mate))
    rsend = []
    for p in peers:
        cols = pl.ds(pl.multiple_of(tensor_index(*p) * 1024, 1024), 1024)
        rsend.append(
            wire.copy(
                res_hbm.at[:, cols],
                res.at[pl.ds(pl.multiple_of(t * 16, 16), 16), :],
                tensor_peer(*p),
            )
        )
    for d in (2, 1, 3):
        for r in back[d]:
            r.wait_recv()
    both(pr, "p1_done", 0)
    both(pr, "p1_done", 1)
    both(pr, "p2_send", None, 3)
    for h in range(4):
        rows = slice(h * 128, (h + 1) * 128)
        maxes = [mx[x, rows, :]] + [to_column(stat_in[i, h : h + 1, :]) for i in range(3)]
        most = jnp.maximum(
            jnp.maximum(maxes[0], maxes[1]), jnp.maximum(maxes[2], maxes[3])
        )
        scale = jnp.exp2(maxes[0] - most)
        over, under = acc[x, rows, :] * scale, tot[x, rows, :] * scale
        for i in range(3):
            scale = jnp.exp2(maxes[1 + i] - most) * to_column(stat_in[i, 4 + h : 5 + h, :])
            over = over + scale * part_in[i, rows, :].astype(F32)
            under = under + scale
        att[:, h * 128 : (h + 1) * 128] = (over / under).astype(BF16)

    local[8].wait()
    turns = (2, 1, 3, 0)

    def projected(dz, dc):
        cols = pl.ds(pl.multiple_of(tensor_index(dz, dc) * 1024, 1024), 1024)
        return jnp.dot(att[...], w[:, cols], preferred_element_type=F32)

    half = {}
    for dz in turns:
        bsend[dz] = projected(dz, 1).astype(BF16)
        half[dz] = wire.copy(bsend.at[dz], brecv.at[dz], mate)
    zsum = {}
    for dz in turns:
        mine = projected(dz, 0)
        half[dz].wait_recv()
        mine = mine + brecv[dz].astype(F32)
        if dz:
            bz[dz - 1] = mine.astype(BF16)
            zsum[dz] = wire.copy(bz.at[dz - 1], zrecv.at[dz - 1], tensor_peer(dz, 0))
        else:
            tacc[...] = mine
    wire.settle(early)
    both(pr, "p2_fwd", None, 0)

    for d in hmate:
        d.wait_recv()
    square = jnp.zeros((128, 384), F32)
    for i in range(8):
        h = hid[i].astype(F32)
        square = square + h * h
    inverse = lax.rsqrt(jnp.sum(square, axis=1, keepdims=True) / 3072.0 + 1e-05)
    for i in range(8):
        n = (hid[i].astype(F32) * inverse * gain[i]).astype(BF16)
        nrm[:, i * 384 : (i + 1) * 384] = n
        nrmt[i] = n.T

    def nxt_at(xq, core):
        return nxt.at[
            pl.ds(pl.multiple_of(core * 384, 384), 384),
            pl.ds(pl.multiple_of(xq * 128, 128), 128),
        ]

    nx = {}
    for d in (2, 1, 3):
        nx[d] = wire.copy(nrmt.at[mod4(x + d) * 2 + c], nxt_at(x, c), {"x": mod4(x + d)})
    for i in range(2):
        nxt[i * 384 : (i + 1) * 384, pl.ds(pl.multiple_of(x * 128, 128), 128)] = nrmt[2 * x + i]
    both(pr, "p2_fwd", None, 1)
    both(pr, "p2_fwd", None, 2)
    nmate = []
    for d in (2, 1, 3):
        nx[d].wait_recv()
        came = nxt_at(mod4(x + 4 - d), c)
        nmate.append(wire.copy(came, came, mate))
    both(pr, "p2_fwd", None, 3)
    for d in rsend:
        d.wait_recv()
    local[7].wait()
    tacc[...] = tacc[...] + res[...].astype(F32)
    for k in range(4):
        both(pr, "p2_done", None, k)
    pre = jnp.zeros((128, 1024), F32)
    for i in range(4):
        pre = pre + jnp.dot(
            nrm[:, i * 768 : (i + 1) * 768],
            pj[pl.ds(8 * i, 8)].reshape(768, 1024),
            preferred_element_type=F32,
        )
    for dz in turns[:3]:
        zsum[dz].wait_recv()
    teacher = (
        tacc[...] + zrecv[0].astype(F32) + zrecv[1].astype(F32) + zrecv[2].astype(F32)
    ).astype(BF16)
    tcb[...] = teacher
    put(tcb, teacher_out)
    mismatch = (pre - teacher.astype(F32)).astype(BF16)
    mis[...] = mismatch
    for i in range(4):
        mch[i, x] = mismatch[:, i * 256 : (i + 1) * 256]

    def mch_at(i):
        return lambda p, h: mch.at[i, p] if h is None else mch.at[i, p, pl.ds(64 * h, 64)]

    sums = []
    for i in range(4):
        ring.ring(i, mch_at(i), "x", x)
        sums.append(
            Scatter(
                wire,
                lambda p, h, i=i: gp.at[i, p] if h is None else gp.at[i, p, h],
                near.at[i],
                far.at[i],
                "y",
                y,
            )
        )

    def product(i):
        ring.done(i)
        g = jnp.dot(nxt[...], mch[i].reshape(512, 256), preferred_element_type=F32)
        gp[i] = g.astype(BF16).reshape(4, 2, 96, 256)
        sums[i].start()

    last = {}

    def across(i):
        sums[i].finish()
        last[i] = wire.copy(gp.at[i, y, 1 - z], zpart.at[i], {"zh": 1 - z})

    def state_grad(dz, dc):
        rows = pj[pl.ds(4 * tensor_index(dz, dc), 4)].reshape(384, 1024)
        return lax.dot_general(
            mis[...], rows, (((1,), (1,)), ((), ())), preferred_element_type=F32
        )

    def to_mate(dz):
        fsend[dz] = state_grad(dz, 1).astype(BF16)
        half[dz] = wire.copy(fsend.at[dz], frecv.at[dz], mate)

    def along_z(dz):
        mine = state_grad(dz, 0)
        half[dz].wait_recv()
        mine = mine + frecv[dz].astype(F32)
        if dz == 0:
            return mine
        fz[dz - 1] = mine.astype(BF16)
        zsum[dz] = wire.copy(fz.at[dz - 1], fzrecv.at[dz - 1], tensor_peer(dz, 0))
        return None

    for dz in turns:
        to_mate(dz)
    along_z(2)
    along_z(1)
    ring.forward(0, mch_at(0), "x", x)
    along_z(3)
    ring.forward(1, mch_at(1), "x", x)
    grad = along_z(0)
    for d in nmate:
        d.wait_recv()
    ring.forward(2, mch_at(2), "x", x)
    product(0)
    ring.forward(3, mch_at(3), "x", x)
    product(1)
    sums[0].middle()
    product(2)
    sums[1].middle()
    product(3)
    for dz in turns[:3]:
        zsum[dz].wait_recv()
    grad = grad + fzrecv[0].astype(F32) + fzrecv[1].astype(F32) + fzrecv[2].astype(F32)
    hidden = hid[t].astype(F32)
    own_gain = gain[t]
    inner = jnp.sum(grad * own_gain * hidden, axis=1, keepdims=True)
    rowbuf[0] = jnp.broadcast_to(to_row(inner), (8, 128))
    rows = [wire.copy(rowbuf.at[0], rowbuf.at[1 + i], tensor_peer(*p)) for i, p in enumerate(peers)]
    part = jnp.sum(grad * hidden * inverse, axis=0, keepdims=True)
    gx[0] = jnp.broadcast_to(part, (8, 384))
    gxd = [wire.copy(gx.at[0], gx.at[d], {"x": mod4(x + d)}) for d in (1, 2, 3)]
    sums[2].middle()
    across(0)
    for d in gxd:
        d.wait_recv()
    gy[0] = gx[0] + gx[1] + gx[2] + gx[3]
    gyd = [wire.copy(gy.at[0], gy.at[d], {"y": mod4(y + d)}) for d in (1, 2, 3)]
    sums[3].middle()
    across(1)
    for d in rows:
        d.wait_recv()
    total = rowbuf[0]
    for i in range(7):
        total = total + rowbuf[1 + i]
    row_inner = to_column(total[0:1, :]) / 3072.0
    sgb[...] = (
        inverse * own_gain * grad - hidden * inverse * inverse * inverse * row_inner
    ).astype(BF16)
    put(sgb, sgrad_out)
    across(2)
    for d in gyd:
        d.wait_recv()
    gz[0] = gy[0] + gy[1] + gy[2] + gy[3]
    gzd = wire.copy(gz.at[0], gz.at[1], {"zh": 1 - z})
    across(3)
    grad_scale = 1.0 / 64.0
    for i in range(4):
        last[i].wait_recv()
        pgb[i] = (gp[i, y, z].astype(F32) + zpart[i].astype(F32)) * grad_scale
        put(pgb.at[i], pgrad_out.at[:, pl.ds(256 * i, 256)])
    gzd.wait_recv()
    ggb[...] = (gz[0] + gz[1]) * grad_scale
    put(ggb, ggrad_out)
    wire.settle()
    assert (wire.send_used, wire.recv_used) == (SENDS, RECVS), (wire.send_used, wire.recv_used)
    for d in written:
        d.wait()


def hand_over(a, b, c, d, a_out, b_out, c_out, d_out):
    a_out[...] = a[...]
    b_out[...] = b[...]
    c_out[...] = c[...]
    d_out[...] = d[0]


def local(
    queries, keys, values, prefix_keys, prefix_values, doc_start, out_weight, residual,
    student_hidden, student_gain, proj_weight,
):
    vmem = pl.BlockSpec(memory_space=pltpu.VMEM)
    anyspace = pl.BlockSpec(memory_space=pl.ANY)
    smem = pl.BlockSpec(memory_space=pltpu.SMEM)
    v = pltpu.VMEM
    shapes = [
        jax.ShapeDtypeStruct((128, 1024), BF16),
        jax.ShapeDtypeStruct((128, 384), BF16),
        jax.ShapeDtypeStruct((96, 1024), F32),
    ]
    outs = pl.pallas_call(
        kernel,
        out_shape=(*shapes, jax.ShapeDtypeStruct((8, 384), F32)),
        in_specs=[anyspace] * 5 + [smem] + [anyspace] * 3 + [vmem] + [anyspace],
        out_specs=(anyspace,) * 4,
        scratch_shapes=[
            v((4, 2, 4, 128, 128), BF16),
            v((32, 96, 1024), BF16),
            v((512, 8192), BF16),
            v((128, 512), BF16),
            v((4, 512, 128), BF16),
            v((3, 512, 128), BF16),
            v((3, 512, 128), BF16),
            v((3, 8, 128), F32),
            v((3, 8, 128), F32),
            v((8, 128, 384), BF16),
            v((128, 1024), BF16),
            v((4, 512, 128), F32),
            v((4, 512, 128), F32),
            v((4, 512, 128), F32),
            v((128, 512), BF16),
            v((4, 128, 1024), BF16),
            v((4, 128, 1024), BF16),
            v((3, 128, 1024), BF16),
            v((3, 128, 1024), BF16),
            v((128, 1024), F32),
            v((128, 3072), BF16),
            v((8, 384, 128), BF16),
            v((768, 512), BF16),
            v((128, 1024), BF16),
            v((4, 4, 128, 256), BF16),
            v((4, 128, 384), BF16),
            v((4, 128, 384), BF16),
            v((3, 128, 384), BF16),
            v((3, 128, 384), BF16),
            v((8, 8, 128), F32),
            v((4, 8, 384), F32),
            v((4, 8, 384), F32),
            v((2, 8, 384), F32),
            v((4, 4, 2, 96, 256), BF16),
            v((4, 2, 96, 256), BF16),
            v((4, 2, 2, 96, 256), BF16),
            v((4, 96, 256), BF16),
            v((128, 1024), BF16),
            v((128, 384), BF16),
            v((4, 96, 256), F32),
            v((8, 384), F32),
            pltpu.SemaphoreType.DMA((SENDS,)),
            pltpu.SemaphoreType.DMA((RECVS,)),
            pltpu.SemaphoreType.DMA((16,)),
        ],
        compiler_params=pltpu.CompilerParams(
            collective_id=0, has_side_effects=True, vmem_limit_bytes=60 * 1024 * 1024
        ),
    )(
        queries, keys, values, prefix_keys, prefix_values, doc_start, out_weight, residual,
        student_hidden, student_gain.reshape(8, 1, 384), proj_weight,
    )
    return pl.pallas_call(
        hand_over,
        out_shape=(*shapes, jax.ShapeDtypeStruct((384,), F32)),
        in_specs=[vmem] * 4,
        out_specs=(vmem,) * 4,
    )(*outs)


def solution(mesh):
    finer = Mesh(mesh.devices.reshape(4, 4, 2, 4, 2), SEQ + TEN)
    rows = P(SEQ, TEN)
    return jax.shard_map(
        local,
        mesh=finer,
        in_specs=(
            rows, rows, rows, rows, rows, P(), P(TEN, None), P(SEQ + TEN, None), rows, P(), rows,
        ),
        out_specs=(rows, rows, rows, P(TEN)),
        check_vma=False,
    )
```

```python
import math

import jax
import jax.numpy as jnp
from jax import lax
from jax.experimental import pallas as pl
from jax.experimental.pallas import tpu as pltpu
from jax.sharding import Mesh
from jax.sharding import PartitionSpec as P

MESH = pl.DeviceIdType.MESH
F32 = jnp.float32
BF16 = jnp.bfloat16
NEG = -1e30
SEQ = ("x", "y", "zh")
TEN = ("zl", "c")
SENDS, RECVS = 141, 191


def mod4(v):
    return lax.rem(v, 4)


class Wire:
    def __init__(self, send, recv):
        self.send, self.recv = send, recv
        self.recv_used, self.send_used, self.spare, self.open = 0, 0, [], []

    def copy(self, src, dst, dev):
        if self.spare:
            i = self.spare.pop(0)
        else:
            i = self.send_used
            self.send_used += 1
        d = pltpu.make_async_remote_copy(
            src_ref=src,
            dst_ref=dst,
            send_sem=self.send.at[i],
            recv_sem=self.recv.at[self.recv_used],
            device_id=dev,
            device_id_type=MESH,
        )
        self.recv_used += 1
        d.start()
        self.open.append((i, d))
        return d

    def settle(self, count=None):
        count = len(self.open) if count is None else count
        for i, d in self.open[:count]:
            d.wait_send()
            self.spare.append(i)
        self.open = self.open[count:]


class Gather:
    def __init__(self, wire, at, first, second, coord):
        self.wire, self.at, self.first, self.second = wire, at, first, second
        self.a, self.b, self.z = coord[first], coord[second], coord["zh"]
        self.r, self.l, self.hr, self.hl = {}, {}, {}, {}
        a = self.a
        self.order = (a, mod4(a + 3), mod4(a + 1), mod4(a + 2))

    def z_send(self):
        own = self.at(self.a, self.b, self.z, 1, None)
        self.zd = self.wire.copy(own, own, {"zh": 1 - self.z})

    def z_wait(self):
        self.zd.wait_recv()

    def ring(self, key, ref_of, axis, pos):
        own = ref_of(pos, None)
        self.r[key] = self.wire.copy(own, own, {axis: mod4(pos + 1)})
        self.l[key] = self.wire.copy(own, own, {axis: mod4(pos + 3)})

    def forward(self, key, ref_of, axis, pos):
        self.r[key].wait_recv()
        left = ref_of(mod4(pos + 3), 0)
        self.hr[key] = self.wire.copy(left, left, {axis: mod4(pos + 1)})
        self.l[key].wait_recv()
        right = ref_of(mod4(pos + 1), 1)
        self.hl[key] = self.wire.copy(right, right, {axis: mod4(pos + 3)})

    def done(self, key):
        self.hr[key].wait_recv()
        self.hl[key].wait_recv()

    def one(self, j):
        zq = self.z if j == 0 else 1 - self.z
        return lambda pos, half: self.at(pos, self.b, zq, 1, half)

    def two(self, j, k):
        aq = self.order[k]
        if j is None:
            return lambda pos, half: self.at(aq, pos, 0, 2, half)
        zq = self.z if j == 0 else 1 - self.z
        return lambda pos, half: self.at(aq, pos, zq, 1, half)

    def p1_send(self, j):
        self.ring(("1", j), self.one(j), self.first, self.a)

    def p1_fwd(self, j):
        self.forward(("1", j), self.one(j), self.first, self.a)

    def p1_done(self, j):
        self.done(("1", j))

    def p2_send(self, j, k):
        self.ring(("2", j, k), self.two(j, k), self.second, self.b)

    def p2_fwd(self, j, k):
        self.forward(("2", j, k), self.two(j, k), self.second, self.b)

    def p2_done(self, j, k):
        self.done(("2", j, k))


class Scatter:
    def __init__(self, wire, part, near, far, axis, pos):
        self.wire, self.part, self.near, self.far = wire, part, near, far
        self.axis, self.pos = axis, pos

    def start(self):
        p, ax = self.pos, self.axis
        opp = mod4(p + 2)
        self.r1 = self.wire.copy(self.part(opp, 0), self.near.at[0], {ax: mod4(p + 1)})
        self.l1 = self.wire.copy(self.part(opp, 1), self.near.at[1], {ax: mod4(p + 3)})

    def middle(self):
        p, ax = self.pos, self.axis
        right, left = mod4(p + 1), mod4(p + 3)
        self.r1.wait_recv()
        ref = self.part(right, 0)
        ref[...] = (ref[...].astype(F32) + self.near[0].astype(F32)).astype(BF16)
        self.r2 = self.wire.copy(self.part(right, None), self.far.at[0], {ax: right})
        self.l1.wait_recv()
        ref = self.part(left, 1)
        ref[...] = (ref[...].astype(F32) + self.near[1].astype(F32)).astype(BF16)
        self.l2 = self.wire.copy(self.part(left, None), self.far.at[1], {ax: left})

    def finish(self):
        self.r2.wait_recv()
        self.l2.wait_recv()
        ref = self.part(self.pos, None)
        ref[...] = (
            ref[...].astype(F32) + self.far[0].astype(F32) + self.far[1].astype(F32)
        ).astype(BF16)


def kernel(
    q_hbm, k_hbm, v_hbm, pk_hbm, pv_hbm, doc, w_hbm, res_hbm, hid_hbm, gain, proj_hbm,
    teacher_out, sgrad_out, pgrad_out, ggrad_out,
    kvb, pj, w, q, qs, part_of, part_in, stat_of, stat_in, hid, res, mx, tot, acc, att,
    bsend, brecv, bz, zrecv, tacc, nrm, nrmt, nxtx, nxty, mis, mch,
    fsend, frecv, fz, fzrecv, rowbuf, gx, gy, gz,
    gp, near, far, zpart, tcb, sgb, pgb, ggb,
    ssem, rsem, lsem,
):
    x, y, z = lax.axis_index("x"), lax.axis_index("y"), lax.axis_index("zh")
    zl, c = lax.axis_index("zl"), lax.axis_index("c")
    coord = {"x": x, "y": y, "zh": z}
    seq = (x * 4 + y) * 2 + z
    t = zl * 2 + c
    wire = Wire(ssem, rsem)
    mate = {"c": 1 - c}

    def tensor_peer(dz, dc):
        return {"zl": mod4(zl + dz), "c": c if dc == 0 else 1 - c}

    def tensor_index(dz, dc):
        return mod4(zl + dz) * 2 + (c if dc == 0 else 1 - c)

    peers = [(dz, dc) for dz in (2, 1, 3, 0) for dc in (0, 1) if (dz, dc) != (0, 0)]

    loads = [
        (pk_hbm, kvb.at[y, z, 0]),
        (pv_hbm, kvb.at[y, z, 1]),
        (k_hbm, kvb.at[y, z, 2]),
        (v_hbm, kvb.at[y, z, 3]),
        (proj_hbm, pj.at[seq]),
        (hid_hbm, hid.at[t]),
        (q_hbm, q),
        (
            res_hbm.at[:, pl.ds(pl.multiple_of(t * 1024, 1024), 1024)],
            res.at[pl.ds(pl.multiple_of(t * 16, 16), 16), :],
        ),
        (w_hbm, w),
    ]
    local = [pltpu.make_async_copy(s, d, lsem.at[i]) for i, (s, d) in enumerate(loads)]
    for d in local:
        d.start()

    written = []

    def put(src, dst):
        d = pltpu.make_async_copy(src, dst, lsem.at[len(loads) + len(written)])
        d.start()
        written.append(d)

    barrier = pltpu.get_barrier_semaphore()
    greet = [
        {"x": mod4(x + 1)}, {"x": mod4(x + 2)}, {"x": mod4(x + 3)},
        {"y": mod4(y + 1)}, {"y": mod4(y + 2)}, {"y": mod4(y + 3)},
        {"zh": 1 - z},
    ] + [tensor_peer(*p) for p in peers]
    for dev in greet:
        pl.semaphore_signal(barrier, inc=1, device_id=dev, device_id_type=MESH)
    pl.semaphore_wait(barrier, len(greet))

    def kv_at(a, b, zq, count, half):
        return kvb.at[a, zq] if half is None else kvb.at[a, zq, pl.ds(2 * half, 2)]

    def q_at(pos, half):
        return qs.at[pos] if half is None else qs.at[pos, pl.ds(256 * half, 256)]

    def pj_at(low, x_first):
        def at(a, b, zq, count, half):
            slot = ((a * 4 + b) if x_first else (b * 4 + a)) * 2 + zq
            where = slot if count == 1 else pl.ds(slot, 2)
            cols = pl.ds(0, 1024) if half is None else pl.ds(512 * half, 512)
            return pj.at[where, pl.ds(low, 48), cols]

        return at

    kv = Gather(wire, kv_at, "y", "x", coord)
    ring = Gather(wire, None, "x", "y", coord)
    pr = (
        Gather(wire, pj_at(0, True), "x", "y", coord),
        Gather(wire, pj_at(48, False), "y", "x", coord),
    )

    def both(streams, name, *args):
        for s in streams:
            getattr(s, name)(*args)

    factor = 128 ** (-0.5) * math.log2(math.e)
    column = lax.broadcasted_iota(jnp.int32, (512, 512), 1)
    position = x * 1024 + (column // 128) * 256 + lax.rem(column, 128)
    token = lax.rem(lax.broadcasted_iota(jnp.int32, (512, 512), 0), 128) + (y * 2 + z) * 128
    diagonal = lax.broadcasted_iota(jnp.int32, (128, 128), 0) == lax.broadcasted_iota(
        jnp.int32, (128, 128), 1
    )

    def wide(v):
        return jnp.concatenate([v] * 4, axis=1)

    def block(xq, kb, vb, visible):
        s = lax.dot_general(
            qs[xq], kb.reshape(512, 128), (((1,), (1,)), ((), ())), preferred_element_type=F32
        ) * factor
        s = jnp.where(visible, s, NEG)
        old = mx[xq]
        new = jnp.maximum(old, jnp.broadcast_to(jnp.max(s, axis=1, keepdims=True), (512, 128)))
        p = jnp.exp2(s - wide(new))
        scale = jnp.exp2(old - new)
        mx[xq] = new
        tot[xq] = tot[xq] * scale + jnp.broadcast_to(
            jnp.sum(p, axis=1, keepdims=True), (512, 128)
        )
        acc[xq] = acc[xq] * scale + jnp.dot(
            p.astype(BF16), vb.reshape(512, 128), preferred_element_type=F32
        )

    def attend(j, xq):
        zq = z if j == 0 else 1 - z
        here = position + zq * 128
        block(xq, kvb[:, zq, 0], kvb[:, zq, 1], here >= doc[0])
        block(xq, kvb[:, zq, 2], kvb[:, zq, 3], here <= token + xq * 1024)

    def to_row(v):
        return jnp.sum(jnp.where(diagonal, v, 0.0), axis=0, keepdims=True)

    def to_column(v):
        wide_row = jnp.broadcast_to(v, (128, 128))
        return jnp.sum(jnp.where(diagonal, wide_row, 0.0), axis=1, keepdims=True)

    back = {}

    def give_back(d):
        xq = mod4(x + d)
        part_of[d - 1] = (acc[xq] / tot[xq]).astype(BF16)
        stat_of[d - 1] = jnp.concatenate(
            [to_row(r[xq, h * 128 : (h + 1) * 128, :]) for r in (mx, tot) for h in range(4)],
            axis=0,
        )
        back[d] = (
            wire.copy(part_of.at[d - 1], part_in.at[d - 1], {"x": xq}),
            wire.copy(stat_of.at[d - 1], stat_in.at[d - 1], {"x": xq}),
        )

    local[6].wait()
    for h in range(4):
        qs[x, h * 128 : (h + 1) * 128, :] = q[:, h * 128 : (h + 1) * 128]
    for d in local[:4]:
        d.wait()
    kv.z_send()
    kv.p1_send(0)
    ring.ring("q", q_at, "x", x)
    local[4].wait()
    both(pr, "p1_send", 0)
    both(pr, "z_send")
    local[5].wait()
    hz = {dz: wire.copy(hid.at[t], hid.at[t], tensor_peer(dz, 0)) for dz in (2, 1, 3)}
    hmate = [wire.copy(hid.at[t], hid.at[t], mate)]
    for i in range(4):
        mx[i] = jnp.full((512, 128), NEG, F32)
        tot[i] = jnp.zeros((512, 128), F32)
        acc[i] = jnp.zeros((512, 128), F32)
    ring.forward("q", q_at, "x", x)
    kv.p1_fwd(0)
    both(pr, "p2_send", 0, 0)
    both(pr, "p1_fwd", 0)
    kv.z_wait()
    kv.p1_send(1)
    both(pr, "p2_send", 0, 1)
    both(pr, "p2_send", 0, 2)
    ring.done("q")
    kv.p1_done(0)
    attend(0, mod4(x + 2))
    attend(0, mod4(x + 1))
    kv.p1_fwd(1)
    both(pr, "p1_done", 0)
    both(pr, "p2_send", 0, 3)
    attend(0, mod4(x + 3))
    attend(0, x)
    rsend = []
    for p in peers:
        cols = pl.ds(pl.multiple_of(tensor_index(*p) * 1024, 1024), 1024)
        rsend.append(
            wire.copy(
                res_hbm.at[:, cols],
                res.at[pl.ds(pl.multiple_of(t * 16, 16), 16), :],
                tensor_peer(*p),
            )
        )
    kv.p1_done(1)
    early = len(wire.open)
    attend(1, mod4(x + 2))
    give_back(2)
    both(pr, "p2_fwd", 0, 0)
    attend(1, mod4(x + 1))
    give_back(1)
    attend(1, mod4(x + 3))
    give_back(3)
    attend(1, x)
    both(pr, "p2_fwd", 0, 1)
    both(pr, "z_wait")
    both(pr, "p1_send", 1)
    both(pr, "p2_send", 1, 0)
    for dz in (2, 1, 3):
        hz[dz].wait_recv()
        slot = mod4(zl + 4 - dz) * 2 + c
        hmate.append(wire.copy(hid.at[slot], hid.at[slot], mate))
    for d in (2, 1, 3):
        for r in back[d]:
            r.wait_recv()
    for h in range(4):
        rows = slice(h * 128, (h + 1) * 128)
        maxes = [mx[x, rows, :]] + [to_column(stat_in[i, h : h + 1, :]) for i in range(3)]
        most = jnp.maximum(
            jnp.maximum(maxes[0], maxes[1]), jnp.maximum(maxes[2], maxes[3])
        )
        scale = jnp.exp2(maxes[0] - most)
        over, under = acc[x, rows, :] * scale, tot[x, rows, :] * scale
        for i in range(3):
            scale = jnp.exp2(maxes[1 + i] - most) * to_column(stat_in[i, 4 + h : 5 + h, :])
            over = over + scale * part_in[i, rows, :].astype(F32)
            under = under + scale
        att[:, h * 128 : (h + 1) * 128] = (over / under).astype(BF16)

    local[8].wait()
    turns = (2, 1, 3, 0)

    def projected(dz, dc):
        cols = pl.ds(pl.multiple_of(tensor_index(dz, dc) * 1024, 1024), 1024)
        return jnp.dot(att[...], w[:, cols], preferred_element_type=F32)

    half = {}
    for dz in turns:
        bsend[dz] = projected(dz, 1).astype(BF16)
        half[dz] = wire.copy(bsend.at[dz], brecv.at[dz], mate)
    zsum = {}
    for dz in turns:
        mine = projected(dz, 0)
        half[dz].wait_recv()
        mine = mine + brecv[dz].astype(F32)
        if dz:
            bz[dz - 1] = mine.astype(BF16)
            zsum[dz] = wire.copy(bz.at[dz - 1], zrecv.at[dz - 1], tensor_peer(dz, 0))
        else:
            tacc[...] = mine
    wire.settle(early)
    both(pr, "p2_fwd", 0, 2)
    both(pr, "p1_fwd", 1)
    both(pr, "p2_send", 1, 1)
    both(pr, "p2_send", 1, 2)
    both(pr, "p2_fwd", 0, 3)
    both(pr, "p1_done", 1)
    both(pr, "p2_send", 1, 3)

    for d in hmate:
        d.wait_recv()
    square = jnp.zeros((128, 384), F32)
    for i in range(8):
        h = hid[i].astype(F32)
        square = square + h * h
    inverse = lax.rsqrt(jnp.sum(square, axis=1, keepdims=True) / 3072.0 + 1e-05)
    for i in range(8):
        n = (hid[i].astype(F32) * inverse * gain[i]).astype(BF16)
        nrm[:, i * 384 : (i + 1) * 384] = n
        nrmt[i // 2, 2 * (i % 2) : 2 * (i % 2) + 2] = n.T.reshape(2, 192, 128)

    halfrows = pl.ds(2 * c, 2)

    def token_cols(pos):
        return pl.ds(pl.multiple_of(pos * 128, 128), 128)

    nx, nmate = {}, []
    for d in (2, 1, 3):
        nx["x", d] = wire.copy(
            nrmt.at[mod4(x + d), halfrows], nxtx.at[halfrows, :, token_cols(x)], {"x": mod4(x + d)}
        )
        nx["y", d] = wire.copy(
            nrmt.at[halfrows, mod4(y + d)], nxty.at[halfrows, :, token_cols(y)], {"y": mod4(y + d)}
        )
    nxtx[:, :, token_cols(x)] = nrmt[x]
    nxty[:, :, token_cols(y)] = nrmt[:, y]
    both(pr, "p2_fwd", 1, 0)
    both(pr, "p2_fwd", 1, 1)
    both(pr, "p2_fwd", 1, 2)
    both(pr, "p2_fwd", 1, 3)
    for d in (2, 1, 3):
        for axis, pos, buf in (("x", x, nxtx), ("y", y, nxty)):
            nx[axis, d].wait_recv()
            came = buf.at[halfrows, :, token_cols(mod4(pos + 4 - d))]
            nmate.append(wire.copy(came, came, mate))
    for d in rsend:
        d.wait_recv()
    local[7].wait()
    tacc[...] = tacc[...] + res[...].astype(F32)
    for j in range(2):
        for k in range(4):
            both(pr, "p2_done", j, k)
    pre = jnp.zeros((128, 1024), F32)
    for i in range(4):
        pre = pre + jnp.dot(
            nrm[:, i * 768 : (i + 1) * 768],
            pj[pl.ds(8 * i, 8)].reshape(768, 1024),
            preferred_element_type=F32,
        )
    for dz in turns[:3]:
        zsum[dz].wait_recv()
    teacher = (
        tacc[...] + zrecv[0].astype(F32) + zrecv[1].astype(F32) + zrecv[2].astype(F32)
    ).astype(BF16)
    tcb[...] = teacher
    put(tcb, teacher_out)
    mismatch = (pre - teacher.astype(F32)).astype(BF16)
    mis[...] = mismatch
    lanes = [("x", x, nxtx, "y", y), ("y", y, nxty, "x", x)] * 2
    for i, lane in enumerate(lanes):
        mch[i, lane[1]] = mismatch[:, i * 256 : (i + 1) * 256]

    def mch_at(i):
        return lambda p, h: mch.at[i, p] if h is None else mch.at[i, p, pl.ds(64 * h, 64)]

    sums = []
    for i, (axis, pos, _, other, there) in enumerate(lanes):
        ring.ring(i, mch_at(i), axis, pos)
        sums.append(
            Scatter(
                wire,
                lambda p, h, i=i: gp.at[i, p] if h is None else gp.at[i, p, h],
                near.at[i],
                far.at[i],
                other,
                there,
            )
        )

    def pass_on(i):
        ring.forward(i, mch_at(i), lanes[i][0], lanes[i][1])

    def product(i):
        ring.done(i)
        g = jnp.dot(
            lanes[i][2][...].reshape(768, 512),
            mch[i].reshape(512, 256),
            preferred_element_type=F32,
        )
        gp[i] = g.astype(BF16).reshape(4, 2, 96, 256)
        sums[i].start()

    last = {}

    def across(i):
        sums[i].finish()
        last[i] = wire.copy(gp.at[i, lanes[i][4], 1 - z], zpart.at[i], {"zh": 1 - z})

    def state_grad(dz, dc):
        rows = pj[pl.ds(4 * tensor_index(dz, dc), 4)].reshape(384, 1024)
        return lax.dot_general(
            mis[...], rows, (((1,), (1,)), ((), ())), preferred_element_type=F32
        )

    def to_mate(dz):
        fsend[dz] = state_grad(dz, 1).astype(BF16)
        half[dz] = wire.copy(fsend.at[dz], frecv.at[dz], mate)

    def along_z(dz):
        mine = state_grad(dz, 0)
        half[dz].wait_recv()
        mine = mine + frecv[dz].astype(F32)
        if dz == 0:
            return mine
        fz[dz - 1] = mine.astype(BF16)
        zsum[dz] = wire.copy(fz.at[dz - 1], fzrecv.at[dz - 1], tensor_peer(dz, 0))
        return None

    for dz in turns:
        to_mate(dz)
    along_z(2)
    along_z(1)
    pass_on(0)
    pass_on(1)
    along_z(3)
    pass_on(2)
    pass_on(3)
    grad = along_z(0)
    for d in nmate:
        d.wait_recv()
    for i in range(4):
        product(i)
    sums[0].middle()
    sums[1].middle()
    for dz in turns[:3]:
        zsum[dz].wait_recv()
    grad = grad + fzrecv[0].astype(F32) + fzrecv[1].astype(F32) + fzrecv[2].astype(F32)
    hidden = hid[t].astype(F32)
    own_gain = gain[t]
    inner = jnp.sum(grad * own_gain * hidden, axis=1, keepdims=True)
    rowbuf[0] = jnp.broadcast_to(to_row(inner), (8, 128))
    rows = [wire.copy(rowbuf.at[0], rowbuf.at[1 + i], tensor_peer(*p)) for i, p in enumerate(peers)]
    part = jnp.sum(grad * hidden * inverse, axis=0, keepdims=True)
    gx[0] = jnp.broadcast_to(part, (8, 384))
    gxd = [wire.copy(gx.at[0], gx.at[d], {"x": mod4(x + d)}) for d in (1, 2, 3)]
    sums[2].middle()
    sums[3].middle()
    across(0)
    for d in gxd:
        d.wait_recv()
    gy[0] = gx[0] + gx[1] + gx[2] + gx[3]
    gyd = [wire.copy(gy.at[0], gy.at[d], {"y": mod4(y + d)}) for d in (1, 2, 3)]
    across(1)
    across(2)
    for d in rows:
        d.wait_recv()
    total = rowbuf[0]
    for i in range(7):
        total = total + rowbuf[1 + i]
    row_inner = to_column(total[0:1, :]) / 3072.0
    sgb[...] = (
        inverse * own_gain * grad - hidden * inverse * inverse * inverse * row_inner
    ).astype(BF16)
    put(sgb, sgrad_out)
    across(3)
    for d in gyd:
        d.wait_recv()
    gz[0] = gy[0] + gy[1] + gy[2] + gy[3]
    gzd = wire.copy(gz.at[0], gz.at[1], {"zh": 1 - z})
    grad_scale = 1.0 / 64.0
    for i in range(4):
        last[i].wait_recv()
        pgb[i] = (gp[i, lanes[i][4], z].astype(F32) + zpart[i].astype(F32)) * grad_scale
        put(pgb.at[i], pgrad_out.at[:, pl.ds(256 * i, 256)])
    gzd.wait_recv()
    ggb[...] = (gz[0] + gz[1]) * grad_scale
    put(ggb, ggrad_out)
    wire.settle()
    assert (wire.send_used, wire.recv_used) == (SENDS, RECVS), (wire.send_used, wire.recv_used)
    for d in written:
        d.wait()


def hand_over(a, b, c, d, a_out, b_out, c_out, d_out):
    a_out[...] = a[...]
    b_out[...] = b[...]
    c_out[...] = c[...]
    d_out[...] = d[0]


def local(
    queries, keys, values, prefix_keys, prefix_values, doc_start, out_weight, residual,
    student_hidden, student_gain, proj_weight,
):
    vmem = pl.BlockSpec(memory_space=pltpu.VMEM)
    anyspace = pl.BlockSpec(memory_space=pl.ANY)
    smem = pl.BlockSpec(memory_space=pltpu.SMEM)
    v = pltpu.VMEM
    shapes = [
        jax.ShapeDtypeStruct((128, 1024), BF16),
        jax.ShapeDtypeStruct((128, 384), BF16),
        jax.ShapeDtypeStruct((96, 1024), F32),
    ]
    outs = pl.pallas_call(
        kernel,
        out_shape=(*shapes, jax.ShapeDtypeStruct((8, 384), F32)),
        in_specs=[anyspace] * 5 + [smem] + [anyspace] * 3 + [vmem] + [anyspace],
        out_specs=(anyspace,) * 4,
        scratch_shapes=[
            v((4, 2, 4, 128, 128), BF16),
            v((32, 96, 1024), BF16),
            v((512, 8192), BF16),
            v((128, 512), BF16),
            v((4, 512, 128), BF16),
            v((3, 512, 128), BF16),
            v((3, 512, 128), BF16),
            v((3, 8, 128), F32),
            v((3, 8, 128), F32),
            v((8, 128, 384), BF16),
            v((128, 1024), BF16),
            v((4, 512, 128), F32),
            v((4, 512, 128), F32),
            v((4, 512, 128), F32),
            v((128, 512), BF16),
            v((4, 128, 1024), BF16),
            v((4, 128, 1024), BF16),
            v((3, 128, 1024), BF16),
            v((3, 128, 1024), BF16),
            v((128, 1024), F32),
            v((128, 3072), BF16),
            v((4, 4, 192, 128), BF16),
            v((4, 192, 512), BF16),
            v((4, 192, 512), BF16),
            v((128, 1024), BF16),
            v((4, 4, 128, 256), BF16),
            v((4, 128, 384), BF16),
            v((4, 128, 384), BF16),
            v((3, 128, 384), BF16),
            v((3, 128, 384), BF16),
            v((8, 8, 128), F32),
            v((4, 8, 384), F32),
            v((4, 8, 384), F32),
            v((2, 8, 384), F32),
            v((4, 4, 2, 96, 256), BF16),
            v((4, 2, 96, 256), BF16),
            v((4, 2, 2, 96, 256), BF16),
            v((4, 96, 256), BF16),
            v((128, 1024), BF16),
            v((128, 384), BF16),
            v((4, 96, 256), F32),
            v((8, 384), F32),
            pltpu.SemaphoreType.DMA((SENDS,)),
            pltpu.SemaphoreType.DMA((RECVS,)),
            pltpu.SemaphoreType.DMA((16,)),
        ],
        compiler_params=pltpu.CompilerParams(
            collective_id=0, has_side_effects=True, vmem_limit_bytes=60 * 1024 * 1024
        ),
    )(
        queries, keys, values, prefix_keys, prefix_values, doc_start, out_weight, residual,
        student_hidden, student_gain.reshape(8, 1, 384), proj_weight,
    )
    return pl.pallas_call(
        hand_over,
        out_shape=(*shapes, jax.ShapeDtypeStruct((384,), F32)),
        in_specs=[vmem] * 4,
        out_specs=(vmem,) * 4,
    )(*outs)


def solution(mesh):
    finer = Mesh(mesh.devices.reshape(4, 4, 2, 4, 2), SEQ + TEN)
    rows = P(SEQ, TEN)
    return jax.shard_map(
        local,
        mesh=finer,
        in_specs=(
            rows, rows, rows, rows, rows, P(), P(TEN, None), P(SEQ + TEN, None), rows, P(), rows,
        ),
        out_specs=(rows, rows, rows, P(TEN)),
        check_vma=False,
    )
```

```python
import math

import jax
import jax.numpy as jnp
from jax import lax
from jax.experimental import pallas as pl
from jax.experimental.pallas import tpu as pltpu
from jax.sharding import Mesh
from jax.sharding import PartitionSpec as P

MESH = pl.DeviceIdType.MESH
F32 = jnp.float32
BF16 = jnp.bfloat16
NEG = -1e30
SEQ = ("x", "y", "zh")
TEN = ("zl", "c")
SENDS, RECVS = 93, 198


def mod4(v):
    return lax.rem(v, 4)


class Wire:
    def __init__(self, send, recv):
        self.send, self.recv = send, recv
        self.recv_used, self.send_used, self.spare, self.open = 0, 0, [], []

    def copy(self, src, dst, dev):
        if self.spare:
            i = self.spare.pop(0)
        else:
            i = self.send_used
            self.send_used += 1
        d = pltpu.make_async_remote_copy(
            src_ref=src,
            dst_ref=dst,
            send_sem=self.send.at[i],
            recv_sem=self.recv.at[self.recv_used],
            device_id=dev,
            device_id_type=MESH,
        )
        self.recv_used += 1
        d.start()
        self.open.append((i, d))
        return d

    def settle(self, count=None):
        count = len(self.open) if count is None else count
        for i, d in self.open[:count]:
            d.wait_send()
            self.spare.append(i)
        self.open = self.open[count:]


class Gather:
    def __init__(self, wire, at, first, second, coord):
        self.wire, self.at, self.first, self.second = wire, at, first, second
        self.a, self.b, self.z = coord[first], coord[second], coord["zh"]
        self.r, self.l, self.hr, self.hl = {}, {}, {}, {}
        a = self.a
        self.order = (a, mod4(a + 3), mod4(a + 1), mod4(a + 2))

    def z_send(self):
        own = self.at(self.a, self.b, self.z, 1, None)
        self.zd = self.wire.copy(own, own, {"zh": 1 - self.z})

    def z_wait(self):
        self.zd.wait_recv()

    def ring(self, key, ref_of, axis, pos):
        own = ref_of(pos, None)
        self.r[key] = self.wire.copy(own, own, {axis: mod4(pos + 1)})
        self.l[key] = self.wire.copy(own, own, {axis: mod4(pos + 3)})

    def forward(self, key, ref_of, axis, pos):
        self.r[key].wait_recv()
        left = ref_of(mod4(pos + 3), 0)
        self.hr[key] = self.wire.copy(left, left, {axis: mod4(pos + 1)})
        self.l[key].wait_recv()
        right = ref_of(mod4(pos + 1), 1)
        self.hl[key] = self.wire.copy(right, right, {axis: mod4(pos + 3)})

    def done(self, key):
        self.hr[key].wait_recv()
        self.hl[key].wait_recv()

    def one(self, j):
        zq = self.z if j == 0 else 1 - self.z
        return lambda pos, half: self.at(pos, self.b, zq, 1, half)

    def two(self, j, k):
        aq = self.order[k]
        if j is None:
            return lambda pos, half: self.at(aq, pos, 0, 2, half)
        zq = self.z if j == 0 else 1 - self.z
        return lambda pos, half: self.at(aq, pos, zq, 1, half)

    def p1_send(self, j):
        self.ring(("1", j), self.one(j), self.first, self.a)

    def p1_fwd(self, j):
        self.forward(("1", j), self.one(j), self.first, self.a)

    def p1_done(self, j):
        self.done(("1", j))

    def p2_send(self, j, k):
        self.ring(("2", j, k), self.two(j, k), self.second, self.b)

    def p2_fwd(self, j, k):
        self.forward(("2", j, k), self.two(j, k), self.second, self.b)

    def p2_done(self, j, k):
        self.done(("2", j, k))


class Scatter:
    def __init__(self, wire, part, near, far, axis, pos):
        self.wire, self.part, self.near, self.far = wire, part, near, far
        self.axis, self.pos = axis, pos

    def start(self):
        p, ax = self.pos, self.axis
        opp = mod4(p + 2)
        self.r1 = self.wire.copy(self.part(opp, 0), self.near.at[0], {ax: mod4(p + 1)})
        self.l1 = self.wire.copy(self.part(opp, 1), self.near.at[1], {ax: mod4(p + 3)})

    def middle(self):
        p, ax = self.pos, self.axis
        right, left = mod4(p + 1), mod4(p + 3)
        self.r1.wait_recv()
        ref = self.part(right, 0)
        ref[...] = (ref[...].astype(F32) + self.near[0].astype(F32)).astype(BF16)
        self.r2 = self.wire.copy(self.part(right, None), self.far.at[0], {ax: right})
        self.l1.wait_recv()
        ref = self.part(left, 1)
        ref[...] = (ref[...].astype(F32) + self.near[1].astype(F32)).astype(BF16)
        self.l2 = self.wire.copy(self.part(left, None), self.far.at[1], {ax: left})

    def finish(self):
        self.r2.wait_recv()
        self.l2.wait_recv()
        ref = self.part(self.pos, None)
        ref[...] = (
            ref[...].astype(F32) + self.far[0].astype(F32) + self.far[1].astype(F32)
        ).astype(BF16)


def kernel(
    q_hbm, k_hbm, v_hbm, pk_hbm, pv_hbm, doc_hbm, w_hbm, res_hbm, hid_hbm, gain_hbm, proj_hbm,
    teacher_out, sgrad_out, pgrad_out, ggrad_out,
    kvb, pj, w, q, qs, part_of, part_in, stat_of, stat_in, hid, res, mx, tot, acc, att,
    bsend, brecv, bz, zrecv, tacc, nrm, nrmt, nxtx, nxty, mis, mch,
    fsend, frecv, fz, fzrecv, rowbuf, gacc, g1, g2, g3, g4, g5,
    gp, near, far, zpart, tcb, sgb, pgb, ggb, doc, gain,
    ssem, rsem, lsem,
):
    x, y, z = lax.axis_index("x"), lax.axis_index("y"), lax.axis_index("zh")
    zl, c = lax.axis_index("zl"), lax.axis_index("c")
    coord = {"x": x, "y": y, "zh": z}
    seq = (x * 4 + y) * 2 + z
    t = zl * 2 + c
    wire = Wire(ssem, rsem)
    mate = {"c": 1 - c}

    def tensor_peer(dz, dc):
        return {"zl": mod4(zl + dz), "c": c if dc == 0 else 1 - c}

    def tensor_index(dz, dc):
        return mod4(zl + dz) * 2 + (c if dc == 0 else 1 - c)

    peers = [(dz, dc) for dz in (2, 1, 3, 0) for dc in (0, 1) if (dz, dc) != (0, 0)]

    loads = [
        (pk_hbm, kvb.at[y, z, 0]),
        (pv_hbm, kvb.at[y, z, 1]),
        (k_hbm, kvb.at[y, z, 2]),
        (v_hbm, kvb.at[y, z, 3]),
        (proj_hbm, pj.at[seq]),
        (hid_hbm, hid.at[t]),
        (q_hbm, q),
        (
            res_hbm.at[:, pl.ds(pl.multiple_of(t * 1024, 1024), 1024)],
            res.at[pl.ds(pl.multiple_of(t * 16, 16), 16), :],
        ),
        (w_hbm, w),
        (doc_hbm, doc),
        (gain_hbm, gain),
    ]
    local = [pltpu.make_async_copy(s, d, lsem.at[i]) for i, (s, d) in enumerate(loads)]
    for d in local:
        d.start()

    written = []

    def put(src, dst):
        d = pltpu.make_async_copy(src, dst, lsem.at[len(loads) + len(written)])
        d.start()
        written.append(d)

    barrier = pltpu.get_barrier_semaphore()
    greet = [
        {"x": mod4(x + 1)}, {"x": mod4(x + 2)}, {"x": mod4(x + 3)},
        {"y": mod4(y + 1)}, {"y": mod4(y + 2)}, {"y": mod4(y + 3)},
        {"zh": 1 - z},
    ] + [tensor_peer(*p) for p in peers]
    for dev in greet:
        pl.semaphore_signal(barrier, inc=1, device_id=dev, device_id_type=MESH)
    pl.semaphore_wait(barrier, len(greet))

    def kv_at(a, b, zq, count, half):
        return kvb.at[a, zq] if half is None else kvb.at[a, zq, pl.ds(2 * half, 2)]

    def q_at(pos, half):
        return qs.at[pos] if half is None else qs.at[pos, pl.ds(256 * half, 256)]

    def pj_at(low, x_first):
        def at(a, b, zq, count, half):
            slot = ((a * 4 + b) if x_first else (b * 4 + a)) * 2 + zq
            where = slot if count == 1 else pl.ds(slot, 2)
            cols = pl.ds(0, 1024) if half is None else pl.ds(512 * half, 512)
            return pj.at[where, pl.ds(low, 48), cols]

        return at

    kv = Gather(wire, kv_at, "y", "x", coord)
    ring = Gather(wire, None, "x", "y", coord)
    pr = (
        Gather(wire, pj_at(0, True), "x", "y", coord),
        Gather(wire, pj_at(48, False), "y", "x", coord),
    )

    def both(streams, name, *args):
        for s in streams:
            getattr(s, name)(*args)

    factor = 128 ** (-0.5) * math.log2(math.e)
    column = lax.broadcasted_iota(jnp.int32, (512, 512), 1)
    position = x * 1024 + (column // 128) * 256 + lax.rem(column, 128)
    token = lax.rem(lax.broadcasted_iota(jnp.int32, (512, 512), 0), 128) + (y * 2 + z) * 128
    diagonal = lax.broadcasted_iota(jnp.int32, (128, 128), 0) == lax.broadcasted_iota(
        jnp.int32, (128, 128), 1
    )

    def wide(v):
        return jnp.concatenate([v] * 4, axis=1)

    def block(xq, kb, vb, visible):
        s = lax.dot_general(
            qs[xq], kb.reshape(512, 128), (((1,), (1,)), ((), ())), preferred_element_type=F32
        ) * factor
        s = jnp.where(visible, s, NEG)
        old = mx[xq]
        new = jnp.maximum(old, jnp.broadcast_to(jnp.max(s, axis=1, keepdims=True), (512, 128)))
        p = jnp.exp2(s - wide(new))
        scale = jnp.exp2(old - new)
        mx[xq] = new
        tot[xq] = tot[xq] * scale + jnp.broadcast_to(
            jnp.sum(p, axis=1, keepdims=True), (512, 128)
        )
        acc[xq] = acc[xq] * scale + jnp.dot(
            p.astype(BF16), vb.reshape(512, 128), preferred_element_type=F32
        )

    def attend(j, xq):
        zq = z if j == 0 else 1 - z
        here = position + zq * 128
        block(xq, kvb[:, zq, 0], kvb[:, zq, 1], here >= doc[0])
        block(xq, kvb[:, zq, 2], kvb[:, zq, 3], here <= token + xq * 1024)

    def to_row(v):
        return jnp.sum(jnp.where(diagonal, v, 0.0), axis=0, keepdims=True)

    def to_column(v):
        wide_row = jnp.broadcast_to(v, (128, 128))
        return jnp.sum(jnp.where(diagonal, wide_row, 0.0), axis=1, keepdims=True)

    back = {}

    def give_back(d):
        xq = mod4(x + d)
        part_of[d - 1] = (acc[xq] / tot[xq]).astype(BF16)
        stat_of[d - 1] = jnp.concatenate(
            [to_row(r[xq, h * 128 : (h + 1) * 128, :]) for r in (mx, tot) for h in range(4)],
            axis=0,
        )
        back[d] = (
            wire.copy(part_of.at[d - 1], part_in.at[d - 1], {"x": xq}),
            wire.copy(stat_of.at[d - 1], stat_in.at[d - 1], {"x": xq}),
        )

    local[6].wait()
    for h in range(4):
        qs[x, h * 128 : (h + 1) * 128, :] = q[:, h * 128 : (h + 1) * 128]
    for d in local[:4]:
        d.wait()
    kv.z_send()
    kv.p1_send(0)
    ring.ring("q", q_at, "x", x)
    for i in range(4):
        mx[i] = jnp.full((512, 128), NEG, F32)
        tot[i] = jnp.zeros((512, 128), F32)
        acc[i] = jnp.zeros((512, 128), F32)
    local[4].wait()
    ring.forward("q", q_at, "x", x)
    kv.p1_fwd(0)
    both(pr, "p1_send", 0)
    pr[1].p2_send(0, 0)
    both(pr, "z_send")
    kv.z_wait()
    kv.p1_send(1)
    ring.done("q")
    kv.p1_done(0)
    local[9].wait()
    attend(0, mod4(x + 2))
    both(pr, "p1_fwd", 0)
    pr[1].p2_send(0, 1)
    pr[1].p2_send(0, 2)
    attend(0, mod4(x + 1))
    kv.p1_fwd(1)
    for k in range(3):
        pr[0].p2_send(0, k)
    attend(0, mod4(x + 3))
    both(pr, "p1_done", 0)
    pr[0].p2_send(0, 3)
    attend(0, x)
    kv.p1_done(1)
    local[5].wait()
    hz = {dz: wire.copy(hid.at[t], hid.at[t], tensor_peer(dz, 0)) for dz in (2, 1, 3)}
    hmate = [wire.copy(hid.at[t], hid.at[t], mate)]
    early = len(wire.open)
    attend(1, mod4(x + 2))
    give_back(2)
    attend(1, mod4(x + 1))
    give_back(1)
    attend(1, mod4(x + 3))
    give_back(3)
    pr[1].p2_send(0, 3)
    both(pr, "z_wait")
    both(pr, "p1_send", 1)
    both(pr, "p2_fwd", 0, 0)
    attend(1, x)
    rsend = []
    for p in peers:
        cols = pl.ds(pl.multiple_of(tensor_index(*p) * 1024, 1024), 1024)
        rsend.append(
            wire.copy(
                res_hbm.at[:, cols],
                res.at[pl.ds(pl.multiple_of(t * 16, 16), 16), :],
                tensor_peer(*p),
            )
        )
    both(pr, "p2_send", 1, 0)
    for d in (2, 1, 3):
        for r in back[d]:
            r.wait_recv()
    for h in range(4):
        rows = slice(h * 128, (h + 1) * 128)
        maxes = [mx[x, rows, :]] + [to_column(stat_in[i, h : h + 1, :]) for i in range(3)]
        most = jnp.maximum(
            jnp.maximum(maxes[0], maxes[1]), jnp.maximum(maxes[2], maxes[3])
        )
        scale = jnp.exp2(maxes[0] - most)
        over, under = acc[x, rows, :] * scale, tot[x, rows, :] * scale
        for i in range(3):
            scale = jnp.exp2(maxes[1 + i] - most) * to_column(stat_in[i, 4 + h : 5 + h, :])
            over = over + scale * part_in[i, rows, :].astype(F32)
            under = under + scale
        att[:, h * 128 : (h + 1) * 128] = (over / under).astype(BF16)

    local[8].wait()
    turns = (2, 1, 3, 0)

    def projected(dz, dc):
        cols = pl.ds(pl.multiple_of(tensor_index(dz, dc) * 1024, 1024), 1024)
        return jnp.dot(att[...], w[:, cols], preferred_element_type=F32)

    half = {}
    for dz in turns:
        bsend[dz] = projected(dz, 1).astype(BF16)
        half[dz] = wire.copy(bsend.at[dz], brecv.at[dz], mate)
    zsum = {}
    for dz in turns:
        mine = projected(dz, 0)
        half[dz].wait_recv()
        mine = mine + brecv[dz].astype(F32)
        if dz:
            bz[dz - 1] = mine.astype(BF16)
            zsum[dz] = wire.copy(bz.at[dz - 1], zrecv.at[dz - 1], tensor_peer(dz, 0))
        else:
            tacc[...] = mine
    wire.settle(early)
    both(pr, "p2_fwd", 0, 1)
    both(pr, "p1_fwd", 1)
    both(pr, "p2_send", 1, 1)
    both(pr, "p2_send", 1, 2)
    both(pr, "p2_fwd", 0, 2)
    both(pr, "p2_fwd", 0, 3)
    both(pr, "p1_done", 1)
    both(pr, "p2_send", 1, 3)
    for dz in (2, 1, 3):
        hz[dz].wait_recv()
        slot = mod4(zl + 4 - dz) * 2 + c
        hmate.append(wire.copy(hid.at[slot], hid.at[slot], mate))
    local[10].wait()

    for d in hmate:
        d.wait_recv()
    square = jnp.zeros((128, 384), F32)
    for i in range(8):
        h = hid[i].astype(F32)
        square = square + h * h
    inverse = lax.rsqrt(jnp.sum(square, axis=1, keepdims=True) / 3072.0 + 1e-05)
    for i in range(8):
        n = (hid[i].astype(F32) * inverse * gain[i]).astype(BF16)
        nrm[:, i * 384 : (i + 1) * 384] = n
        nrmt[i // 2, 2 * (i % 2) : 2 * (i % 2) + 2] = n.T.reshape(2, 192, 128)

    halfrows = pl.ds(2 * c, 2)

    def token_cols(pos):
        return pl.ds(pl.multiple_of(pos * 128, 128), 128)

    nx, nmate, middle = {}, [], len(wire.open)
    for d in (2, 1, 3):
        nx["x", d] = wire.copy(
            nrmt.at[mod4(x + d), halfrows], nxtx.at[halfrows, :, token_cols(x)], {"x": mod4(x + d)}
        )
        nx["y", d] = wire.copy(
            nrmt.at[halfrows, mod4(y + d)], nxty.at[halfrows, :, token_cols(y)], {"y": mod4(y + d)}
        )
    nxtx[:, :, token_cols(x)] = nrmt[x]
    nxty[:, :, token_cols(y)] = nrmt[:, y]
    both(pr, "p2_fwd", 1, 0)
    both(pr, "p2_fwd", 1, 1)
    both(pr, "p2_fwd", 1, 2)
    both(pr, "p2_fwd", 1, 3)
    for d in (2, 1, 3):
        for axis, pos, buf in (("x", x, nxtx), ("y", y, nxty)):
            nx[axis, d].wait_recv()
            came = buf.at[halfrows, :, token_cols(mod4(pos + 4 - d))]
            nmate.append(wire.copy(came, came, mate))
    for d in rsend:
        d.wait_recv()
    local[7].wait()
    tacc[...] = tacc[...] + res[...].astype(F32)
    wire.settle(middle)
    for j in range(2):
        for k in range(4):
            both(pr, "p2_done", j, k)
    pre = jnp.zeros((128, 1024), F32)
    for i in range(4):
        pre = pre + jnp.dot(
            nrm[:, i * 768 : (i + 1) * 768],
            pj[pl.ds(8 * i, 8)].reshape(768, 1024),
            preferred_element_type=F32,
        )
    for dz in turns[:3]:
        zsum[dz].wait_recv()
    teacher = (
        tacc[...] + zrecv[0].astype(F32) + zrecv[1].astype(F32) + zrecv[2].astype(F32)
    ).astype(BF16)
    tcb[...] = teacher
    put(tcb, teacher_out)
    mismatch = (pre - teacher.astype(F32)).astype(BF16)
    mis[...] = mismatch
    lanes = [("x", x, nxtx, "y", y), ("y", y, nxty, "x", x)] * 2
    for i, lane in enumerate(lanes):
        mch[i, lane[1]] = mismatch[:, i * 256 : (i + 1) * 256]

    def mch_at(i):
        return lambda p, h: mch.at[i, p] if h is None else mch.at[i, p, pl.ds(64 * h, 64)]

    sums = []
    for i, (axis, pos, _, other, there) in enumerate(lanes):
        ring.ring(i, mch_at(i), axis, pos)
        sums.append(
            Scatter(
                wire,
                lambda p, h, i=i: gp.at[i, p] if h is None else gp.at[i, p, h],
                near.at[i],
                far.at[i],
                other,
                there,
            )
        )

    def pass_on(i):
        ring.forward(i, mch_at(i), lanes[i][0], lanes[i][1])

    def product(i):
        ring.done(i)
        g = jnp.dot(
            lanes[i][2][...].reshape(768, 512),
            mch[i].reshape(512, 256),
            preferred_element_type=F32,
        )
        gp[i] = g.astype(BF16).reshape(4, 2, 96, 256)
        sums[i].start()

    last = {}

    def across(i):
        sums[i].finish()
        last[i] = wire.copy(gp.at[i, lanes[i][4], 1 - z], zpart.at[i], {"zh": 1 - z})

    def state_grad(dz, dc):
        rows = pj[pl.ds(4 * tensor_index(dz, dc), 4)].reshape(384, 1024)
        return lax.dot_general(
            mis[...], rows, (((1,), (1,)), ((), ())), preferred_element_type=F32
        )

    inner = jnp.zeros((128, 384), F32)

    def parts(dz, dc, mine):
        i = tensor_index(dz, dc)
        here = mine * hid[i].astype(F32)
        g1[0, pl.ds(i, 1), :] = jnp.sum(here * inverse, axis=0, keepdims=True)
        return inner + here * gain[i]

    def to_mate(dz):
        mine = state_grad(dz, 1)
        fsend[dz] = mine.astype(BF16)
        half[dz] = wire.copy(fsend.at[dz], frecv.at[dz], mate)
        return parts(dz, 1, mine)

    def along_z(dz):
        mine = state_grad(dz, 0)
        added = parts(dz, 0, mine)
        half[dz].wait_recv()
        mine = mine + frecv[dz].astype(F32)
        if dz:
            fz[dz - 1] = mine.astype(BF16)
            zsum[dz] = wire.copy(fz.at[dz - 1], fzrecv.at[dz - 1], tensor_peer(dz, 0))
        else:
            gacc[...] = mine
        return added

    for dz in turns:
        inner = to_mate(dz)
    inner = along_z(2)
    inner = along_z(1)
    pass_on(0)
    pass_on(1)
    inner = along_z(3)
    pass_on(2)
    pass_on(3)
    inner = along_z(0)
    rowbuf[0] = jnp.broadcast_to(to_row(jnp.sum(inner, axis=1, keepdims=True)), (8, 128))
    rows = [wire.copy(rowbuf.at[0], rowbuf.at[1 + i], tensor_peer(*p)) for i, p in enumerate(peers)]
    g1d = [wire.copy(g1.at[0], g1.at[d], {"x": mod4(x + d)}) for d in (1, 2, 3)]
    for d in nmate:
        d.wait_recv()
    for i in range(4):
        product(i)
    for d in g1d:
        d.wait_recv()
    g2[0] = g1[0] + g1[1] + g1[2] + g1[3]
    g2d = [wire.copy(g2.at[0], g2.at[d], {"y": mod4(y + d)}) for d in (1, 2, 3)]
    sums[0].middle()
    sums[1].middle()
    sums[2].middle()
    sums[3].middle()
    for d in g2d:
        d.wait_recv()
    g3[0] = g2[0] + g2[1] + g2[2] + g2[3]
    g3d = wire.copy(g3.at[0], g3.at[1], {"zh": 1 - z})
    across(0)
    across(1)
    for dz in turns[:3]:
        zsum[dz].wait_recv()
    grad = (
        gacc[...] + fzrecv[0].astype(F32) + fzrecv[1].astype(F32) + fzrecv[2].astype(F32)
    )
    for d in rows:
        d.wait_recv()
    total = rowbuf[0]
    for i in range(7):
        total = total + rowbuf[1 + i]
    row_inner = to_column(total[0:1, :]) / 3072.0
    sgb[...] = (
        inverse * gain[t] * grad - hid[t].astype(F32) * inverse * inverse * inverse * row_inner
    ).astype(BF16)
    put(sgb, sgrad_out)
    across(2)
    across(3)
    g3d.wait_recv()
    whole = g3[0] + g3[1]
    for i in range(8):
        g4[i] = jnp.broadcast_to(whole[i : i + 1, :], (8, 384))
    g4d = [
        wire.copy(g4.at[tensor_index(*p)], g5.at[i], tensor_peer(*p)) for i, p in enumerate(peers)
    ]
    grad_scale = 1.0 / 64.0
    for i in range(4):
        last[i].wait_recv()
        pgb[i] = (gp[i, lanes[i][4], z].astype(F32) + zpart[i].astype(F32)) * grad_scale
        put(pgb.at[i], pgrad_out.at[:, pl.ds(256 * i, 256)])
    total = g4[t]
    for i, d in enumerate(g4d):
        d.wait_recv()
        total = total + g5[i]
    ggb[...] = total * grad_scale
    put(ggb, ggrad_out)
    wire.settle()
    assert (wire.send_used, wire.recv_used) == (SENDS, RECVS), (wire.send_used, wire.recv_used)
    for d in written:
        d.wait()


def hand_over(a, b, c, d, a_out, b_out, c_out, d_out):
    a_out[...] = a[...]
    b_out[...] = b[...]
    c_out[...] = c[...]
    d_out[...] = d[0]


def local(
    queries, keys, values, prefix_keys, prefix_values, doc_start, out_weight, residual,
    student_hidden, student_gain, proj_weight,
):
    vmem = pl.BlockSpec(memory_space=pltpu.VMEM)
    anyspace = pl.BlockSpec(memory_space=pl.ANY)
    v = pltpu.VMEM
    shapes = [
        jax.ShapeDtypeStruct((128, 1024), BF16),
        jax.ShapeDtypeStruct((128, 384), BF16),
        jax.ShapeDtypeStruct((96, 1024), F32),
    ]
    outs = pl.pallas_call(
        kernel,
        out_shape=(*shapes, jax.ShapeDtypeStruct((8, 384), F32)),
        in_specs=[anyspace] * 11,
        out_specs=(anyspace,) * 4,
        scratch_shapes=[
            v((4, 2, 4, 128, 128), BF16),
            v((32, 96, 1024), BF16),
            v((512, 8192), BF16),
            v((128, 512), BF16),
            v((4, 512, 128), BF16),
            v((3, 512, 128), BF16),
            v((3, 512, 128), BF16),
            v((3, 8, 128), F32),
            v((3, 8, 128), F32),
            v((8, 128, 384), BF16),
            v((128, 1024), BF16),
            v((4, 512, 128), F32),
            v((4, 512, 128), F32),
            v((4, 512, 128), F32),
            v((128, 512), BF16),
            v((4, 128, 1024), BF16),
            v((4, 128, 1024), BF16),
            v((3, 128, 1024), BF16),
            v((3, 128, 1024), BF16),
            v((128, 1024), F32),
            v((128, 3072), BF16),
            v((4, 4, 192, 128), BF16),
            v((4, 192, 512), BF16),
            v((4, 192, 512), BF16),
            v((128, 1024), BF16),
            v((4, 4, 128, 256), BF16),
            v((4, 128, 384), BF16),
            v((4, 128, 384), BF16),
            v((3, 128, 384), BF16),
            v((3, 128, 384), BF16),
            v((8, 8, 128), F32),
            v((128, 384), F32),
            v((4, 8, 384), F32),
            v((4, 8, 384), F32),
            v((2, 8, 384), F32),
            v((8, 8, 384), F32),
            v((7, 8, 384), F32),
            v((4, 4, 2, 96, 256), BF16),
            v((4, 2, 96, 256), BF16),
            v((4, 2, 2, 96, 256), BF16),
            v((4, 96, 256), BF16),
            v((128, 1024), BF16),
            v((128, 384), BF16),
            v((4, 96, 256), F32),
            v((8, 384), F32),
            pltpu.SMEM((1,), jnp.int32),
            v((8, 1, 384), F32),
            pltpu.SemaphoreType.DMA((SENDS,)),
            pltpu.SemaphoreType.DMA((RECVS,)),
            pltpu.SemaphoreType.DMA((18,)),
        ],
        compiler_params=pltpu.CompilerParams(
            collective_id=0, has_side_effects=True, vmem_limit_bytes=60 * 1024 * 1024
        ),
    )(
        queries, keys, values, prefix_keys, prefix_values, doc_start, out_weight, residual,
        student_hidden, student_gain.reshape(8, 1, 384), proj_weight,
    )
    return pl.pallas_call(
        hand_over,
        out_shape=(*shapes, jax.ShapeDtypeStruct((384,), F32)),
        in_specs=[vmem] * 4,
        out_specs=(vmem,) * 4,
    )(*outs)


def solution(mesh):
    finer = Mesh(mesh.devices.reshape(4, 4, 2, 4, 2), SEQ + TEN)
    rows = P(SEQ, TEN)
    return jax.shard_map(
        local,
        mesh=finer,
        in_specs=(
            rows, rows, rows, rows, rows, P(), P(TEN, None), P(SEQ + TEN, None), rows, P(), rows,
        ),
        out_specs=(rows, rows, rows, P(TEN)),
        check_vma=False,
    )
```

```python
import math

import jax
import jax.numpy as jnp
from jax import lax
from jax.experimental import pallas as pl
from jax.experimental.pallas import tpu as pltpu
from jax.sharding import Mesh
from jax.sharding import PartitionSpec as P

MESH = pl.DeviceIdType.MESH
F32 = jnp.float32
BF16 = jnp.bfloat16
NEG = -1e30
SEQ = ("x", "y", "zh")
TEN = ("zl", "c")
SENDS, RECVS = 95, 198


def mod4(v):
    return lax.rem(v, 4)


class Wire:
    def __init__(self, send, recv):
        self.send, self.recv = send, recv
        self.recv_used, self.send_used, self.spare, self.open = 0, 0, [], []

    def copy(self, src, dst, dev):
        if self.spare:
            i = self.spare.pop(0)
        else:
            i = self.send_used
            self.send_used += 1
        d = pltpu.make_async_remote_copy(
            src_ref=src,
            dst_ref=dst,
            send_sem=self.send.at[i],
            recv_sem=self.recv.at[self.recv_used],
            device_id=dev,
            device_id_type=MESH,
        )
        self.recv_used += 1
        d.start()
        self.open.append((i, d))
        return d

    def settle(self, count=None):
        count = len(self.open) if count is None else count
        for i, d in self.open[:count]:
            d.wait_send()
            self.spare.append(i)
        self.open = self.open[count:]


class Gather:
    def __init__(self, wire, at, first, second, coord):
        self.wire, self.at, self.first, self.second = wire, at, first, second
        self.a, self.b, self.z = coord[first], coord[second], coord["zh"]
        self.r, self.l, self.hr, self.hl = {}, {}, {}, {}
        a = self.a
        self.order = (a, mod4(a + 3), mod4(a + 1), mod4(a + 2))

    def z_send(self):
        own = self.at(self.a, self.b, self.z, 1, None)
        self.zd = self.wire.copy(own, own, {"zh": 1 - self.z})

    def z_wait(self):
        self.zd.wait_recv()

    def ring(self, key, ref_of, axis, pos):
        own = ref_of(pos, None)
        self.r[key] = self.wire.copy(own, own, {axis: mod4(pos + 1)})
        self.l[key] = self.wire.copy(own, own, {axis: mod4(pos + 3)})

    def forward(self, key, ref_of, axis, pos):
        self.r[key].wait_recv()
        left = ref_of(mod4(pos + 3), 0)
        self.hr[key] = self.wire.copy(left, left, {axis: mod4(pos + 1)})
        self.l[key].wait_recv()
        right = ref_of(mod4(pos + 1), 1)
        self.hl[key] = self.wire.copy(right, right, {axis: mod4(pos + 3)})

    def done(self, key):
        self.hr[key].wait_recv()
        self.hl[key].wait_recv()

    def one(self, j):
        zq = self.z if j == 0 else 1 - self.z
        return lambda pos, half: self.at(pos, self.b, zq, 1, half)

    def two(self, j, k):
        aq = self.order[k]
        if j is None:
            return lambda pos, half: self.at(aq, pos, 0, 2, half)
        zq = self.z if j == 0 else 1 - self.z
        return lambda pos, half: self.at(aq, pos, zq, 1, half)

    def p1_send(self, j):
        self.ring(("1", j), self.one(j), self.first, self.a)

    def p1_fwd(self, j):
        self.forward(("1", j), self.one(j), self.first, self.a)

    def p1_done(self, j):
        self.done(("1", j))

    def p2_send(self, j, k):
        self.ring(("2", j, k), self.two(j, k), self.second, self.b)

    def p2_fwd(self, j, k):
        self.forward(("2", j, k), self.two(j, k), self.second, self.b)

    def p2_done(self, j, k):
        self.done(("2", j, k))


class Scatter:
    def __init__(self, wire, part, near, far, axis, pos):
        self.wire, self.part, self.near, self.far = wire, part, near, far
        self.axis, self.pos = axis, pos

    def start(self):
        p, ax = self.pos, self.axis
        opp = mod4(p + 2)
        self.r1 = self.wire.copy(self.part(opp, 0), self.near.at[0], {ax: mod4(p + 1)})
        self.l1 = self.wire.copy(self.part(opp, 1), self.near.at[1], {ax: mod4(p + 3)})

    def middle(self):
        p, ax = self.pos, self.axis
        right, left = mod4(p + 1), mod4(p + 3)
        self.r1.wait_recv()
        ref = self.part(right, 0)
        ref[...] = (ref[...].astype(F32) + self.near[0].astype(F32)).astype(BF16)
        self.r2 = self.wire.copy(self.part(right, None), self.far.at[0], {ax: right})
        self.l1.wait_recv()
        ref = self.part(left, 1)
        ref[...] = (ref[...].astype(F32) + self.near[1].astype(F32)).astype(BF16)
        self.l2 = self.wire.copy(self.part(left, None), self.far.at[1], {ax: left})

    def finish(self):
        self.r2.wait_recv()
        self.l2.wait_recv()
        ref = self.part(self.pos, None)
        ref[...] = (
            ref[...].astype(F32) + self.far[0].astype(F32) + self.far[1].astype(F32)
        ).astype(BF16)


def kernel(
    q_hbm, k_hbm, v_hbm, pk_hbm, pv_hbm, doc_hbm, w_hbm, res_hbm, hid_hbm, gain_hbm, proj_hbm,
    teacher_out, sgrad_out, pgrad_out, ggrad_out,
    kvb, pj, w, q, qs, part_of, part_in, stat_of, stat_in, hid, res, mx, tot, acc, att,
    bsend, brecv, bz, zrecv, tacc, nrm, nrmt, nxtx, nxty, mis, mch,
    fsend, frecv, fz, fzrecv, rowbuf, gacc, g1, g2, g3, g4, g5,
    gp, near, far, zpart, tcb, sgb, pgb, ggb, doc, gain,
    ssem, rsem, lsem,
):
    x, y, z = lax.axis_index("x"), lax.axis_index("y"), lax.axis_index("zh")
    zl, c = lax.axis_index("zl"), lax.axis_index("c")
    coord = {"x": x, "y": y, "zh": z}
    seq = (x * 4 + y) * 2 + z
    t = zl * 2 + c
    wire = Wire(ssem, rsem)
    mate = {"c": 1 - c}

    def tensor_peer(dz, dc):
        return {"zl": mod4(zl + dz), "c": c if dc == 0 else 1 - c}

    def tensor_index(dz, dc):
        return mod4(zl + dz) * 2 + (c if dc == 0 else 1 - c)

    peers = [(dz, dc) for dz in (2, 1, 3, 0) for dc in (0, 1) if (dz, dc) != (0, 0)]

    loads = [
        (pk_hbm, kvb.at[y, z, 0]),
        (pv_hbm, kvb.at[y, z, 1]),
        (k_hbm, kvb.at[y, z, 2]),
        (v_hbm, kvb.at[y, z, 3]),
        (proj_hbm, pj.at[seq]),
        (hid_hbm, hid.at[t]),
        (q_hbm, q),
        (
            res_hbm.at[:, pl.ds(pl.multiple_of(t * 1024, 1024), 1024)],
            res.at[pl.ds(pl.multiple_of(t * 16, 16), 16), :],
        ),
        (w_hbm, w),
        (doc_hbm, doc),
        (gain_hbm, gain),
    ]
    local = [pltpu.make_async_copy(s, d, lsem.at[i]) for i, (s, d) in enumerate(loads)]
    for d in local:
        d.start()

    written = []

    def put(src, dst):
        d = pltpu.make_async_copy(src, dst, lsem.at[len(loads) + len(written)])
        d.start()
        written.append(d)

    barrier = pltpu.get_barrier_semaphore()
    greet = [
        {"x": mod4(x + 1)}, {"x": mod4(x + 2)}, {"x": mod4(x + 3)},
        {"y": mod4(y + 1)}, {"y": mod4(y + 2)}, {"y": mod4(y + 3)},
        {"zh": 1 - z},
    ] + [tensor_peer(*p) for p in peers]
    for dev in greet:
        pl.semaphore_signal(barrier, inc=1, device_id=dev, device_id_type=MESH)
    pl.semaphore_wait(barrier, len(greet))

    def kv_at(a, b, zq, count, half):
        return kvb.at[a, zq] if half is None else kvb.at[a, zq, pl.ds(2 * half, 2)]

    def q_at(pos, half):
        return qs.at[pos] if half is None else qs.at[pos, pl.ds(256 * half, 256)]

    def pj_at(low, x_first):
        def at(a, b, zq, count, half):
            slot = ((a * 4 + b) if x_first else (b * 4 + a)) * 2 + zq
            where = slot if count == 1 else pl.ds(slot, 2)
            cols = pl.ds(0, 1024) if half is None else pl.ds(512 * half, 512)
            return pj.at[where, pl.ds(low, 48), cols]

        return at

    kv = Gather(wire, kv_at, "y", "x", coord)
    ring = Gather(wire, None, "x", "y", coord)
    pr = (
        Gather(wire, pj_at(0, True), "x", "y", coord),
        Gather(wire, pj_at(48, False), "y", "x", coord),
    )

    def both(streams, name, *args):
        for s in streams:
            getattr(s, name)(*args)

    factor = 128 ** (-0.5) * math.log2(math.e)
    column = lax.broadcasted_iota(jnp.int32, (512, 512), 1)
    position = x * 1024 + (column // 128) * 256 + lax.rem(column, 128)
    token = lax.rem(lax.broadcasted_iota(jnp.int32, (512, 512), 0), 128) + (y * 2 + z) * 128
    diagonal = lax.broadcasted_iota(jnp.int32, (128, 128), 0) == lax.broadcasted_iota(
        jnp.int32, (128, 128), 1
    )

    def wide(v):
        return jnp.concatenate([v] * 4, axis=1)

    def block(xq, kb, vb, visible):
        s = lax.dot_general(
            qs[xq], kb.reshape(512, 128), (((1,), (1,)), ((), ())), preferred_element_type=F32
        ) * factor
        s = jnp.where(visible, s, NEG)
        old = mx[xq]
        new = jnp.maximum(old, jnp.broadcast_to(jnp.max(s, axis=1, keepdims=True), (512, 128)))
        p = jnp.exp2(s - wide(new))
        scale = jnp.exp2(old - new)
        mx[xq] = new
        tot[xq] = tot[xq] * scale + jnp.broadcast_to(
            jnp.sum(p, axis=1, keepdims=True), (512, 128)
        )
        acc[xq] = acc[xq] * scale + jnp.dot(
            p.astype(BF16), vb.reshape(512, 128), preferred_element_type=F32
        )

    def attend(j, xq):
        zq = z if j == 0 else 1 - z
        here = position + zq * 128
        block(xq, kvb[:, zq, 0], kvb[:, zq, 1], here >= doc[0])
        block(xq, kvb[:, zq, 2], kvb[:, zq, 3], here <= token + xq * 1024)

    def to_row(v):
        return jnp.sum(jnp.where(diagonal, v, 0.0), axis=0, keepdims=True)

    def to_column(v):
        wide_row = jnp.broadcast_to(v, (128, 128))
        return jnp.sum(jnp.where(diagonal, wide_row, 0.0), axis=1, keepdims=True)

    back = {}

    def give_back(d):
        xq = mod4(x + d)
        part_of[d - 1] = (acc[xq] / tot[xq]).astype(BF16)
        stat_of[d - 1] = jnp.concatenate(
            [to_row(r[xq, h * 128 : (h + 1) * 128, :]) for r in (mx, tot) for h in range(4)],
            axis=0,
        )
        back[d] = (
            wire.copy(part_of.at[d - 1], part_in.at[d - 1], {"x": xq}),
            wire.copy(stat_of.at[d - 1], stat_in.at[d - 1], {"x": xq}),
        )

    local[6].wait()
    for h in range(4):
        qs[x, h * 128 : (h + 1) * 128, :] = q[:, h * 128 : (h + 1) * 128]
    for d in local[:4]:
        d.wait()
    kv.z_send()
    kv.p1_send(0)
    ring.ring("q", q_at, "x", x)
    for i in range(4):
        mx[i] = jnp.full((512, 128), NEG, F32)
        tot[i] = jnp.zeros((512, 128), F32)
        acc[i] = jnp.zeros((512, 128), F32)
    local[4].wait()
    ring.forward("q", q_at, "x", x)
    kv.p1_fwd(0)
    both(pr, "p1_send", 0)
    pr[1].p2_send(0, 0)
    both(pr, "z_send")
    kv.z_wait()
    kv.p1_send(1)
    ring.done("q")
    kv.p1_done(0)
    local[9].wait()
    attend(0, mod4(x + 2))
    both(pr, "p1_fwd", 0)
    pr[1].p2_send(0, 1)
    pr[1].p2_send(0, 2)
    attend(0, mod4(x + 1))
    kv.p1_fwd(1)
    for k in range(3):
        pr[0].p2_send(0, k)
    attend(0, mod4(x + 3))
    both(pr, "p1_done", 0)
    pr[0].p2_send(0, 3)
    attend(0, x)
    kv.p1_done(1)
    local[5].wait()
    hz = {dz: wire.copy(hid.at[t], hid.at[t], tensor_peer(dz, 0)) for dz in (2, 1, 3)}
    hmate = [wire.copy(hid.at[t], hid.at[t], mate)]
    early = len(wire.open)
    attend(1, mod4(x + 2))
    give_back(2)
    attend(1, mod4(x + 1))
    give_back(1)
    attend(1, mod4(x + 3))
    give_back(3)
    pr[1].p2_send(0, 3)
    both(pr, "z_wait")
    both(pr, "p1_send", 1)
    both(pr, "p2_fwd", 0, 0)
    attend(1, x)
    rsend = []
    for p in peers:
        cols = pl.ds(pl.multiple_of(tensor_index(*p) * 1024, 1024), 1024)
        rsend.append(
            wire.copy(
                res_hbm.at[:, cols],
                res.at[pl.ds(pl.multiple_of(t * 16, 16), 16), :],
                tensor_peer(*p),
            )
        )
    both(pr, "p2_send", 1, 0)
    both(pr, "p2_fwd", 0, 1)
    both(pr, "p2_fwd", 0, 2)
    for d in (2, 1, 3):
        for r in back[d]:
            r.wait_recv()
    for h in range(4):
        rows = slice(h * 128, (h + 1) * 128)
        maxes = [mx[x, rows, :]] + [to_column(stat_in[i, h : h + 1, :]) for i in range(3)]
        most = jnp.maximum(
            jnp.maximum(maxes[0], maxes[1]), jnp.maximum(maxes[2], maxes[3])
        )
        scale = jnp.exp2(maxes[0] - most)
        over, under = acc[x, rows, :] * scale, tot[x, rows, :] * scale
        for i in range(3):
            scale = jnp.exp2(maxes[1 + i] - most) * to_column(stat_in[i, 4 + h : 5 + h, :])
            over = over + scale * part_in[i, rows, :].astype(F32)
            under = under + scale
        att[:, h * 128 : (h + 1) * 128] = (over / under).astype(BF16)

    local[8].wait()
    turns = (2, 1, 3, 0)

    def projected(dz, dc):
        cols = pl.ds(pl.multiple_of(tensor_index(dz, dc) * 1024, 1024), 1024)
        return jnp.dot(att[...], w[:, cols], preferred_element_type=F32)

    half = {}
    for dz in turns:
        bsend[dz] = projected(dz, 1).astype(BF16)
        half[dz] = wire.copy(bsend.at[dz], brecv.at[dz], mate)
    both(pr, "p1_fwd", 1)
    both(pr, "p2_send", 1, 1)
    both(pr, "p2_send", 1, 2)
    zsum = {}
    for dz in turns:
        mine = projected(dz, 0)
        half[dz].wait_recv()
        mine = mine + brecv[dz].astype(F32)
        if dz:
            bz[dz - 1] = mine.astype(BF16)
            zsum[dz] = wire.copy(bz.at[dz - 1], zrecv.at[dz - 1], tensor_peer(dz, 0))
        else:
            tacc[...] = mine
    wire.settle(early)
    both(pr, "p2_fwd", 0, 3)
    both(pr, "p1_done", 1)
    both(pr, "p2_send", 1, 3)
    for dz in (2, 1, 3):
        hz[dz].wait_recv()
        slot = mod4(zl + 4 - dz) * 2 + c
        hmate.append(wire.copy(hid.at[slot], hid.at[slot], mate))
    local[10].wait()

    for d in hmate:
        d.wait_recv()
    square = jnp.zeros((128, 384), F32)
    for i in range(8):
        h = hid[i].astype(F32)
        square = square + h * h
    inverse = lax.rsqrt(jnp.sum(square, axis=1, keepdims=True) / 3072.0 + 1e-05)
    for i in range(8):
        n = (hid[i].astype(F32) * inverse * gain[i]).astype(BF16)
        nrm[:, i * 384 : (i + 1) * 384] = n
        nrmt[i // 2, 2 * (i % 2) : 2 * (i % 2) + 2] = n.T.reshape(2, 192, 128)

    halfrows = pl.ds(2 * c, 2)

    def token_cols(pos):
        return pl.ds(pl.multiple_of(pos * 128, 128), 128)

    nxtx[:, :, token_cols(x)] = nrmt[x]
    nxty[:, :, token_cols(y)] = nrmt[:, y]
    middle = len(wire.open)
    for k in range(4):
        both(pr, "p2_fwd", 1, k)
    nx, nmate = {}, []
    for d in (2, 1, 3):
        nx["x", d] = wire.copy(
            nrmt.at[mod4(x + d), halfrows], nxtx.at[halfrows, :, token_cols(x)], {"x": mod4(x + d)}
        )
        nx["y", d] = wire.copy(
            nrmt.at[halfrows, mod4(y + d)], nxty.at[halfrows, :, token_cols(y)], {"y": mod4(y + d)}
        )
    for d in rsend:
        d.wait_recv()
    local[7].wait()
    tacc[...] = tacc[...] + res[...].astype(F32)
    wire.settle(middle)
    for j in range(2):
        for k in range(4):
            both(pr, "p2_done", j, k)
    pre = jnp.zeros((128, 1024), F32)
    for i in range(4):
        pre = pre + jnp.dot(
            nrm[:, i * 768 : (i + 1) * 768],
            pj[pl.ds(8 * i, 8)].reshape(768, 1024),
            preferred_element_type=F32,
        )
    for dz in turns[:3]:
        zsum[dz].wait_recv()
    teacher = (
        tacc[...] + zrecv[0].astype(F32) + zrecv[1].astype(F32) + zrecv[2].astype(F32)
    ).astype(BF16)
    tcb[...] = teacher
    put(tcb, teacher_out)
    mismatch = (pre - teacher.astype(F32)).astype(BF16)
    mis[...] = mismatch
    lanes = [("x", x, nxtx, "y", y), ("y", y, nxty, "x", x)] * 2
    for i, lane in enumerate(lanes):
        mch[i, lane[1]] = mismatch[:, i * 256 : (i + 1) * 256]

    def mch_at(i):
        return lambda p, h: mch.at[i, p] if h is None else mch.at[i, p, pl.ds(64 * h, 64)]

    sums = []
    for i, (axis, pos, _, other, there) in enumerate(lanes):
        ring.ring(i, mch_at(i), axis, pos)
        sums.append(
            Scatter(
                wire,
                lambda p, h, i=i: gp.at[i, p] if h is None else gp.at[i, p, h],
                near.at[i],
                far.at[i],
                other,
                there,
            )
        )

    def pass_on(i):
        ring.forward(i, mch_at(i), lanes[i][0], lanes[i][1])

    def product(i):
        ring.done(i)
        g = jnp.dot(
            lanes[i][2][...].reshape(768, 512),
            mch[i].reshape(512, 256),
            preferred_element_type=F32,
        )
        gp[i] = g.astype(BF16).reshape(4, 2, 96, 256)
        sums[i].start()

    last = {}

    def across(i):
        sums[i].finish()
        last[i] = wire.copy(gp.at[i, lanes[i][4], 1 - z], zpart.at[i], {"zh": 1 - z})

    def state_grad(dz, dc):
        rows = pj[pl.ds(4 * tensor_index(dz, dc), 4)].reshape(384, 1024)
        return lax.dot_general(
            mis[...], rows, (((1,), (1,)), ((), ())), preferred_element_type=F32
        )

    inner = jnp.zeros((128, 384), F32)

    def parts(dz, dc, mine):
        i = tensor_index(dz, dc)
        here = mine * hid[i].astype(F32)
        g1[0, pl.ds(i, 1), :] = jnp.sum(here * inverse, axis=0, keepdims=True)
        return inner + here * gain[i]

    def to_mate(dz):
        mine = state_grad(dz, 1)
        fsend[dz] = mine.astype(BF16)
        half[dz] = wire.copy(fsend.at[dz], frecv.at[dz], mate)
        return parts(dz, 1, mine)

    def along_z(dz):
        mine = state_grad(dz, 0)
        added = parts(dz, 0, mine)
        half[dz].wait_recv()
        mine = mine + frecv[dz].astype(F32)
        if dz:
            fz[dz - 1] = mine.astype(BF16)
            zsum[dz] = wire.copy(fz.at[dz - 1], fzrecv.at[dz - 1], tensor_peer(dz, 0))
        else:
            gacc[...] = mine
        return added

    for dz in turns:
        inner = to_mate(dz)
    inner = along_z(2)
    inner = along_z(1)
    for d in (2, 1, 3):
        for axis, pos, buf in (("x", x, nxtx), ("y", y, nxty)):
            nx[axis, d].wait_recv()
            came = buf.at[halfrows, :, token_cols(mod4(pos + 4 - d))]
            nmate.append(wire.copy(came, came, mate))
    pass_on(0)
    pass_on(1)
    inner = along_z(3)
    pass_on(2)
    pass_on(3)
    inner = along_z(0)
    rowbuf[0] = jnp.broadcast_to(to_row(jnp.sum(inner, axis=1, keepdims=True)), (8, 128))
    rows = [wire.copy(rowbuf.at[0], rowbuf.at[1 + i], tensor_peer(*p)) for i, p in enumerate(peers)]
    g1d = [wire.copy(g1.at[0], g1.at[d], {"x": mod4(x + d)}) for d in (1, 2, 3)]
    for d in nmate:
        d.wait_recv()
    for i in range(4):
        product(i)
    for d in g1d:
        d.wait_recv()
    g2[0] = g1[0] + g1[1] + g1[2] + g1[3]
    g2d = [wire.copy(g2.at[0], g2.at[d], {"y": mod4(y + d)}) for d in (1, 2, 3)]
    sums[0].middle()
    sums[1].middle()
    for d in g2d:
        d.wait_recv()
    whole = g2[0] + g2[1] + g2[2] + g2[3]
    for i in range(8):
        g4[i] = jnp.concatenate(
            [whole[i : i + 1, 128 * j : 128 * j + 128] for j in range(3)] + [jnp.zeros((5, 128), F32)],
            axis=0,
        )
    g4d = [
        wire.copy(g4.at[tensor_index(*p)], g5.at[i], tensor_peer(*p)) for i, p in enumerate(peers)
    ]
    sums[2].middle()
    sums[3].middle()
    across(0)
    across(1)
    across(2)
    across(3)
    total = g4[t]
    for i, d in enumerate(g4d):
        d.wait_recv()
        total = total + g5[i]
    g3[0] = total
    g3d = wire.copy(g3.at[0], g3.at[1], {"zh": 1 - z})
    for dz in turns[:3]:
        zsum[dz].wait_recv()
    grad = (
        gacc[...] + fzrecv[0].astype(F32) + fzrecv[1].astype(F32) + fzrecv[2].astype(F32)
    )
    for d in rows:
        d.wait_recv()
    total = rowbuf[0]
    for i in range(7):
        total = total + rowbuf[1 + i]
    row_inner = to_column(total[0:1, :]) / 3072.0
    sgb[...] = (
        inverse * gain[t] * grad - hid[t].astype(F32) * inverse * inverse * inverse * row_inner
    ).astype(BF16)
    put(sgb, sgrad_out)
    grad_scale = 1.0 / 64.0
    for i in range(4):
        last[i].wait_recv()
        pgb[i] = (gp[i, lanes[i][4], z].astype(F32) + zpart[i].astype(F32)) * grad_scale
        put(pgb.at[i], pgrad_out.at[:, pl.ds(256 * i, 256)])
    g3d.wait_recv()
    ggb[...] = (g3[0] + g3[1]) * grad_scale
    put(ggb, ggrad_out)
    wire.settle()
    assert (wire.send_used, wire.recv_used) == (SENDS, RECVS), (wire.send_used, wire.recv_used)
    for d in written:
        d.wait()


def hand_over(a, b, c, d, a_out, b_out, c_out, d_out):
    a_out[...] = a[...]
    b_out[...] = b[...]
    c_out[...] = c[...]
    for j in range(3):
        d_out[pl.ds(128 * j, 128)] = d[j]


def local(
    queries, keys, values, prefix_keys, prefix_values, doc_start, out_weight, residual,
    student_hidden, student_gain, proj_weight,
):
    vmem = pl.BlockSpec(memory_space=pltpu.VMEM)
    anyspace = pl.BlockSpec(memory_space=pl.ANY)
    v = pltpu.VMEM
    shapes = [
        jax.ShapeDtypeStruct((128, 1024), BF16),
        jax.ShapeDtypeStruct((128, 384), BF16),
        jax.ShapeDtypeStruct((96, 1024), F32),
    ]
    outs = pl.pallas_call(
        kernel,
        out_shape=(*shapes, jax.ShapeDtypeStruct((8, 128), F32)),
        in_specs=[anyspace] * 11,
        out_specs=(anyspace,) * 4,
        scratch_shapes=[
            v((4, 2, 4, 128, 128), BF16),
            v((32, 96, 1024), BF16),
            v((512, 8192), BF16),
            v((128, 512), BF16),
            v((4, 512, 128), BF16),
            v((3, 512, 128), BF16),
            v((3, 512, 128), BF16),
            v((3, 8, 128), F32),
            v((3, 8, 128), F32),
            v((8, 128, 384), BF16),
            v((128, 1024), BF16),
            v((4, 512, 128), F32),
            v((4, 512, 128), F32),
            v((4, 512, 128), F32),
            v((128, 512), BF16),
            v((4, 128, 1024), BF16),
            v((4, 128, 1024), BF16),
            v((3, 128, 1024), BF16),
            v((3, 128, 1024), BF16),
            v((128, 1024), F32),
            v((128, 3072), BF16),
            v((4, 4, 192, 128), BF16),
            v((4, 192, 512), BF16),
            v((4, 192, 512), BF16),
            v((128, 1024), BF16),
            v((4, 4, 128, 256), BF16),
            v((4, 128, 384), BF16),
            v((4, 128, 384), BF16),
            v((3, 128, 384), BF16),
            v((3, 128, 384), BF16),
            v((8, 8, 128), F32),
            v((128, 384), F32),
            v((4, 8, 384), F32),
            v((4, 8, 384), F32),
            v((2, 8, 128), F32),
            v((8, 8, 128), F32),
            v((7, 8, 128), F32),
            v((4, 4, 2, 96, 256), BF16),
            v((4, 2, 96, 256), BF16),
            v((4, 2, 2, 96, 256), BF16),
            v((4, 96, 256), BF16),
            v((128, 1024), BF16),
            v((128, 384), BF16),
            v((4, 96, 256), F32),
            v((8, 128), F32),
            pltpu.SMEM((1,), jnp.int32),
            v((8, 1, 384), F32),
            pltpu.SemaphoreType.DMA((SENDS,)),
            pltpu.SemaphoreType.DMA((RECVS,)),
            pltpu.SemaphoreType.DMA((18,)),
        ],
        compiler_params=pltpu.CompilerParams(
            collective_id=0, has_side_effects=True, vmem_limit_bytes=60 * 1024 * 1024
        ),
    )(
        queries, keys, values, prefix_keys, prefix_values, doc_start, out_weight, residual,
        student_hidden, student_gain.reshape(8, 1, 384), proj_weight,
    )
    return pl.pallas_call(
        hand_over,
        out_shape=(*shapes, jax.ShapeDtypeStruct((384,), F32)),
        in_specs=[vmem] * 4,
        out_specs=(vmem,) * 4,
    )(*outs)


def solution(mesh):
    finer = Mesh(mesh.devices.reshape(4, 4, 2, 4, 2), SEQ + TEN)
    rows = P(SEQ, TEN)
    return jax.shard_map(
        local,
        mesh=finer,
        in_specs=(
            rows, rows, rows, rows, rows, P(), P(TEN, None), P(SEQ + TEN, None), rows, P(), rows,
        ),
        out_specs=(rows, rows, rows, P(TEN)),
        check_vma=False,
    )
```

```python
import math

import jax
import jax.numpy as jnp
from jax import lax
from jax.experimental import pallas as pl
from jax.experimental.pallas import tpu as pltpu
from jax.sharding import Mesh
from jax.sharding import PartitionSpec as P

MESH = pl.DeviceIdType.MESH
F32 = jnp.float32
BF16 = jnp.bfloat16
NEG = -1e30
SEQ = ("x", "y", "zh")
TEN = ("zl", "c")
SENDS, RECVS = 95, 191


def mod4(v):
    return lax.rem(v, 4)


class Wire:
    def __init__(self, send, recv):
        self.send, self.recv = send, recv
        self.recv_used, self.send_used, self.spare, self.open = 0, 0, [], []

    def copy(self, src, dst, dev):
        if self.spare:
            i = self.spare.pop(0)
        else:
            i = self.send_used
            self.send_used += 1
        d = pltpu.make_async_remote_copy(
            src_ref=src,
            dst_ref=dst,
            send_sem=self.send.at[i],
            recv_sem=self.recv.at[self.recv_used],
            device_id=dev,
            device_id_type=MESH,
        )
        self.recv_used += 1
        d.start()
        self.open.append((i, d))
        return d

    def settle(self, count=None):
        count = len(self.open) if count is None else count
        for i, d in self.open[:count]:
            d.wait_send()
            self.spare.append(i)
        self.open = self.open[count:]


class Gather:
    def __init__(self, wire, at, first, second, coord):
        self.wire, self.at, self.first, self.second = wire, at, first, second
        self.a, self.b, self.z = coord[first], coord[second], coord["zh"]
        self.r, self.l, self.hr, self.hl = {}, {}, {}, {}
        a = self.a
        self.order = (a, mod4(a + 3), mod4(a + 1), mod4(a + 2))

    def z_send(self):
        own = self.at(self.a, self.b, self.z, 1, None)
        self.zd = self.wire.copy(own, own, {"zh": 1 - self.z})

    def z_wait(self):
        self.zd.wait_recv()

    def ring(self, key, ref_of, axis, pos):
        own = ref_of(pos, None)
        self.r[key] = self.wire.copy(own, own, {axis: mod4(pos + 1)})
        self.l[key] = self.wire.copy(own, own, {axis: mod4(pos + 3)})

    def forward(self, key, ref_of, axis, pos):
        self.r[key].wait_recv()
        left = ref_of(mod4(pos + 3), 0)
        self.hr[key] = self.wire.copy(left, left, {axis: mod4(pos + 1)})
        self.l[key].wait_recv()
        right = ref_of(mod4(pos + 1), 1)
        self.hl[key] = self.wire.copy(right, right, {axis: mod4(pos + 3)})

    def done(self, key):
        self.hr[key].wait_recv()
        self.hl[key].wait_recv()

    def one(self, j):
        zq = self.z if j == 0 else 1 - self.z
        return lambda pos, half: self.at(pos, self.b, zq, 1, half)

    def two(self, j, k):
        aq = self.order[k]
        if j is None:
            return lambda pos, half: self.at(aq, pos, 0, 2, half)
        zq = self.z if j == 0 else 1 - self.z
        return lambda pos, half: self.at(aq, pos, zq, 1, half)

    def p1_send(self, j):
        self.ring(("1", j), self.one(j), self.first, self.a)

    def p1_fwd(self, j):
        self.forward(("1", j), self.one(j), self.first, self.a)

    def p1_done(self, j):
        self.done(("1", j))

    def p2_send(self, j, k):
        self.ring(("2", j, k), self.two(j, k), self.second, self.b)

    def p2_fwd(self, j, k):
        self.forward(("2", j, k), self.two(j, k), self.second, self.b)

    def p2_done(self, j, k):
        self.done(("2", j, k))


class Scatter:
    def __init__(self, wire, part, near, far, axis, pos):
        self.wire, self.part, self.near, self.far = wire, part, near, far
        self.axis, self.pos = axis, pos

    def start(self):
        p, ax = self.pos, self.axis
        opp = mod4(p + 2)
        self.r1 = self.wire.copy(self.part(opp, 0), self.near.at[0], {ax: mod4(p + 1)})
        self.l1 = self.wire.copy(self.part(opp, 1), self.near.at[1], {ax: mod4(p + 3)})

    def middle(self):
        p, ax = self.pos, self.axis
        right, left = mod4(p + 1), mod4(p + 3)
        self.r1.wait_recv()
        ref = self.part(right, 0)
        ref[...] = (ref[...].astype(F32) + self.near[0].astype(F32)).astype(BF16)
        self.r2 = self.wire.copy(self.part(right, None), self.far.at[0], {ax: right})
        self.l1.wait_recv()
        ref = self.part(left, 1)
        ref[...] = (ref[...].astype(F32) + self.near[1].astype(F32)).astype(BF16)
        self.l2 = self.wire.copy(self.part(left, None), self.far.at[1], {ax: left})

    def finish(self):
        self.r2.wait_recv()
        self.l2.wait_recv()
        ref = self.part(self.pos, None)
        ref[...] = (
            ref[...].astype(F32) + self.far[0].astype(F32) + self.far[1].astype(F32)
        ).astype(BF16)


def kernel(
    q_hbm, k_hbm, v_hbm, pk_hbm, pv_hbm, doc_hbm, w_hbm, res_hbm, hid_hbm, gain_hbm, proj_hbm,
    teacher_out, sgrad_out, pgrad_out, ggrad_out,
    kvb, pj, w, q, qs, part_of, part_in, stat_of, stat_in, hid, res, mx, tot, acc, att,
    bsend, brecv, bz, zrecv, tacc, nrm, nrmt, nxtx, nxty, mis, mch,
    fsend, frecv, fz, fzrecv, facc, glocal, g1, g2, g3, g4, g5,
    gp, near, far, zpart, tcb, sgb, pgb, ggb, doc, gain,
    ssem, rsem, lsem,
):
    x, y, z = lax.axis_index("x"), lax.axis_index("y"), lax.axis_index("zh")
    zl, c = lax.axis_index("zl"), lax.axis_index("c")
    coord = {"x": x, "y": y, "zh": z}
    seq = (x * 4 + y) * 2 + z
    t = zl * 2 + c
    wire = Wire(ssem, rsem)
    mate = {"c": 1 - c}

    def tensor_peer(dz, dc):
        return {"zl": mod4(zl + dz), "c": c if dc == 0 else 1 - c}

    def tensor_index(dz, dc):
        return mod4(zl + dz) * 2 + (c if dc == 0 else 1 - c)

    peers = [(dz, dc) for dz in (2, 1, 3, 0) for dc in (0, 1) if (dz, dc) != (0, 0)]

    loads = [
        (pk_hbm, kvb.at[y, z, 0]),
        (pv_hbm, kvb.at[y, z, 1]),
        (k_hbm, kvb.at[y, z, 2]),
        (v_hbm, kvb.at[y, z, 3]),
        (proj_hbm, pj.at[seq]),
        (hid_hbm, hid.at[t]),
        (q_hbm, q),
        (
            res_hbm.at[:, pl.ds(pl.multiple_of(t * 1024, 1024), 1024)],
            res.at[pl.ds(pl.multiple_of(t * 16, 16), 16), :],
        ),
        (w_hbm, w),
        (doc_hbm, doc),
        (gain_hbm, gain),
    ]
    local = [pltpu.make_async_copy(s, d, lsem.at[i]) for i, (s, d) in enumerate(loads)]
    for d in local:
        d.start()

    written = []

    def put(src, dst):
        d = pltpu.make_async_copy(src, dst, lsem.at[len(loads) + len(written)])
        d.start()
        written.append(d)

    barrier = pltpu.get_barrier_semaphore()
    greet = [
        {"x": mod4(x + 1)}, {"x": mod4(x + 2)}, {"x": mod4(x + 3)},
        {"y": mod4(y + 1)}, {"y": mod4(y + 2)}, {"y": mod4(y + 3)},
        {"zh": 1 - z},
    ] + [tensor_peer(*p) for p in peers]
    for dev in greet:
        pl.semaphore_signal(barrier, inc=1, device_id=dev, device_id_type=MESH)
    pl.semaphore_wait(barrier, len(greet))

    def kv_at(a, b, zq, count, half):
        return kvb.at[a, zq] if half is None else kvb.at[a, zq, pl.ds(2 * half, 2)]

    def q_at(pos, half):
        return qs.at[pos] if half is None else qs.at[pos, pl.ds(256 * half, 256)]

    def pj_at(low, x_first):
        def at(a, b, zq, count, half):
            slot = ((a * 4 + b) if x_first else (b * 4 + a)) * 2 + zq
            where = slot if count == 1 else pl.ds(slot, 2)
            cols = pl.ds(0, 1024) if half is None else pl.ds(512 * half, 512)
            return pj.at[where, pl.ds(low, 48), cols]

        return at

    kv = Gather(wire, kv_at, "y", "x", coord)
    ring = Gather(wire, None, "x", "y", coord)
    pr = (
        Gather(wire, pj_at(0, True), "x", "y", coord),
        Gather(wire, pj_at(48, False), "y", "x", coord),
    )

    def both(streams, name, *args):
        for s in streams:
            getattr(s, name)(*args)

    factor = 128 ** (-0.5) * math.log2(math.e)
    column = lax.broadcasted_iota(jnp.int32, (512, 512), 1)
    position = x * 1024 + (column // 128) * 256 + lax.rem(column, 128)
    token = lax.rem(lax.broadcasted_iota(jnp.int32, (512, 512), 0), 128) + (y * 2 + z) * 128
    diagonal = lax.broadcasted_iota(jnp.int32, (128, 128), 0) == lax.broadcasted_iota(
        jnp.int32, (128, 128), 1
    )

    def wide(v):
        return jnp.concatenate([v] * 4, axis=1)

    def block(xq, kb, vb, visible):
        s = lax.dot_general(
            qs[xq], kb.reshape(512, 128), (((1,), (1,)), ((), ())), preferred_element_type=F32
        ) * factor
        s = jnp.where(visible, s, NEG)
        old = mx[xq]
        new = jnp.maximum(old, jnp.broadcast_to(jnp.max(s, axis=1, keepdims=True), (512, 128)))
        p = jnp.exp2(s - wide(new))
        scale = jnp.exp2(old - new)
        mx[xq] = new
        tot[xq] = tot[xq] * scale + jnp.broadcast_to(
            jnp.sum(p, axis=1, keepdims=True), (512, 128)
        )
        acc[xq] = acc[xq] * scale + jnp.dot(
            p.astype(BF16), vb.reshape(512, 128), preferred_element_type=F32
        )

    def attend(j, xq):
        zq = z if j == 0 else 1 - z
        here = position + zq * 128
        block(xq, kvb[:, zq, 0], kvb[:, zq, 1], here >= doc[0])
        block(xq, kvb[:, zq, 2], kvb[:, zq, 3], here <= token + xq * 1024)

    def to_row(v):
        return jnp.sum(jnp.where(diagonal, v, 0.0), axis=0, keepdims=True)

    def to_column(v):
        wide_row = jnp.broadcast_to(v, (128, 128))
        return jnp.sum(jnp.where(diagonal, wide_row, 0.0), axis=1, keepdims=True)

    back = {}

    def give_back(d):
        xq = mod4(x + d)
        part_of[d - 1] = (acc[xq] / tot[xq]).astype(BF16)
        stat_of[d - 1] = jnp.concatenate(
            [to_row(r[xq, h * 128 : (h + 1) * 128, :]) for r in (mx, tot) for h in range(4)],
            axis=0,
        )
        back[d] = (
            wire.copy(part_of.at[d - 1], part_in.at[d - 1], {"x": xq}),
            wire.copy(stat_of.at[d - 1], stat_in.at[d - 1], {"x": xq}),
        )

    local[6].wait()
    for h in range(4):
        qs[x, h * 128 : (h + 1) * 128, :] = q[:, h * 128 : (h + 1) * 128]
    for d in local[:4]:
        d.wait()
    kv.z_send()
    kv.p1_send(0)
    ring.ring("q", q_at, "x", x)
    for i in range(4):
        mx[i] = jnp.full((512, 128), NEG, F32)
        tot[i] = jnp.zeros((512, 128), F32)
        acc[i] = jnp.zeros((512, 128), F32)
    local[4].wait()
    ring.forward("q", q_at, "x", x)
    kv.p1_fwd(0)
    both(pr, "p1_send", 0)
    pr[1].p2_send(0, 0)
    both(pr, "z_send")
    kv.z_wait()
    kv.p1_send(1)
    ring.done("q")
    kv.p1_done(0)
    local[9].wait()
    attend(0, mod4(x + 2))
    both(pr, "p1_fwd", 0)
    pr[1].p2_send(0, 1)
    pr[1].p2_send(0, 2)
    attend(0, mod4(x + 1))
    kv.p1_fwd(1)
    for k in range(3):
        pr[0].p2_send(0, k)
    attend(0, mod4(x + 3))
    both(pr, "p1_done", 0)
    pr[0].p2_send(0, 3)
    attend(0, x)
    kv.p1_done(1)
    local[5].wait()
    hz = {dz: wire.copy(hid.at[t], hid.at[t], tensor_peer(dz, 0)) for dz in (2, 1, 3)}
    hmate = [wire.copy(hid.at[t], hid.at[t], mate)]
    early = len(wire.open)
    attend(1, mod4(x + 2))
    give_back(2)
    attend(1, mod4(x + 1))
    give_back(1)
    attend(1, mod4(x + 3))
    give_back(3)
    pr[1].p2_send(0, 3)
    both(pr, "z_wait")
    both(pr, "p1_send", 1)
    both(pr, "p2_fwd", 0, 0)
    attend(1, x)
    rsend = []
    for p in peers:
        cols = pl.ds(pl.multiple_of(tensor_index(*p) * 1024, 1024), 1024)
        rsend.append(
            wire.copy(
                res_hbm.at[:, cols],
                res.at[pl.ds(pl.multiple_of(t * 16, 16), 16), :],
                tensor_peer(*p),
            )
        )
    both(pr, "p2_send", 1, 0)
    both(pr, "p2_fwd", 0, 1)
    both(pr, "p2_fwd", 0, 2)
    for d in (2, 1, 3):
        for r in back[d]:
            r.wait_recv()
    for h in range(4):
        rows = slice(h * 128, (h + 1) * 128)
        maxes = [mx[x, rows, :]] + [to_column(stat_in[i, h : h + 1, :]) for i in range(3)]
        most = jnp.maximum(
            jnp.maximum(maxes[0], maxes[1]), jnp.maximum(maxes[2], maxes[3])
        )
        scale = jnp.exp2(maxes[0] - most)
        over, under = acc[x, rows, :] * scale, tot[x, rows, :] * scale
        for i in range(3):
            scale = jnp.exp2(maxes[1 + i] - most) * to_column(stat_in[i, 4 + h : 5 + h, :])
            over = over + scale * part_in[i, rows, :].astype(F32)
            under = under + scale
        att[:, h * 128 : (h + 1) * 128] = (over / under).astype(BF16)

    local[8].wait()
    turns = (2, 1, 3, 0)

    def projected(dz, dc):
        cols = pl.ds(pl.multiple_of(tensor_index(dz, dc) * 1024, 1024), 1024)
        return jnp.dot(att[...], w[:, cols], preferred_element_type=F32)

    half = {}
    for dz in turns:
        bsend[dz] = projected(dz, 1).astype(BF16)
        half[dz] = wire.copy(bsend.at[dz], brecv.at[dz], mate)
    both(pr, "p1_fwd", 1)
    both(pr, "p2_send", 1, 1)
    both(pr, "p2_send", 1, 2)
    zsum = {}
    for dz in turns:
        mine = projected(dz, 0)
        half[dz].wait_recv()
        mine = mine + brecv[dz].astype(F32)
        if dz:
            bz[dz - 1] = mine.astype(BF16)
            zsum[dz] = wire.copy(bz.at[dz - 1], zrecv.at[dz - 1], tensor_peer(dz, 0))
        else:
            tacc[...] = mine
    wire.settle(early)
    both(pr, "p2_fwd", 0, 3)
    both(pr, "p1_done", 1)
    both(pr, "p2_send", 1, 3)
    for dz in (2, 1, 3):
        hz[dz].wait_recv()
        slot = mod4(zl + 4 - dz) * 2 + c
        hmate.append(wire.copy(hid.at[slot], hid.at[slot], mate))
    local[10].wait()

    for d in hmate:
        d.wait_recv()
    square = jnp.zeros((128, 384), F32)
    for i in range(8):
        h = hid[i].astype(F32)
        square = square + h * h
    inverse = lax.rsqrt(jnp.sum(square, axis=1, keepdims=True) / 3072.0 + 1e-05)
    for i in range(8):
        n = (hid[i].astype(F32) * inverse * gain[i]).astype(BF16)
        nrm[:, i * 384 : (i + 1) * 384] = n
        nrmt[i // 2, 2 * (i % 2) : 2 * (i % 2) + 2] = n.T.reshape(2, 192, 128)

    halfrows = pl.ds(2 * c, 2)

    def token_cols(pos):
        return pl.ds(pl.multiple_of(pos * 128, 128), 128)

    nxtx[:, :, token_cols(x)] = nrmt[x]
    nxty[:, :, token_cols(y)] = nrmt[:, y]
    middle = len(wire.open)
    for k in range(4):
        both(pr, "p2_fwd", 1, k)
    nx, nmate = {}, []
    for d in (2, 1, 3):
        nx["x", d] = wire.copy(
            nrmt.at[mod4(x + d), halfrows], nxtx.at[halfrows, :, token_cols(x)], {"x": mod4(x + d)}
        )
        nx["y", d] = wire.copy(
            nrmt.at[halfrows, mod4(y + d)], nxty.at[halfrows, :, token_cols(y)], {"y": mod4(y + d)}
        )
    for d in rsend:
        d.wait_recv()
    local[7].wait()
    tacc[...] = tacc[...] + res[...].astype(F32)
    wire.settle(middle)
    for j in range(2):
        for k in range(4):
            both(pr, "p2_done", j, k)
    pre = jnp.zeros((128, 1024), F32)
    for i in range(4):
        pre = pre + jnp.dot(
            nrm[:, i * 768 : (i + 1) * 768],
            pj[pl.ds(8 * i, 8)].reshape(768, 1024),
            preferred_element_type=F32,
        )
    for dz in turns[:3]:
        zsum[dz].wait_recv()
    teacher = (
        tacc[...] + zrecv[0].astype(F32) + zrecv[1].astype(F32) + zrecv[2].astype(F32)
    ).astype(BF16)
    tcb[...] = teacher
    put(tcb, teacher_out)
    mismatch = (pre - teacher.astype(F32)).astype(BF16)
    mis[...] = mismatch
    lanes = [("x", x, nxtx, "y", y), ("y", y, nxty, "x", x)] * 2
    for i, lane in enumerate(lanes):
        mch[i, lane[1]] = mismatch[:, i * 256 : (i + 1) * 256]

    def mch_at(i):
        return lambda p, h: mch.at[i, p] if h is None else mch.at[i, p, pl.ds(64 * h, 64)]

    sums = []
    for i, (axis, pos, _, other, there) in enumerate(lanes):
        ring.ring(i, mch_at(i), axis, pos)
        sums.append(
            Scatter(
                wire,
                lambda p, h, i=i: gp.at[i, p] if h is None else gp.at[i, p, h],
                near.at[i],
                far.at[i],
                other,
                there,
            )
        )

    def pass_on(i):
        ring.forward(i, mch_at(i), lanes[i][0], lanes[i][1])

    def product(i):
        ring.done(i)
        g = jnp.dot(
            lanes[i][2][...].reshape(768, 512),
            mch[i].reshape(512, 256),
            preferred_element_type=F32,
        )
        gp[i] = g.astype(BF16).reshape(4, 2, 96, 256)
        sums[i].start()

    last = {}

    def across(i):
        sums[i].finish()
        last[i] = wire.copy(gp.at[i, lanes[i][4], 1 - z], zpart.at[i], {"zh": 1 - z})

    def state_grad(dz, dc):
        rows = pj[pl.ds(4 * tensor_index(dz, dc), 4)].reshape(384, 1024)
        return lax.dot_general(
            mis[...], rows, (((1,), (1,)), ((), ())), preferred_element_type=F32
        )

    inner = jnp.zeros((128, 384), F32)

    def parts(dz, dc, mine):
        i = tensor_index(dz, dc)
        here = mine * hid[i].astype(F32)
        glocal[pl.ds(i, 1), :] = jnp.sum(here * inverse, axis=0, keepdims=True)
        return inner + here * gain[i]

    def to_mate(dz):
        mine = state_grad(dz, 1)
        fsend[dz] = mine.astype(BF16)
        half[dz] = wire.copy(fsend.at[dz], frecv.at[dz], mate)
        return parts(dz, 1, mine)

    def own_part(dz):
        mine = state_grad(dz, 0)
        facc[dz] = mine
        return parts(dz, 0, mine)

    def along_z(dz):
        half[dz].wait_recv()
        facc[dz] = facc[dz] + frecv[dz].astype(F32)
        if dz:
            fz[dz - 1] = facc[dz].astype(BF16)
            zsum[dz] = wire.copy(fz.at[dz - 1], fzrecv.at[dz - 1], tensor_peer(dz, 0))

    for dz in turns:
        inner = to_mate(dz)
    for dz in turns:
        inner = own_part(dz)
    as_row = to_row(jnp.sum(inner, axis=1, keepdims=True))
    whole = glocal[...]
    for i in range(8):
        g4[i] = jnp.concatenate(
            [whole[i : i + 1, 128 * j : 128 * j + 128] for j in range(3)]
            + [as_row, jnp.zeros((4, 128), F32)],
            axis=0,
        )
    g4d = [
        wire.copy(g4.at[tensor_index(*p)], g5.at[i], tensor_peer(*p)) for i, p in enumerate(peers)
    ]
    pass_on(0)
    pass_on(1)
    for dz in turns:
        along_z(dz)
    pass_on(2)
    pass_on(3)
    for d in (2, 1, 3):
        for axis, pos, buf in (("x", x, nxtx), ("y", y, nxty)):
            nx[axis, d].wait_recv()
            came = buf.at[halfrows, :, token_cols(mod4(pos + 4 - d))]
            nmate.append(wire.copy(came, came, mate))
    total = g4[t]
    for i, d in enumerate(g4d):
        d.wait_recv()
        total = total + g5[i]
    g1[0] = total
    row_inner = to_column(total[3:4, :]) / 3072.0
    g1d = [wire.copy(g1.at[0], g1.at[d], {"x": mod4(x + d)}) for d in (1, 2, 3)]
    for d in nmate:
        d.wait_recv()
    for i in range(4):
        product(i)
    for d in g1d:
        d.wait_recv()
    g2[0] = g1[0] + g1[1] + g1[2] + g1[3]
    g2d = [wire.copy(g2.at[0], g2.at[d], {"y": mod4(y + d)}) for d in (1, 2, 3)]
    sums[0].middle()
    sums[1].middle()
    for d in g2d:
        d.wait_recv()
    g3[0] = g2[0] + g2[1] + g2[2] + g2[3]
    g3d = wire.copy(g3.at[0], g3.at[1], {"zh": 1 - z})
    sums[2].middle()
    sums[3].middle()
    across(0)
    across(1)
    across(2)
    across(3)
    for dz in turns[:3]:
        zsum[dz].wait_recv()
    grad = (
        facc[0] + fzrecv[0].astype(F32) + fzrecv[1].astype(F32) + fzrecv[2].astype(F32)
    )
    sgb[...] = (
        inverse * gain[t] * grad - hid[t].astype(F32) * inverse * inverse * inverse * row_inner
    ).astype(BF16)
    put(sgb, sgrad_out)
    grad_scale = 1.0 / 64.0
    for i in range(4):
        last[i].wait_recv()
        pgb[i] = (gp[i, lanes[i][4], z].astype(F32) + zpart[i].astype(F32)) * grad_scale
        put(pgb.at[i], pgrad_out.at[:, pl.ds(256 * i, 256)])
    g3d.wait_recv()
    ggb[...] = (g3[0] + g3[1]) * grad_scale
    put(ggb, ggrad_out)
    wire.settle()
    assert (wire.send_used, wire.recv_used) == (SENDS, RECVS), (wire.send_used, wire.recv_used)
    for d in written:
        d.wait()


def hand_over(a, b, c, d, a_out, b_out, c_out, d_out):
    a_out[...] = a[...]
    b_out[...] = b[...]
    c_out[...] = c[...]
    for j in range(3):
        d_out[pl.ds(128 * j, 128)] = d[j]


def local(
    queries, keys, values, prefix_keys, prefix_values, doc_start, out_weight, residual,
    student_hidden, student_gain, proj_weight,
):
    vmem = pl.BlockSpec(memory_space=pltpu.VMEM)
    anyspace = pl.BlockSpec(memory_space=pl.ANY)
    v = pltpu.VMEM
    shapes = [
        jax.ShapeDtypeStruct((128, 1024), BF16),
        jax.ShapeDtypeStruct((128, 384), BF16),
        jax.ShapeDtypeStruct((96, 1024), F32),
    ]
    outs = pl.pallas_call(
        kernel,
        out_shape=(*shapes, jax.ShapeDtypeStruct((8, 128), F32)),
        in_specs=[anyspace] * 11,
        out_specs=(anyspace,) * 4,
        scratch_shapes=[
            v((4, 2, 4, 128, 128), BF16),
            v((32, 96, 1024), BF16),
            v((512, 8192), BF16),
            v((128, 512), BF16),
            v((4, 512, 128), BF16),
            v((3, 512, 128), BF16),
            v((3, 512, 128), BF16),
            v((3, 8, 128), F32),
            v((3, 8, 128), F32),
            v((8, 128, 384), BF16),
            v((128, 1024), BF16),
            v((4, 512, 128), F32),
            v((4, 512, 128), F32),
            v((4, 512, 128), F32),
            v((128, 512), BF16),
            v((4, 128, 1024), BF16),
            v((4, 128, 1024), BF16),
            v((3, 128, 1024), BF16),
            v((3, 128, 1024), BF16),
            v((128, 1024), F32),
            v((128, 3072), BF16),
            v((4, 4, 192, 128), BF16),
            v((4, 192, 512), BF16),
            v((4, 192, 512), BF16),
            v((128, 1024), BF16),
            v((4, 4, 128, 256), BF16),
            v((4, 128, 384), BF16),
            v((4, 128, 384), BF16),
            v((3, 128, 384), BF16),
            v((3, 128, 384), BF16),
            v((4, 128, 384), F32),
            v((8, 384), F32),
            v((4, 8, 128), F32),
            v((4, 8, 128), F32),
            v((2, 8, 128), F32),
            v((8, 8, 128), F32),
            v((7, 8, 128), F32),
            v((4, 4, 2, 96, 256), BF16),
            v((4, 2, 96, 256), BF16),
            v((4, 2, 2, 96, 256), BF16),
            v((4, 96, 256), BF16),
            v((128, 1024), BF16),
            v((128, 384), BF16),
            v((4, 96, 256), F32),
            v((8, 128), F32),
            pltpu.SMEM((1,), jnp.int32),
            v((8, 1, 384), F32),
            pltpu.SemaphoreType.DMA((SENDS,)),
            pltpu.SemaphoreType.DMA((RECVS,)),
            pltpu.SemaphoreType.DMA((18,)),
        ],
        compiler_params=pltpu.CompilerParams(
            collective_id=0, has_side_effects=True, vmem_limit_bytes=60 * 1024 * 1024
        ),
    )(
        queries, keys, values, prefix_keys, prefix_values, doc_start, out_weight, residual,
        student_hidden, student_gain.reshape(8, 1, 384), proj_weight,
    )
    return pl.pallas_call(
        hand_over,
        out_shape=(*shapes, jax.ShapeDtypeStruct((384,), F32)),
        in_specs=[vmem] * 4,
        out_specs=(vmem,) * 4,
    )(*outs)


def solution(mesh):
    finer = Mesh(mesh.devices.reshape(4, 4, 2, 4, 2), SEQ + TEN)
    rows = P(SEQ, TEN)
    return jax.shard_map(
        local,
        mesh=finer,
        in_specs=(
            rows, rows, rows, rows, rows, P(), P(TEN, None), P(SEQ + TEN, None), rows, P(), rows,
        ),
        out_specs=(rows, rows, rows, P(TEN)),
        check_vma=False,
    )
```

```python
import math

import jax
import jax.numpy as jnp
from jax import lax
from jax.experimental import pallas as pl
from jax.experimental.pallas import tpu as pltpu
from jax.sharding import Mesh
from jax.sharding import PartitionSpec as P

MESH = pl.DeviceIdType.MESH
F32 = jnp.float32
BF16 = jnp.bfloat16
NEG = -1e30
SEQ = ("x", "y", "zh")
TEN = ("zl", "c")
SENDS, RECVS = 95, 191


def mod4(v):
    return lax.rem(v, 4)


class Wire:
    def __init__(self, send, recv):
        self.send, self.recv = send, recv
        self.recv_used, self.send_used, self.spare, self.open = 0, 0, [], []

    def copy(self, src, dst, dev):
        if self.spare:
            i = self.spare.pop(0)
        else:
            i = self.send_used
            self.send_used += 1
        d = pltpu.make_async_remote_copy(
            src_ref=src,
            dst_ref=dst,
            send_sem=self.send.at[i],
            recv_sem=self.recv.at[self.recv_used],
            device_id=dev,
            device_id_type=MESH,
        )
        self.recv_used += 1
        d.start()
        self.open.append((i, d))
        return d

    def settle(self, count=None):
        count = len(self.open) if count is None else count
        for i, d in self.open[:count]:
            d.wait_send()
            self.spare.append(i)
        self.open = self.open[count:]


class Gather:
    def __init__(self, wire, at, first, second, coord):
        self.wire, self.at, self.first, self.second = wire, at, first, second
        self.a, self.b, self.z = coord[first], coord[second], coord["zh"]
        self.r, self.l, self.hr, self.hl = {}, {}, {}, {}
        a = self.a
        self.order = (a, mod4(a + 3), mod4(a + 1), mod4(a + 2))

    def z_send(self):
        own = self.at(self.a, self.b, self.z, 1, None)
        self.zd = self.wire.copy(own, own, {"zh": 1 - self.z})

    def z_wait(self):
        self.zd.wait_recv()

    def ring(self, key, ref_of, axis, pos):
        own = ref_of(pos, None)
        self.r[key] = self.wire.copy(own, own, {axis: mod4(pos + 1)})
        self.l[key] = self.wire.copy(own, own, {axis: mod4(pos + 3)})

    def forward(self, key, ref_of, axis, pos):
        self.r[key].wait_recv()
        left = ref_of(mod4(pos + 3), 0)
        self.hr[key] = self.wire.copy(left, left, {axis: mod4(pos + 1)})
        self.l[key].wait_recv()
        right = ref_of(mod4(pos + 1), 1)
        self.hl[key] = self.wire.copy(right, right, {axis: mod4(pos + 3)})

    def done(self, key):
        self.hr[key].wait_recv()
        self.hl[key].wait_recv()

    def one(self, j):
        zq = self.z if j == 0 else 1 - self.z
        return lambda pos, half: self.at(pos, self.b, zq, 1, half)

    def two(self, j, k):
        aq = self.order[k]
        if j is None:
            return lambda pos, half: self.at(aq, pos, 0, 2, half)
        zq = self.z if j == 0 else 1 - self.z
        return lambda pos, half: self.at(aq, pos, zq, 1, half)

    def p1_send(self, j):
        self.ring(("1", j), self.one(j), self.first, self.a)

    def p1_fwd(self, j):
        self.forward(("1", j), self.one(j), self.first, self.a)

    def p1_done(self, j):
        self.done(("1", j))

    def p2_send(self, j, k):
        self.ring(("2", j, k), self.two(j, k), self.second, self.b)

    def p2_fwd(self, j, k):
        self.forward(("2", j, k), self.two(j, k), self.second, self.b)

    def p2_done(self, j, k):
        self.done(("2", j, k))


class Scatter:
    def __init__(self, wire, part, near, far, axis, pos):
        self.wire, self.part, self.near, self.far = wire, part, near, far
        self.axis, self.pos = axis, pos

    def start(self):
        p, ax = self.pos, self.axis
        opp = mod4(p + 2)
        self.r1 = self.wire.copy(self.part(opp, 0), self.near.at[0], {ax: mod4(p + 1)})
        self.l1 = self.wire.copy(self.part(opp, 1), self.near.at[1], {ax: mod4(p + 3)})

    def middle(self):
        p, ax = self.pos, self.axis
        right, left = mod4(p + 1), mod4(p + 3)
        self.r1.wait_recv()
        ref = self.part(right, 0)
        ref[...] = (ref[...].astype(F32) + self.near[0].astype(F32)).astype(BF16)
        self.r2 = self.wire.copy(self.part(right, None), self.far.at[0], {ax: right})
        self.l1.wait_recv()
        ref = self.part(left, 1)
        ref[...] = (ref[...].astype(F32) + self.near[1].astype(F32)).astype(BF16)
        self.l2 = self.wire.copy(self.part(left, None), self.far.at[1], {ax: left})

    def finish(self):
        self.r2.wait_recv()
        self.l2.wait_recv()
        ref = self.part(self.pos, None)
        ref[...] = (
            ref[...].astype(F32) + self.far[0].astype(F32) + self.far[1].astype(F32)
        ).astype(BF16)


def kernel(
    q_hbm, k_hbm, v_hbm, pk_hbm, pv_hbm, doc_hbm, w_hbm, res_hbm, hid_hbm, gain_hbm, proj_hbm,
    teacher_out, sgrad_out, pgrad_out, ggrad_out,
    kvb, pj, w, q, qs, part_of, part_in, stat_of, stat_in, hid, res, mx, tot, acc, att,
    bsend, brecv, bz, zrecv, tacc, nrm, nrmt, nxtx, nxty, mis, mch,
    fsend, frecv, fz, fzrecv, facc, glocal, g1, g2, g3, g4, g5,
    gp, near, far, zpart, tcb, sgb, pgb, ggb, doc, gain,
    ssem, rsem, lsem,
):
    x, y, z = lax.axis_index("x"), lax.axis_index("y"), lax.axis_index("zh")
    zl, c = lax.axis_index("zl"), lax.axis_index("c")
    coord = {"x": x, "y": y, "zh": z}
    seq = (x * 4 + y) * 2 + z
    t = zl * 2 + c
    wire = Wire(ssem, rsem)
    mate = {"c": 1 - c}

    def tensor_peer(dz, dc):
        return {"zl": mod4(zl + dz), "c": c if dc == 0 else 1 - c}

    def tensor_index(dz, dc):
        return mod4(zl + dz) * 2 + (c if dc == 0 else 1 - c)

    peers = [(dz, dc) for dz in (2, 1, 3, 0) for dc in (0, 1) if (dz, dc) != (0, 0)]

    loads = [
        (pk_hbm, kvb.at[y, z, 0]),
        (pv_hbm, kvb.at[y, z, 1]),
        (k_hbm, kvb.at[y, z, 2]),
        (v_hbm, kvb.at[y, z, 3]),
        (proj_hbm, pj.at[seq]),
        (hid_hbm, hid.at[t]),
        (q_hbm, q),
        (
            res_hbm.at[:, pl.ds(pl.multiple_of(t * 1024, 1024), 1024)],
            res.at[pl.ds(pl.multiple_of(t * 16, 16), 16), :],
        ),
        (w_hbm, w),
        (doc_hbm, doc),
        (gain_hbm, gain),
    ]
    local = [pltpu.make_async_copy(s, d, lsem.at[i]) for i, (s, d) in enumerate(loads)]
    for d in local:
        d.start()

    written = []

    def put(src, dst):
        d = pltpu.make_async_copy(src, dst, lsem.at[len(loads) + len(written)])
        d.start()
        written.append(d)

    barrier = pltpu.get_barrier_semaphore()
    greet = [
        {"x": mod4(x + 1)}, {"x": mod4(x + 2)}, {"x": mod4(x + 3)},
        {"y": mod4(y + 1)}, {"y": mod4(y + 2)}, {"y": mod4(y + 3)},
        {"zh": 1 - z},
    ] + [tensor_peer(*p) for p in peers]
    for dev in greet:
        pl.semaphore_signal(barrier, inc=1, device_id=dev, device_id_type=MESH)
    pl.semaphore_wait(barrier, len(greet))

    def kv_at(a, b, zq, count, half):
        return kvb.at[a, zq] if half is None else kvb.at[a, zq, pl.ds(2 * half, 2)]

    def q_at(pos, half):
        return qs.at[pos] if half is None else qs.at[pos, pl.ds(256 * half, 256)]

    def pj_at(low, x_first):
        def at(a, b, zq, count, half):
            slot = ((a * 4 + b) if x_first else (b * 4 + a)) * 2 + zq
            where = slot if count == 1 else pl.ds(slot, 2)
            cols = pl.ds(0, 1024) if half is None else pl.ds(512 * half, 512)
            return pj.at[where, pl.ds(low, 48), cols]

        return at

    kv = Gather(wire, kv_at, "y", "x", coord)
    ring = Gather(wire, None, "x", "y", coord)
    pr = (
        Gather(wire, pj_at(0, True), "x", "y", coord),
        Gather(wire, pj_at(48, False), "y", "x", coord),
    )

    def both(streams, name, *args):
        for s in streams:
            getattr(s, name)(*args)

    factor = 128 ** (-0.5) * math.log2(math.e)
    column = lax.broadcasted_iota(jnp.int32, (512, 512), 1)
    position = x * 1024 + (column // 128) * 256 + lax.rem(column, 128)
    token = lax.rem(lax.broadcasted_iota(jnp.int32, (512, 512), 0), 128) + (y * 2 + z) * 128
    diagonal = lax.broadcasted_iota(jnp.int32, (128, 128), 0) == lax.broadcasted_iota(
        jnp.int32, (128, 128), 1
    )

    def wide(v):
        return jnp.concatenate([v] * 4, axis=1)

    def block(xq, kb, vb, visible):
        s = lax.dot_general(
            qs[xq], kb.reshape(512, 128), (((1,), (1,)), ((), ())), preferred_element_type=F32
        ) * factor
        s = jnp.where(visible, s, NEG)
        old = mx[xq]
        new = jnp.maximum(old, jnp.broadcast_to(jnp.max(s, axis=1, keepdims=True), (512, 128)))
        p = jnp.exp2(s - wide(new))
        scale = jnp.exp2(old - new)
        mx[xq] = new
        tot[xq] = tot[xq] * scale + jnp.broadcast_to(
            jnp.sum(p, axis=1, keepdims=True), (512, 128)
        )
        acc[xq] = acc[xq] * scale + jnp.dot(
            p.astype(BF16), vb.reshape(512, 128), preferred_element_type=F32
        )

    def attend(j, xq):
        zq = z if j == 0 else 1 - z
        here = position + zq * 128
        block(xq, kvb[:, zq, 0], kvb[:, zq, 1], here >= doc[0])
        block(xq, kvb[:, zq, 2], kvb[:, zq, 3], here <= token + xq * 1024)

    def to_row(v):
        return jnp.sum(jnp.where(diagonal, v, 0.0), axis=0, keepdims=True)

    def to_column(v):
        wide_row = jnp.broadcast_to(v, (128, 128))
        return jnp.sum(jnp.where(diagonal, wide_row, 0.0), axis=1, keepdims=True)

    back = {}

    def give_back(d):
        xq = mod4(x + d)
        part_of[d - 1] = (acc[xq] / tot[xq]).astype(BF16)
        stat_of[d - 1] = jnp.concatenate(
            [to_row(r[xq, h * 128 : (h + 1) * 128, :]) for r in (mx, tot) for h in range(4)],
            axis=0,
        )
        back[d] = (
            wire.copy(part_of.at[d - 1], part_in.at[d - 1], {"x": xq}),
            wire.copy(stat_of.at[d - 1], stat_in.at[d - 1], {"x": xq}),
        )

    local[6].wait()
    for h in range(4):
        qs[x, h * 128 : (h + 1) * 128, :] = q[:, h * 128 : (h + 1) * 128]
    for d in local[:4]:
        d.wait()
    kv.z_send()
    kv.p1_send(0)
    ring.ring("q", q_at, "x", x)
    for i in range(4):
        mx[i] = jnp.full((512, 128), NEG, F32)
        tot[i] = jnp.zeros((512, 128), F32)
        acc[i] = jnp.zeros((512, 128), F32)
    local[4].wait()
    ring.forward("q", q_at, "x", x)
    kv.p1_fwd(0)
    both(pr, "p1_send", 0)
    pr[1].p2_send(0, 0)
    both(pr, "z_send")
    kv.z_wait()
    kv.p1_send(1)
    ring.done("q")
    kv.p1_done(0)
    local[9].wait()
    attend(0, mod4(x + 2))
    both(pr, "p1_fwd", 0)
    pr[1].p2_send(0, 1)
    pr[1].p2_send(0, 2)
    attend(0, mod4(x + 1))
    kv.p1_fwd(1)
    for k in range(3):
        pr[0].p2_send(0, k)
    attend(0, mod4(x + 3))
    both(pr, "p1_done", 0)
    pr[0].p2_send(0, 3)
    attend(0, x)
    kv.p1_done(1)
    local[5].wait()
    hz = {dz: wire.copy(hid.at[t], hid.at[t], tensor_peer(dz, 0)) for dz in (2, 1, 3)}
    hmate = [wire.copy(hid.at[t], hid.at[t], mate)]
    early = len(wire.open)
    attend(1, mod4(x + 2))
    give_back(2)
    attend(1, mod4(x + 1))
    give_back(1)
    attend(1, mod4(x + 3))
    give_back(3)
    pr[1].p2_send(0, 3)
    both(pr, "z_wait")
    both(pr, "p1_send", 1)
    both(pr, "p2_fwd", 0, 0)
    attend(1, x)
    rsend = []
    for p in peers:
        cols = pl.ds(pl.multiple_of(tensor_index(*p) * 1024, 1024), 1024)
        rsend.append(
            wire.copy(
                res_hbm.at[:, cols],
                res.at[pl.ds(pl.multiple_of(t * 16, 16), 16), :],
                tensor_peer(*p),
            )
        )
    both(pr, "p2_send", 1, 0)
    both(pr, "p2_fwd", 0, 1)
    both(pr, "p2_fwd", 0, 2)
    for d in (2, 1, 3):
        for r in back[d]:
            r.wait_recv()
    for h in range(4):
        rows = slice(h * 128, (h + 1) * 128)
        maxes = [mx[x, rows, :]] + [to_column(stat_in[i, h : h + 1, :]) for i in range(3)]
        most = jnp.maximum(
            jnp.maximum(maxes[0], maxes[1]), jnp.maximum(maxes[2], maxes[3])
        )
        scale = jnp.exp2(maxes[0] - most)
        over, under = acc[x, rows, :] * scale, tot[x, rows, :] * scale
        for i in range(3):
            scale = jnp.exp2(maxes[1 + i] - most) * to_column(stat_in[i, 4 + h : 5 + h, :])
            over = over + scale * part_in[i, rows, :].astype(F32)
            under = under + scale
        att[:, h * 128 : (h + 1) * 128] = (over / under).astype(BF16)

    local[8].wait()
    turns = (2, 1, 3, 0)

    def projected(dz, dc):
        cols = pl.ds(pl.multiple_of(tensor_index(dz, dc) * 1024, 1024), 1024)
        return jnp.dot(att[...], w[:, cols], preferred_element_type=F32)

    half = {}
    for dz in turns:
        bsend[dz] = projected(dz, 1).astype(BF16)
        half[dz] = wire.copy(bsend.at[dz], brecv.at[dz], mate)
    both(pr, "p1_fwd", 1)
    both(pr, "p2_send", 1, 1)
    both(pr, "p2_send", 1, 2)
    zsum = {}
    for dz in turns:
        mine = projected(dz, 0)
        half[dz].wait_recv()
        mine = mine + brecv[dz].astype(F32)
        if dz:
            bz[dz - 1] = mine.astype(BF16)
            zsum[dz] = wire.copy(bz.at[dz - 1], zrecv.at[dz - 1], tensor_peer(dz, 0))
        else:
            tacc[...] = mine
    wire.settle(early)
    both(pr, "p2_fwd", 0, 3)
    both(pr, "p1_done", 1)
    both(pr, "p2_send", 1, 3)
    for dz in (2, 1, 3):
        hz[dz].wait_recv()
        slot = mod4(zl + 4 - dz) * 2 + c
        hmate.append(wire.copy(hid.at[slot], hid.at[slot], mate))
    local[10].wait()

    for d in hmate:
        d.wait_recv()
    square = jnp.zeros((128, 384), F32)
    for i in range(8):
        h = hid[i].astype(F32)
        square = square + h * h
    inverse = lax.rsqrt(jnp.sum(square, axis=1, keepdims=True) / 3072.0 + 1e-05)
    for i in range(8):
        n = (hid[i].astype(F32) * inverse * gain[i]).astype(BF16)
        nrm[:, i * 384 : (i + 1) * 384] = n
        nrmt[i // 2, 2 * (i % 2) : 2 * (i % 2) + 2] = n.T.reshape(2, 192, 128)

    halfrows = pl.ds(2 * c, 2)

    def token_cols(pos):
        return pl.ds(pl.multiple_of(pos * 128, 128), 128)

    nxtx[:, :, token_cols(x)] = nrmt[x]
    nxty[:, :, token_cols(y)] = nrmt[:, y]
    middle = len(wire.open)
    for k in range(4):
        both(pr, "p2_fwd", 1, k)
    nx, nmate = {}, []
    for d in (2, 1, 3):
        nx["x", d] = wire.copy(
            nrmt.at[mod4(x + d), halfrows], nxtx.at[halfrows, :, token_cols(x)], {"x": mod4(x + d)}
        )
        nx["y", d] = wire.copy(
            nrmt.at[halfrows, mod4(y + d)], nxty.at[halfrows, :, token_cols(y)], {"y": mod4(y + d)}
        )
    for d in rsend:
        d.wait_recv()
    local[7].wait()
    tacc[...] = tacc[...] + res[...].astype(F32)
    wire.settle(middle)
    for j in range(2):
        for k in range(4):
            both(pr, "p2_done", j, k)
    pre = jnp.zeros((128, 1024), F32)
    for i in range(4):
        pre = pre + jnp.dot(
            nrm[:, i * 768 : (i + 1) * 768],
            pj[pl.ds(8 * i, 8)].reshape(768, 1024),
            preferred_element_type=F32,
        )
    for dz in turns[:3]:
        zsum[dz].wait_recv()
    teacher = (
        tacc[...] + zrecv[0].astype(F32) + zrecv[1].astype(F32) + zrecv[2].astype(F32)
    ).astype(BF16)
    tcb[...] = teacher
    put(tcb, teacher_out)
    mismatch = (pre - teacher.astype(F32)).astype(BF16)
    mis[...] = mismatch
    lanes = [("x", x, nxtx, "y", y), ("y", y, nxty, "x", x)] * 2
    for i, lane in enumerate(lanes):
        mch[i, lane[1]] = mismatch[:, i * 256 : (i + 1) * 256]

    def mch_at(i):
        return lambda p, h: mch.at[i, p] if h is None else mch.at[i, p, pl.ds(64 * h, 64)]

    sums = []
    for i, (axis, pos, _, other, there) in enumerate(lanes):
        ring.ring(i, mch_at(i), axis, pos)
        sums.append(
            Scatter(
                wire,
                lambda p, h, i=i: gp.at[i, p] if h is None else gp.at[i, p, h],
                near.at[i],
                far.at[i],
                other,
                there,
            )
        )

    def pass_on(i):
        ring.forward(i, mch_at(i), lanes[i][0], lanes[i][1])

    def product(i):
        ring.done(i)
        g = jnp.dot(
            lanes[i][2][...].reshape(768, 512),
            mch[i].reshape(512, 256),
            preferred_element_type=F32,
        )
        gp[i] = g.astype(BF16).reshape(4, 2, 96, 256)
        sums[i].start()

    last = {}

    def across(i):
        sums[i].finish()
        last[i] = wire.copy(gp.at[i, lanes[i][4], 1 - z], zpart.at[i], {"zh": 1 - z})

    def state_grad(dz, dc):
        rows = pj[pl.ds(4 * tensor_index(dz, dc), 4)].reshape(384, 1024)
        return lax.dot_general(
            mis[...], rows, (((1,), (1,)), ((), ())), preferred_element_type=F32
        )

    inner = jnp.zeros((128, 384), F32)

    def parts(dz, dc, mine):
        i = tensor_index(dz, dc)
        here = mine * hid[i].astype(F32)
        glocal[pl.ds(i, 1), :] = jnp.sum(here * inverse, axis=0, keepdims=True)
        return inner + here * gain[i]

    def to_mate(dz):
        mine = state_grad(dz, 1)
        fsend[dz] = mine.astype(BF16)
        half[dz] = wire.copy(fsend.at[dz], frecv.at[dz], mate)
        return parts(dz, 1, mine)

    def own_part(dz):
        mine = state_grad(dz, 0)
        facc[dz] = mine
        return parts(dz, 0, mine)

    def along_z(dz):
        half[dz].wait_recv()
        facc[dz] = facc[dz] + frecv[dz].astype(F32)
        if dz:
            fz[dz - 1] = facc[dz].astype(BF16)
            zsum[dz] = wire.copy(fz.at[dz - 1], fzrecv.at[dz - 1], tensor_peer(dz, 0))

    for dz in turns:
        inner = to_mate(dz)
    for dz in turns:
        inner = own_part(dz)
    as_row = to_row(jnp.sum(inner, axis=1, keepdims=True))
    whole = glocal[...]
    for i in range(8):
        g4[i] = jnp.concatenate(
            [whole[i : i + 1, 128 * j : 128 * j + 128] for j in range(3)]
            + [as_row, jnp.zeros((4, 128), F32)],
            axis=0,
        )
    g4d = [
        wire.copy(g4.at[tensor_index(*p)], g5.at[i], tensor_peer(*p)) for i, p in enumerate(peers)
    ]
    pass_on(0)
    pass_on(1)
    for dz in turns:
        along_z(dz)
    pass_on(2)
    pass_on(3)
    for d in (2, 1, 3):
        for axis, pos, buf in (("x", x, nxtx), ("y", y, nxty)):
            nx[axis, d].wait_recv()
            came = buf.at[halfrows, :, token_cols(mod4(pos + 4 - d))]
            nmate.append(wire.copy(came, came, mate))
    for d in nmate:
        d.wait_recv()
    for i in range(4):
        product(i)
    sums[0].middle()
    total = g4[t]
    for i, d in enumerate(g4d):
        d.wait_recv()
        total = total + g5[i]
    g1[0] = total
    row_inner = to_column(total[3:4, :]) / 3072.0
    g1d = [wire.copy(g1.at[0], g1.at[d], {"x": mod4(x + d)}) for d in (1, 2, 3)]
    sums[1].middle()
    sums[2].middle()
    sums[3].middle()
    for d in g1d:
        d.wait_recv()
    g2[0] = g1[0] + g1[1] + g1[2] + g1[3]
    g2d = [wire.copy(g2.at[0], g2.at[d], {"y": mod4(y + d)}) for d in (1, 2, 3)]
    across(0)
    across(1)
    across(2)
    for d in g2d:
        d.wait_recv()
    g3[0] = g2[0] + g2[1] + g2[2] + g2[3]
    g3d = wire.copy(g3.at[0], g3.at[1], {"zh": 1 - z})
    across(3)
    for dz in turns[:3]:
        zsum[dz].wait_recv()
    grad = (
        facc[0] + fzrecv[0].astype(F32) + fzrecv[1].astype(F32) + fzrecv[2].astype(F32)
    )
    sgb[...] = (
        inverse * gain[t] * grad - hid[t].astype(F32) * inverse * inverse * inverse * row_inner
    ).astype(BF16)
    put(sgb, sgrad_out)
    grad_scale = 1.0 / 64.0
    for i in range(4):
        last[i].wait_recv()
        pgb[i] = (gp[i, lanes[i][4], z].astype(F32) + zpart[i].astype(F32)) * grad_scale
        put(pgb.at[i], pgrad_out.at[:, pl.ds(256 * i, 256)])
    g3d.wait_recv()
    ggb[...] = (g3[0] + g3[1]) * grad_scale
    put(ggb, ggrad_out)
    wire.settle()
    assert (wire.send_used, wire.recv_used) == (SENDS, RECVS), (wire.send_used, wire.recv_used)
    for d in written:
        d.wait()


def hand_over(a, b, c, d, a_out, b_out, c_out, d_out):
    a_out[...] = a[...]
    b_out[...] = b[...]
    c_out[...] = c[...]
    for j in range(3):
        d_out[pl.ds(128 * j, 128)] = d[j]


def local(
    queries, keys, values, prefix_keys, prefix_values, doc_start, out_weight, residual,
    student_hidden, student_gain, proj_weight,
):
    vmem = pl.BlockSpec(memory_space=pltpu.VMEM)
    anyspace = pl.BlockSpec(memory_space=pl.ANY)
    v = pltpu.VMEM
    shapes = [
        jax.ShapeDtypeStruct((128, 1024), BF16),
        jax.ShapeDtypeStruct((128, 384), BF16),
        jax.ShapeDtypeStruct((96, 1024), F32),
    ]
    outs = pl.pallas_call(
        kernel,
        out_shape=(*shapes, jax.ShapeDtypeStruct((8, 128), F32)),
        in_specs=[anyspace] * 11,
        out_specs=(anyspace,) * 4,
        scratch_shapes=[
            v((4, 2, 4, 128, 128), BF16),
            v((32, 96, 1024), BF16),
            v((512, 8192), BF16),
            v((128, 512), BF16),
            v((4, 512, 128), BF16),
            v((3, 512, 128), BF16),
            v((3, 512, 128), BF16),
            v((3, 8, 128), F32),
            v((3, 8, 128), F32),
            v((8, 128, 384), BF16),
            v((128, 1024), BF16),
            v((4, 512, 128), F32),
            v((4, 512, 128), F32),
            v((4, 512, 128), F32),
            v((128, 512), BF16),
            v((4, 128, 1024), BF16),
            v((4, 128, 1024), BF16),
            v((3, 128, 1024), BF16),
            v((3, 128, 1024), BF16),
            v((128, 1024), F32),
            v((128, 3072), BF16),
            v((4, 4, 192, 128), BF16),
            v((4, 192, 512), BF16),
            v((4, 192, 512), BF16),
            v((128, 1024), BF16),
            v((4, 4, 128, 256), BF16),
            v((4, 128, 384), BF16),
            v((4, 128, 384), BF16),
            v((3, 128, 384), BF16),
            v((3, 128, 384), BF16),
            v((4, 128, 384), F32),
            v((8, 384), F32),
            v((4, 8, 128), F32),
            v((4, 8, 128), F32),
            v((2, 8, 128), F32),
            v((8, 8, 128), F32),
            v((7, 8, 128), F32),
            v((4, 4, 2, 96, 256), BF16),
            v((4, 2, 96, 256), BF16),
            v((4, 2, 2, 96, 256), BF16),
            v((4, 96, 256), BF16),
            v((128, 1024), BF16),
            v((128, 384), BF16),
            v((4, 96, 256), F32),
            v((8, 128), F32),
            pltpu.SMEM((1,), jnp.int32),
            v((8, 1, 384), F32),
            pltpu.SemaphoreType.DMA((SENDS,)),
            pltpu.SemaphoreType.DMA((RECVS,)),
            pltpu.SemaphoreType.DMA((18,)),
        ],
        compiler_params=pltpu.CompilerParams(
            collective_id=0, has_side_effects=True, vmem_limit_bytes=60 * 1024 * 1024
        ),
    )(
        queries, keys, values, prefix_keys, prefix_values, doc_start, out_weight, residual,
        student_hidden, student_gain.reshape(8, 1, 384), proj_weight,
    )
    return pl.pallas_call(
        hand_over,
        out_shape=(*shapes, jax.ShapeDtypeStruct((384,), F32)),
        in_specs=[vmem] * 4,
        out_specs=(vmem,) * 4,
    )(*outs)


def solution(mesh):
    finer = Mesh(mesh.devices.reshape(4, 4, 2, 4, 2), SEQ + TEN)
    rows = P(SEQ, TEN)
    return jax.shard_map(
        local,
        mesh=finer,
        in_specs=(
            rows, rows, rows, rows, rows, P(), P(TEN, None), P(SEQ + TEN, None), rows, P(), rows,
        ),
        out_specs=(rows, rows, rows, P(TEN)),
        check_vma=False,
    )
```

```python
import math

import jax
import jax.numpy as jnp
from jax import lax
from jax.experimental import pallas as pl
from jax.experimental.pallas import tpu as pltpu
from jax.sharding import Mesh
from jax.sharding import PartitionSpec as P

MESH = pl.DeviceIdType.MESH
F32 = jnp.float32
BF16 = jnp.bfloat16
NEG = -1e30
SEQ = ("x", "y", "zh")
TEN = ("zl", "c")
SENDS, RECVS = 95, 191


def mod4(v):
    return lax.rem(v, 4)


class Wire:
    def __init__(self, send, recv):
        self.send, self.recv = send, recv
        self.recv_used, self.send_used, self.spare, self.open = 0, 0, [], []

    def copy(self, src, dst, dev):
        if self.spare:
            i = self.spare.pop(0)
        else:
            i = self.send_used
            self.send_used += 1
        d = pltpu.make_async_remote_copy(
            src_ref=src,
            dst_ref=dst,
            send_sem=self.send.at[i],
            recv_sem=self.recv.at[self.recv_used],
            device_id=dev,
            device_id_type=MESH,
        )
        self.recv_used += 1
        d.start()
        self.open.append((i, d))
        return d

    def settle(self, count=None):
        count = len(self.open) if count is None else count
        for i, d in self.open[:count]:
            d.wait_send()
            self.spare.append(i)
        self.open = self.open[count:]


class Gather:
    def __init__(self, wire, at, first, second, coord):
        self.wire, self.at, self.first, self.second = wire, at, first, second
        self.a, self.b, self.z = coord[first], coord[second], coord["zh"]
        self.r, self.l, self.hr, self.hl = {}, {}, {}, {}
        a = self.a
        self.order = (a, mod4(a + 3), mod4(a + 1), mod4(a + 2))

    def z_send(self):
        own = self.at(self.a, self.b, self.z, 1, None)
        self.zd = self.wire.copy(own, own, {"zh": 1 - self.z})

    def z_wait(self):
        self.zd.wait_recv()

    def ring(self, key, ref_of, axis, pos):
        own = ref_of(pos, None)
        self.r[key] = self.wire.copy(own, own, {axis: mod4(pos + 1)})
        self.l[key] = self.wire.copy(own, own, {axis: mod4(pos + 3)})

    def forward(self, key, ref_of, axis, pos):
        self.r[key].wait_recv()
        left = ref_of(mod4(pos + 3), 0)
        self.hr[key] = self.wire.copy(left, left, {axis: mod4(pos + 1)})
        self.l[key].wait_recv()
        right = ref_of(mod4(pos + 1), 1)
        self.hl[key] = self.wire.copy(right, right, {axis: mod4(pos + 3)})

    def done(self, key):
        self.hr[key].wait_recv()
        self.hl[key].wait_recv()

    def one(self, j):
        zq = self.z if j == 0 else 1 - self.z
        return lambda pos, half: self.at(pos, self.b, zq, 1, half)

    def two(self, j, k):
        aq = self.order[k]
        if j is None:
            return lambda pos, half: self.at(aq, pos, 0, 2, half)
        zq = self.z if j == 0 else 1 - self.z
        return lambda pos, half: self.at(aq, pos, zq, 1, half)

    def p1_send(self, j):
        self.ring(("1", j), self.one(j), self.first, self.a)

    def p1_fwd(self, j):
        self.forward(("1", j), self.one(j), self.first, self.a)

    def p1_done(self, j):
        self.done(("1", j))

    def p2_send(self, j, k):
        self.ring(("2", j, k), self.two(j, k), self.second, self.b)

    def p2_fwd(self, j, k):
        self.forward(("2", j, k), self.two(j, k), self.second, self.b)

    def p2_done(self, j, k):
        self.done(("2", j, k))


class Scatter:
    def __init__(self, wire, part, near, far, axis, pos):
        self.wire, self.part, self.near, self.far = wire, part, near, far
        self.axis, self.pos = axis, pos

    def start(self):
        p, ax = self.pos, self.axis
        opp = mod4(p + 2)
        self.r1 = self.wire.copy(self.part(opp, 0), self.near.at[0], {ax: mod4(p + 1)})
        self.l1 = self.wire.copy(self.part(opp, 1), self.near.at[1], {ax: mod4(p + 3)})

    def middle(self):
        p, ax = self.pos, self.axis
        right, left = mod4(p + 1), mod4(p + 3)
        self.r1.wait_recv()
        ref = self.part(right, 0)
        ref[...] = (ref[...].astype(F32) + self.near[0].astype(F32)).astype(BF16)
        self.r2 = self.wire.copy(self.part(right, None), self.far.at[0], {ax: right})
        self.l1.wait_recv()
        ref = self.part(left, 1)
        ref[...] = (ref[...].astype(F32) + self.near[1].astype(F32)).astype(BF16)
        self.l2 = self.wire.copy(self.part(left, None), self.far.at[1], {ax: left})

    def finish(self):
        self.r2.wait_recv()
        self.l2.wait_recv()
        ref = self.part(self.pos, None)
        ref[...] = (
            ref[...].astype(F32) + self.far[0].astype(F32) + self.far[1].astype(F32)
        ).astype(BF16)


def kernel(
    q_hbm, k_hbm, v_hbm, pk_hbm, pv_hbm, doc_hbm, w_hbm, res_hbm, hid_hbm, gain_hbm, proj_hbm,
    teacher_out, sgrad_out, pgrad_out, ggrad_out,
    kvb, pj, w, q, qs, part_of, part_in, stat_of, stat_in, hid, res, mx, tot, acc, att,
    bsend, brecv, bz, zrecv, tacc, nrm, nrmt, nxtx, nxty, mis, mch,
    fsend, frecv, fz, fzrecv, facc, glocal, g1, g2, g3, g4, g5,
    gp, near, far, zpart, tcb, sgb, pgb, ggb, doc, gain,
    ssem, rsem, lsem,
):
    x, y, z = lax.axis_index("x"), lax.axis_index("y"), lax.axis_index("zh")
    zl, c = lax.axis_index("zl"), lax.axis_index("c")
    coord = {"x": x, "y": y, "zh": z}
    seq = (x * 4 + y) * 2 + z
    t = zl * 2 + c
    wire = Wire(ssem, rsem)
    mate = {"c": 1 - c}

    def tensor_peer(dz, dc):
        return {"zl": mod4(zl + dz), "c": c if dc == 0 else 1 - c}

    def tensor_index(dz, dc):
        return mod4(zl + dz) * 2 + (c if dc == 0 else 1 - c)

    peers = [(dz, dc) for dz in (2, 1, 3, 0) for dc in (0, 1) if (dz, dc) != (0, 0)]

    loads = [
        (pk_hbm, kvb.at[y, z, 0]),
        (pv_hbm, kvb.at[y, z, 1]),
        (k_hbm, kvb.at[y, z, 2]),
        (v_hbm, kvb.at[y, z, 3]),
        (proj_hbm, pj.at[seq]),
        (hid_hbm, hid.at[t]),
        (q_hbm, q),
        (
            res_hbm.at[:, pl.ds(pl.multiple_of(t * 1024, 1024), 1024)],
            res.at[pl.ds(pl.multiple_of(t * 16, 16), 16), :],
        ),
        (w_hbm, w),
        (doc_hbm, doc),
        (gain_hbm, gain),
    ]
    local = [pltpu.make_async_copy(s, d, lsem.at[i]) for i, (s, d) in enumerate(loads)]
    for d in local:
        d.start()

    written = []

    def put(src, dst):
        d = pltpu.make_async_copy(src, dst, lsem.at[len(loads) + len(written)])
        d.start()
        written.append(d)

    barrier = pltpu.get_barrier_semaphore()
    greet = [
        {"x": mod4(x + 1)}, {"x": mod4(x + 2)}, {"x": mod4(x + 3)},
        {"y": mod4(y + 1)}, {"y": mod4(y + 2)}, {"y": mod4(y + 3)},
        {"zh": 1 - z},
    ] + [tensor_peer(*p) for p in peers]
    for dev in greet:
        pl.semaphore_signal(barrier, inc=1, device_id=dev, device_id_type=MESH)
    pl.semaphore_wait(barrier, len(greet))

    def kv_at(a, b, zq, count, half):
        return kvb.at[a, zq] if half is None else kvb.at[a, zq, pl.ds(2 * half, 2)]

    def q_at(pos, half):
        return qs.at[pos] if half is None else qs.at[pos, pl.ds(256 * half, 256)]

    def pj_at(low, x_first):
        def at(a, b, zq, count, half):
            slot = ((a * 4 + b) if x_first else (b * 4 + a)) * 2 + zq
            where = slot if count == 1 else pl.ds(slot, 2)
            cols = pl.ds(0, 1024) if half is None else pl.ds(512 * half, 512)
            return pj.at[where, pl.ds(low, 48), cols]

        return at

    kv = Gather(wire, kv_at, "y", "x", coord)
    ring = Gather(wire, None, "x", "y", coord)
    pr = (
        Gather(wire, pj_at(0, True), "x", "y", coord),
        Gather(wire, pj_at(48, False), "y", "x", coord),
    )

    def both(streams, name, *args):
        for s in streams:
            getattr(s, name)(*args)

    factor = 128 ** (-0.5) * math.log2(math.e)
    column = lax.broadcasted_iota(jnp.int32, (512, 512), 1)
    position = x * 1024 + (column // 128) * 256 + lax.rem(column, 128)
    token = lax.rem(lax.broadcasted_iota(jnp.int32, (512, 512), 0), 128) + (y * 2 + z) * 128
    diagonal = lax.broadcasted_iota(jnp.int32, (128, 128), 0) == lax.broadcasted_iota(
        jnp.int32, (128, 128), 1
    )

    def wide(v):
        return jnp.concatenate([v] * 4, axis=1)

    def block(xq, kb, vb, visible):
        s = lax.dot_general(
            qs[xq], kb.reshape(512, 128), (((1,), (1,)), ((), ())), preferred_element_type=F32
        ) * factor
        s = jnp.where(visible, s, NEG)
        old = mx[xq]
        new = jnp.maximum(old, jnp.broadcast_to(jnp.max(s, axis=1, keepdims=True), (512, 128)))
        p = jnp.exp2(s - wide(new))
        scale = jnp.exp2(old - new)
        mx[xq] = new
        tot[xq] = tot[xq] * scale + jnp.broadcast_to(
            jnp.sum(p, axis=1, keepdims=True), (512, 128)
        )
        acc[xq] = acc[xq] * scale + jnp.dot(
            p.astype(BF16), vb.reshape(512, 128), preferred_element_type=F32
        )

    def attend(j, xq):
        zq = z if j == 0 else 1 - z
        here = position + zq * 128
        block(xq, kvb[:, zq, 0], kvb[:, zq, 1], here >= doc[0])
        block(xq, kvb[:, zq, 2], kvb[:, zq, 3], here <= token + xq * 1024)

    def to_row(v):
        return jnp.sum(jnp.where(diagonal, v, 0.0), axis=0, keepdims=True)

    def to_column(v):
        wide_row = jnp.broadcast_to(v, (128, 128))
        return jnp.sum(jnp.where(diagonal, wide_row, 0.0), axis=1, keepdims=True)

    back = {}

    def give_back(d):
        xq = mod4(x + d)
        part_of[d - 1] = (acc[xq] / tot[xq]).astype(BF16)
        stat_of[d - 1] = jnp.concatenate(
            [to_row(r[xq, h * 128 : (h + 1) * 128, :]) for r in (mx, tot) for h in range(4)],
            axis=0,
        )
        back[d] = (
            wire.copy(part_of.at[d - 1], part_in.at[d - 1], {"x": xq}),
            wire.copy(stat_of.at[d - 1], stat_in.at[d - 1], {"x": xq}),
        )

    local[6].wait()
    for h in range(4):
        qs[x, h * 128 : (h + 1) * 128, :] = q[:, h * 128 : (h + 1) * 128]
    for d in local[:4]:
        d.wait()
    kv.z_send()
    kv.p1_send(0)
    ring.ring("q", q_at, "x", x)
    for i in range(4):
        mx[i] = jnp.full((512, 128), NEG, F32)
        tot[i] = jnp.zeros((512, 128), F32)
        acc[i] = jnp.zeros((512, 128), F32)
    local[4].wait()
    ring.forward("q", q_at, "x", x)
    kv.p1_fwd(0)
    both(pr, "p1_send", 0)
    pr[1].p2_send(0, 0)
    both(pr, "z_send")
    kv.z_wait()
    kv.p1_send(1)
    ring.done("q")
    kv.p1_done(0)
    local[9].wait()
    attend(0, mod4(x + 2))
    both(pr, "p1_fwd", 0)
    pr[1].p2_send(0, 1)
    pr[1].p2_send(0, 2)
    attend(0, mod4(x + 1))
    kv.p1_fwd(1)
    for k in range(3):
        pr[0].p2_send(0, k)
    attend(0, mod4(x + 3))
    both(pr, "p1_done", 0)
    pr[0].p2_send(0, 3)
    attend(0, x)
    kv.p1_done(1)
    local[5].wait()
    hz = {dz: wire.copy(hid.at[t], hid.at[t], tensor_peer(dz, 0)) for dz in (2, 1, 3)}
    hmate = [wire.copy(hid.at[t], hid.at[t], mate)]
    early = len(wire.open)
    attend(1, mod4(x + 2))
    give_back(2)
    attend(1, mod4(x + 1))
    give_back(1)
    attend(1, mod4(x + 3))
    give_back(3)
    pr[1].p2_send(0, 3)
    both(pr, "z_wait")
    both(pr, "p1_send", 1)
    both(pr, "p2_fwd", 0, 0)
    attend(1, x)
    rsend = []
    for p in peers:
        cols = pl.ds(pl.multiple_of(tensor_index(*p) * 1024, 1024), 1024)
        rsend.append(
            wire.copy(
                res_hbm.at[:, cols],
                res.at[pl.ds(pl.multiple_of(t * 16, 16), 16), :],
                tensor_peer(*p),
            )
        )
    both(pr, "p2_send", 1, 0)
    both(pr, "p2_fwd", 0, 1)
    both(pr, "p2_fwd", 0, 2)
    for d in (2, 1, 3):
        for r in back[d]:
            r.wait_recv()
    for h in range(4):
        rows = slice(h * 128, (h + 1) * 128)
        maxes = [mx[x, rows, :]] + [to_column(stat_in[i, h : h + 1, :]) for i in range(3)]
        most = jnp.maximum(
            jnp.maximum(maxes[0], maxes[1]), jnp.maximum(maxes[2], maxes[3])
        )
        scale = jnp.exp2(maxes[0] - most)
        over, under = acc[x, rows, :] * scale, tot[x, rows, :] * scale
        for i in range(3):
            scale = jnp.exp2(maxes[1 + i] - most) * to_column(stat_in[i, 4 + h : 5 + h, :])
            over = over + scale * part_in[i, rows, :].astype(F32)
            under = under + scale
        att[:, h * 128 : (h + 1) * 128] = (over / under).astype(BF16)

    local[8].wait()
    turns = (2, 1, 3, 0)

    def projected(dz, dc):
        cols = pl.ds(pl.multiple_of(tensor_index(dz, dc) * 1024, 1024), 1024)
        return jnp.dot(att[...], w[:, cols], preferred_element_type=F32)

    half = {}
    for dz in turns:
        bsend[dz] = projected(dz, 1).astype(BF16)
        half[dz] = wire.copy(bsend.at[dz], brecv.at[dz], mate)
    both(pr, "p1_fwd", 1)
    both(pr, "p2_send", 1, 1)
    both(pr, "p2_send", 1, 2)
    zsum = {}
    for dz in turns:
        mine = projected(dz, 0)
        half[dz].wait_recv()
        mine = mine + brecv[dz].astype(F32)
        if dz:
            bz[dz - 1] = mine.astype(BF16)
            zsum[dz] = wire.copy(bz.at[dz - 1], zrecv.at[dz - 1], tensor_peer(dz, 0))
        else:
            tacc[...] = mine
    wire.settle(early)
    both(pr, "p2_fwd", 0, 3)
    both(pr, "p1_done", 1)
    both(pr, "p2_send", 1, 3)
    for dz in (2, 1, 3):
        hz[dz].wait_recv()
        slot = mod4(zl + 4 - dz) * 2 + c
        hmate.append(wire.copy(hid.at[slot], hid.at[slot], mate))
    local[10].wait()

    for d in hmate:
        d.wait_recv()
    square = jnp.zeros((128, 384), F32)
    for i in range(8):
        h = hid[i].astype(F32)
        square = square + h * h
    inverse = lax.rsqrt(jnp.sum(square, axis=1, keepdims=True) / 3072.0 + 1e-05)
    for i in range(8):
        n = (hid[i].astype(F32) * inverse * gain[i]).astype(BF16)
        nrm[:, i * 384 : (i + 1) * 384] = n
        nrmt[i // 2, 2 * (i % 2) : 2 * (i % 2) + 2] = n.T.reshape(2, 192, 128)

    halfrows = pl.ds(2 * c, 2)

    def token_cols(pos):
        return pl.ds(pl.multiple_of(pos * 128, 128), 128)

    nxtx[:, :, token_cols(x)] = nrmt[x]
    nxty[:, :, token_cols(y)] = nrmt[:, y]
    middle = len(wire.open)
    for k in range(4):
        both(pr, "p2_fwd", 1, k)
    nx, nmate = {}, []
    for d in (2, 1, 3):
        nx["x", d] = wire.copy(
            nrmt.at[mod4(x + d), halfrows], nxtx.at[halfrows, :, token_cols(x)], {"x": mod4(x + d)}
        )
        nx["y", d] = wire.copy(
            nrmt.at[halfrows, mod4(y + d)], nxty.at[halfrows, :, token_cols(y)], {"y": mod4(y + d)}
        )
    for d in rsend:
        d.wait_recv()
    local[7].wait()
    tacc[...] = tacc[...] + res[...].astype(F32)
    wire.settle(middle)
    for j in range(2):
        for k in range(4):
            both(pr, "p2_done", j, k)
    pre = jnp.zeros((128, 1024), F32)
    for i in range(4):
        pre = pre + jnp.dot(
            nrm[:, i * 768 : (i + 1) * 768],
            pj[pl.ds(8 * i, 8)].reshape(768, 1024),
            preferred_element_type=F32,
        )
    for dz in turns[:3]:
        zsum[dz].wait_recv()
    teacher = (
        tacc[...] + zrecv[0].astype(F32) + zrecv[1].astype(F32) + zrecv[2].astype(F32)
    ).astype(BF16)
    tcb[...] = teacher
    put(tcb, teacher_out)
    mismatch = (pre - teacher.astype(F32)).astype(BF16)
    mis[...] = mismatch
    lanes = [("x", x, nxtx, "y", y), ("y", y, nxty, "x", x)] * 2
    for i, lane in enumerate(lanes):
        mch[i, lane[1]] = mismatch[:, i * 256 : (i + 1) * 256]

    def mch_at(i):
        return lambda p, h: mch.at[i, p] if h is None else mch.at[i, p, pl.ds(64 * h, 64)]

    sums = []
    for i, (axis, pos, _, other, there) in enumerate(lanes):
        ring.ring(i, mch_at(i), axis, pos)
        sums.append(
            Scatter(
                wire,
                lambda p, h, i=i: gp.at[i, p] if h is None else gp.at[i, p, h],
                near.at[i],
                far.at[i],
                other,
                there,
            )
        )

    def pass_on(i):
        ring.forward(i, mch_at(i), lanes[i][0], lanes[i][1])

    def product(i):
        ring.done(i)
        g = jnp.dot(
            lanes[i][2][...].reshape(768, 512),
            mch[i].reshape(512, 256),
            preferred_element_type=F32,
        )
        gp[i] = g.astype(BF16).reshape(4, 2, 96, 256)
        sums[i].start()

    last = {}

    def across(i):
        sums[i].finish()
        last[i] = wire.copy(gp.at[i, lanes[i][4], 1 - z], zpart.at[i], {"zh": 1 - z})

    def state_grad(dz, dc):
        rows = pj[pl.ds(4 * tensor_index(dz, dc), 4)].reshape(384, 1024)
        return lax.dot_general(
            mis[...], rows, (((1,), (1,)), ((), ())), preferred_element_type=F32
        )

    inner = jnp.zeros((128, 384), F32)

    def parts(dz, dc, mine):
        i = tensor_index(dz, dc)
        here = mine * hid[i].astype(F32)
        glocal[pl.ds(i, 1), :] = jnp.sum(here * inverse, axis=0, keepdims=True)
        return inner + here * gain[i]

    def to_mate(dz):
        mine = state_grad(dz, 1)
        fsend[dz] = mine.astype(BF16)
        half[dz] = wire.copy(fsend.at[dz], frecv.at[dz], mate)
        return parts(dz, 1, mine)

    def own_part(dz):
        mine = state_grad(dz, 0)
        facc[dz] = mine
        return parts(dz, 0, mine)

    def along_z(dz):
        half[dz].wait_recv()
        facc[dz] = facc[dz] + frecv[dz].astype(F32)
        if dz:
            fz[dz - 1] = facc[dz].astype(BF16)
            zsum[dz] = wire.copy(fz.at[dz - 1], fzrecv.at[dz - 1], tensor_peer(dz, 0))

    for dz in turns:
        inner = to_mate(dz)
    for dz in turns:
        inner = own_part(dz)
    as_row = to_row(jnp.sum(inner, axis=1, keepdims=True))
    whole = glocal[...]
    for i in range(8):
        g4[i] = jnp.concatenate(
            [whole[i : i + 1, 128 * j : 128 * j + 128] for j in range(3)]
            + [as_row, jnp.zeros((4, 128), F32)],
            axis=0,
        )
    g4d = [
        wire.copy(g4.at[tensor_index(*p)], g5.at[i], tensor_peer(*p)) for i, p in enumerate(peers)
    ]
    for dz in turns:
        along_z(dz)
    pass_on(0)
    pass_on(1)
    pass_on(2)
    pass_on(3)
    for d in (2, 1, 3):
        for axis, pos, buf in (("x", x, nxtx), ("y", y, nxty)):
            nx[axis, d].wait_recv()
            came = buf.at[halfrows, :, token_cols(mod4(pos + 4 - d))]
            nmate.append(wire.copy(came, came, mate))
    for d in nmate:
        d.wait_recv()
    for i in range(4):
        product(i)
    sums[0].middle()
    total = g4[t]
    for i, d in enumerate(g4d):
        d.wait_recv()
        total = total + g5[i]
    g1[0] = total
    row_inner = to_column(total[3:4, :]) / 3072.0
    g1d = [wire.copy(g1.at[0], g1.at[d], {"x": mod4(x + d)}) for d in (1, 2, 3)]
    sums[1].middle()
    sums[2].middle()
    sums[3].middle()
    for d in g1d:
        d.wait_recv()
    g2[0] = g1[0] + g1[1] + g1[2] + g1[3]
    g2d = [wire.copy(g2.at[0], g2.at[d], {"y": mod4(y + d)}) for d in (1, 2, 3)]
    across(0)
    across(1)
    across(2)
    for d in g2d:
        d.wait_recv()
    g3[0] = g2[0] + g2[1] + g2[2] + g2[3]
    g3d = wire.copy(g3.at[0], g3.at[1], {"zh": 1 - z})
    across(3)
    for dz in turns[:3]:
        zsum[dz].wait_recv()
    grad = (
        facc[0] + fzrecv[0].astype(F32) + fzrecv[1].astype(F32) + fzrecv[2].astype(F32)
    )
    sgb[...] = (
        inverse * gain[t] * grad - hid[t].astype(F32) * inverse * inverse * inverse * row_inner
    ).astype(BF16)
    put(sgb, sgrad_out)
    grad_scale = 1.0 / 64.0
    for i in range(4):
        last[i].wait_recv()
        pgb[i] = (gp[i, lanes[i][4], z].astype(F32) + zpart[i].astype(F32)) * grad_scale
        put(pgb.at[i], pgrad_out.at[:, pl.ds(256 * i, 256)])
    g3d.wait_recv()
    ggb[...] = (g3[0] + g3[1]) * grad_scale
    put(ggb, ggrad_out)
    wire.settle()
    assert (wire.send_used, wire.recv_used) == (SENDS, RECVS), (wire.send_used, wire.recv_used)
    for d in written:
        d.wait()


def hand_over(a, b, c, d, a_out, b_out, c_out, d_out):
    a_out[...] = a[...]
    b_out[...] = b[...]
    c_out[...] = c[...]
    for j in range(3):
        d_out[pl.ds(128 * j, 128)] = d[j]


def local(
    queries, keys, values, prefix_keys, prefix_values, doc_start, out_weight, residual,
    student_hidden, student_gain, proj_weight,
):
    vmem = pl.BlockSpec(memory_space=pltpu.VMEM)
    anyspace = pl.BlockSpec(memory_space=pl.ANY)
    v = pltpu.VMEM
    shapes = [
        jax.ShapeDtypeStruct((128, 1024), BF16),
        jax.ShapeDtypeStruct((128, 384), BF16),
        jax.ShapeDtypeStruct((96, 1024), F32),
    ]
    outs = pl.pallas_call(
        kernel,
        out_shape=(*shapes, jax.ShapeDtypeStruct((8, 128), F32)),
        in_specs=[anyspace] * 11,
        out_specs=(anyspace,) * 4,
        scratch_shapes=[
            v((4, 2, 4, 128, 128), BF16),
            v((32, 96, 1024), BF16),
            v((512, 8192), BF16),
            v((128, 512), BF16),
            v((4, 512, 128), BF16),
            v((3, 512, 128), BF16),
            v((3, 512, 128), BF16),
            v((3, 8, 128), F32),
            v((3, 8, 128), F32),
            v((8, 128, 384), BF16),
            v((128, 1024), BF16),
            v((4, 512, 128), F32),
            v((4, 512, 128), F32),
            v((4, 512, 128), F32),
            v((128, 512), BF16),
            v((4, 128, 1024), BF16),
            v((4, 128, 1024), BF16),
            v((3, 128, 1024), BF16),
            v((3, 128, 1024), BF16),
            v((128, 1024), F32),
            v((128, 3072), BF16),
            v((4, 4, 192, 128), BF16),
            v((4, 192, 512), BF16),
            v((4, 192, 512), BF16),
            v((128, 1024), BF16),
            v((4, 4, 128, 256), BF16),
            v((4, 128, 384), BF16),
            v((4, 128, 384), BF16),
            v((3, 128, 384), BF16),
            v((3, 128, 384), BF16),
            v((4, 128, 384), F32),
            v((8, 384), F32),
            v((4, 8, 128), F32),
            v((4, 8, 128), F32),
            v((2, 8, 128), F32),
            v((8, 8, 128), F32),
            v((7, 8, 128), F32),
            v((4, 4, 2, 96, 256), BF16),
            v((4, 2, 96, 256), BF16),
            v((4, 2, 2, 96, 256), BF16),
            v((4, 96, 256), BF16),
            v((128, 1024), BF16),
            v((128, 384), BF16),
            v((4, 96, 256), F32),
            v((8, 128), F32),
            pltpu.SMEM((1,), jnp.int32),
            v((8, 1, 384), F32),
            pltpu.SemaphoreType.DMA((SENDS,)),
            pltpu.SemaphoreType.DMA((RECVS,)),
            pltpu.SemaphoreType.DMA((18,)),
        ],
        compiler_params=pltpu.CompilerParams(
            collective_id=0, has_side_effects=True, vmem_limit_bytes=60 * 1024 * 1024
        ),
    )(
        queries, keys, values, prefix_keys, prefix_values, doc_start, out_weight, residual,
        student_hidden, student_gain.reshape(8, 1, 384), proj_weight,
    )
    return pl.pallas_call(
        hand_over,
        out_shape=(*shapes, jax.ShapeDtypeStruct((384,), F32)),
        in_specs=[vmem] * 4,
        out_specs=(vmem,) * 4,
    )(*outs)


def solution(mesh):
    finer = Mesh(mesh.devices.reshape(4, 4, 2, 4, 2), SEQ + TEN)
    rows = P(SEQ, TEN)
    return jax.shard_map(
        local,
        mesh=finer,
        in_specs=(
            rows, rows, rows, rows, rows, P(), P(TEN, None), P(SEQ + TEN, None), rows, P(), rows,
        ),
        out_specs=(rows, rows, rows, P(TEN)),
        check_vma=False,
    )
```
